512 devices in a mesh: mode: 16 (over z_hi, x), mer: 32 (over y, z_lo, core).
Axes of the slice: x: 4, y: 8, z: 8 (z_hi: 4, z_lo: 2; z = z_hi * 2 + z_lo), core: 2. Of those that a mesh axis runs over, the one named last changes fastest.
Arguments:
- field: float32 [128, 6, 16384], P('mode', None, 'mer'), may hold values from -6 to 6
- velocity: bfloat16 [3, 256, 16384], P(None, None, ('mer', 'mode')), may hold values from -4 to 4
- stiffness: float32 [64, 64], replicated, may hold values from -0.75 to 0.75
- curl_matrix: float32 [64, 64], replicated, may hold values from -0.75 to 0.75
- mass: float32 [16384], P('mer'), may hold values from 0.5 to 2
- connect: int32 [512, 64], P('mer'), may hold values from 0 to 767
- wall_index: int32 [2048], P('mer'), may hold values from 0 to 511, as said below
- dtn: bfloat16 [128, 2048, 2048], P('mode', 'mer'), as said below
Outputs:
- advanced: float32 [128, 6, 16384], P('mode', None, 'mer')
- wall_flux: float32 [2, 128, 2, 2048], P(None, 'mode', None, 'mer')
The draws below stay inside these ranges and needn't reach their ends.
Inputs may be any that keep to these rules, and one draw needn't show every extreme that they name: `wall_index`: within each block of 64 consecutive entries the numbers are distinct. `dtn`: each mode's matrix is symmetric.
All inputs are finite; a program needn't handle non-finite values.
Results may differ from the reference program's by a relative error of at most 0.005.
Values may be sent and summed in bfloat16 or wider, within the bound.
No kernel may reach another device: no remote copies, remote signals or barrier semaphores. Data moves between devices by JAX's collectives and lax.ppermute only.
A program may use at most 64 MiB of HBM per device.

```python
import math
import jax
import jax.numpy as jnp
from jax import lax

MODES = 128
NPHI = 256
NODES_DEV = 512
NODES = 16384
GHOST = 256
ELEM_DEV = 16
ELEMS = 512
NP = 64
WALL_DEV = 64
WALL = 2048


def draw_wall_index(key, part):
    blocks = WALL // WALL_DEV
    scores = jax.random.randint(key, (blocks, NODES_DEV), 0, 1 << 20)
    scores = scores * NODES_DEV + jnp.arange(NODES_DEV, dtype=jnp.int32)[None, :]
    order = jnp.argsort(scores, axis=1, stable=True)
    return order[:, :WALL_DEV].reshape(WALL).astype(jnp.int32)


def draw_dtn(key, part):
    base = jax.random.normal(key, (MODES, WALL, WALL), jnp.float32) * WALL ** (-0.5)
    sym = 0.5 * (base + jnp.swapaxes(base, 1, 2))
    sym = sym + jnp.eye(WALL, dtype=jnp.float32)[None]
    return sym.astype(jnp.bfloat16)


def place_ends(values, stream_key, smallest, high):
    longest = values.shape.index(max(values.shape))
    spots = []
    for shift in (0, 1):
        where = [jax.random.randint(jax.random.fold_in(stream_key, axis), (), 0, length) for axis, length in enumerate(values.shape)]
        where[longest] = (where[longest] + shift) % values.shape[longest]
        spots.append(tuple(where))
    return values.at[spots[0]].set(smallest).at[spots[1]].set(high)


def steps_of(key, extent, cuts, low, high):
    gain, own = 1.0, jax.random.fold_in(key, 6)
    for position, shards_of in cuts:
        draws = jnp.exp(jax.random.uniform(jax.random.fold_in(own, position), (shards_of,), jnp.float32, low / len(cuts), high / len(cuts)))
        gain = gain * jnp.repeat(draws, extent[position] // shards_of).reshape([-1 if axis == position else 1 for axis in range(len(extent))])
    return gain


def scatter_about(own_key, dims, deviation, limit, cuts=(), held_as=jnp.bfloat16):
    entries = deviation * jax.random.normal(own_key, dims, jnp.float32)
    if cuts:
        entries = entries * steps_of(own_key, dims, cuts, -0.22, 0.18)
    return jnp.clip(entries, -limit, limit).astype(held_as)


def setup_inputs(seed: int = 0) -> dict:
    key_of = jax.random.split(jax.random.key(seed), 9)
    return {
        "field": scatter_about(key_of[0], (MODES, 6, NODES), 1.0, 6.0, ((0, 16), (2, 32)), jnp.float32),
        "velocity": scatter_about(key_of[1], (3, NPHI, NODES), 0.5, 4.0, ((2, 512),)),
        "stiffness": scatter_about(key_of[2], (NP, NP), NP ** -0.5, 0.75, (), jnp.float32),
        "curl_matrix": scatter_about(key_of[3], (NP, NP), NP ** -0.5, 0.75, (), jnp.float32),
        "mass": jnp.clip(jnp.exp(math.log(2.0) - 1.3862944 * jax.random.uniform(key_of[4], (NODES,), jnp.float32) ** steps_of(key_of[4], (NODES,), ((0, 32),), -0.2, 0.2)), 0.5, 2.0),
        "connect": place_ends(jax.random.randint(key_of[5], (ELEMS, NP), 0, NODES_DEV + GHOST), jax.random.fold_in(key_of[5], 1), 0, (NODES_DEV + GHOST) - 1).astype(jnp.int32),
        "wall_index": draw_wall_index(jax.random.fold_in(key_of[8], 71), 0),
        "dtn": draw_dtn(jax.random.fold_in(key_of[8], 71), 0),
    }


HI = lax.Precision.HIGHEST


def tables(modes, nphi):
    m = jnp.arange(modes, dtype=jnp.float32)
    k = jnp.arange(nphi, dtype=jnp.float32)
    angle = 2.0 * jnp.pi * m[:, None] * k[None, :] / nphi
    forward = jnp.stack([jnp.cos(angle), -jnp.sin(angle)], 1)
    return forward, forward / nphi


def induced(field, velocity):
    modes = field.shape[0]
    nphi = velocity.shape[1]
    forward, inverse = tables(modes, nphi)
    phys = jnp.einsum('mpcn,mpk->ckn', field.reshape(modes, 2, 3, -1), forward, precision=HI)
    vel = velocity.astype(jnp.float32)
    cross = jnp.stack([vel[1] * phys[2] - vel[2] * phys[1], vel[2] * phys[0] - vel[0] * phys[2], vel[0] * phys[1] - vel[1] * phys[0]])
    back = jnp.einsum('ckn,mpk->mpcn', cross, inverse, precision=HI)
    return back.reshape(modes, 6, -1)


def rate(field, velocity, stiffness, curl_matrix, mass, connect, wall_index, dtn):
    emf = induced(field, velocity)
    block = jnp.arange(ELEMS, dtype=jnp.int32) // ELEM_DEV
    glob = block[:, None] * NODES_DEV + connect
    valid = (glob < NODES).T
    where_node = jnp.where(glob < NODES, glob, 0).T

    def one_mode(pair):
        fmode, emode = pair
        values = jnp.where(valid, fmode[:, where_node], 0.0)
        evals = jnp.where(valid, emode[:, where_node], 0.0).reshape(2, 3, NP, -1)
        evals = jnp.roll(evals, 1, axis=1).reshape(6, NP, -1)
        local = -1.0 * jnp.einsum('pq,aqe->ape', stiffness, values, precision=HI)
        local = local + jnp.einsum('pq,aqe->ape', curl_matrix, evals, precision=HI)
        local = jnp.where(valid, local, 0.0)
        return jnp.zeros((6, NODES), jnp.float32).at[:, where_node].add(local)

    assembled = lax.map(one_mode, (field, emf))
    wall_node = (jnp.arange(WALL, dtype=jnp.int32) // WALL_DEV) * NODES_DEV + wall_index
    trace = field[:, jnp.array([2, 5])][:, :, wall_node].astype(jnp.bfloat16)

    def one_flux(pair):
        mat, tr = pair
        return jnp.dot(tr.astype(jnp.float32), mat.astype(jnp.float32).T, precision=HI)

    flux = lax.map(one_flux, (dtn, trace))
    coef = (jnp.arange(MODES, dtype=jnp.float32) / MODES) ** 2
    total = assembled - 4.0 * coef[:, None, None] * mass[None, None, :] * field
    total = total.at[:, 2, wall_node].add(-0.5 * flux[:, 0])
    total = total.at[:, 5, wall_node].add(-0.5 * flux[:, 1])
    return total / mass[None, None, :], flux


def reference(field, velocity, stiffness, curl_matrix, mass, connect, wall_index, dtn):
    args = (velocity, stiffness, curl_matrix, mass, connect, wall_index, dtn)
    first, flux_one = rate(field, *args)
    section = field + 0.2 * first
    second, flux_two = rate(section, *args)
    return 0.5 * (field + section + 0.2 * second), jnp.stack([flux_one, flux_two])
```

```python
import numpy as np
import jax
import jax.numpy as jnp
from jax import lax
from jax.experimental import pallas as pl
from jax.experimental.pallas import tpu as pltpu
from jax.sharding import PartitionSpec as P


BF = jnp.bfloat16
F32 = jnp.float32
PARAMS = pltpu.CompilerParams(vmem_limit_bytes=56 * 2**20)


def nt(a, b):
    return lax.dot_general(a, b, (((1,), (1,)), ((), ())), preferred_element_type=F32)


def nn(a, b):
    return jnp.dot(a, b, preferred_element_type=F32)


def tables(modes, nphi, mode_dev):
    mode = np.arange(modes).reshape(-1, 1, mode_dev)
    k = np.arange(nphi).reshape(-1, 1, 1, 1)
    angle = 2.0 * np.pi * ((mode[None] * k) % nphi) / nphi
    fwd = np.concatenate([np.cos(angle), -np.sin(angle)], 2).reshape(nphi, 2 * modes)
    return fwd.astype(BF), (fwd.T / nphi).astype(BF)


def lane_group(shape):
    return lax.broadcasted_iota(jnp.int32, shape, len(shape) - 1) // 32


def pick(group, parts):
    out = parts[0]
    for g, part in enumerate(parts[1:], 1):
        out = jnp.where(group == g, part, out)
    return out


def shift(x, groups):
    return x if groups % 4 == 0 else pltpu.roll(x, 32 * (groups % 4), 1)


def pack(rows, out_ref):
    group = lane_group((8, 128))
    for v in range(4):
        tiles = {cp: r[:, 128 * v : 128 * v + 128] for cp, r in rows.items()}
        for q in range(4):
            halves = [
                pick(group, [shift(tiles[c % 3, p], c - q) for c in range(4)]) for p in range(2)
            ]
            out_ref[4 * v + q] = jnp.concatenate(halves, 0).astype(BF)


def unpack(ref, slots):
    group = lane_group((16, 128))
    cols = []
    for v in range(slots // 4):
        tiles = [ref[4 * v + q].astype(F32) for q in range(4)]
        cols.append(
            jnp.concatenate(
                [pick(group, [shift(tiles[q], q - c) for q in range(4)]) for c in range(3)], 0
            ).astype(BF)
        )
    return jnp.concatenate(cols, 1)


def wall_onehot(wall):
    nodes = lax.broadcasted_iota(jnp.int32, (512, 128), 0)
    return (nodes == wall).astype(F32).astype(BF)


def pack_kernel(field_ref, out_ref):
    pack({(c, p): field_ref[3 * p + c] for c in range(3) for p in range(2)}, out_ref)


def trace_kernel(field_ref, wall_ref, out_ref):
    last = jnp.concatenate([field_ref[2], field_ref[5]], 0).astype(BF)
    tr = nn(last, wall_onehot(wall_ref[...])).astype(BF)
    for j in range(out_ref.shape[0]):
        out_ref[j] = tr


def prep_kernel(vel_ref, stiff_ref, curl_ref, conn_ref, far_ref, *refs):
    va_ref, vb_ref, so_ref, sp_ref, co_ref, cp_ref, tall_ref, wide_ref, ws_ref, wc_ref = refs
    vel = [vel_ref[c].astype(F32) for c in range(3)]
    zero = jnp.zeros_like(vel[0])
    va_ref[...] = jnp.concatenate([vel[0], vel[1], vel[2], zero], 0).T
    vb_ref[...] = jnp.concatenate([vel[1], vel[2], vel[0], zero], 0).T
    row = lax.broadcasted_iota(jnp.int32, (256, 64), 0)
    col = lax.broadcasted_iota(jnp.int32, (256, 64), 1)
    spread = (row % 64 == col).astype(F32).astype(BF)
    near = lax.broadcasted_iota(jnp.int32, (256, 256), 0) // 64
    same = near == lax.broadcasted_iota(jnp.int32, (256, 256), 1) // 64

    def blocks(ref, sign):
        once = nt(spread, ref[...].astype(BF)).astype(BF)
        return jnp.where(same, sign * nt(once, spread), 0.0).astype(BF)

    stiff = blocks(stiff_ref, -1.0)
    curl = blocks(curl_ref, 1.0)

    def operator(conn, first, width, s_out, c_out):
        conn = conn.astype(F32)
        across = conn.T
        nodes = lax.broadcasted_iota(jnp.int32, (768, 128), 0).astype(F32)
        lanes = lax.broadcasted_iota(jnp.int32, (128, width), 1).astype(F32) + first
        for t in range(8):
            tall_ref[:, 128 * t : 128 * t + 128] = (nodes == conn[t : t + 1]).astype(F32).astype(BF)
            wide_ref[128 * t : 128 * t + 128, :width] = (
                (lanes == across[:, t : t + 1]).astype(F32).astype(BF)
            )
        for u in range(4):
            some = wide_ref[256 * u : 256 * u + 256, :width]
            ws_ref[256 * u : 256 * u + 256, :width] = nn(stiff, some).astype(BF)
            wc_ref[256 * u : 256 * u + 256, :width] = nn(curl, some).astype(BF)
        tall = tall_ref[...]
        return nn(tall, ws_ref[:, :width]), nn(tall, wc_ref[:, :width])

    s_far, c_far = operator(far_ref[...], 512.0, 256, None, None)
    sp_ref[...] = s_far[:512].astype(BF)
    cp_ref[...] = c_far[:512].astype(BF)
    s_own, c_own = operator(conn_ref[...], 0.0, 512, None, None)
    so_ref[...] = s_own.astype(BF)
    co_ref[...] = c_own.astype(BF)
    so_ref[:256, :256] = (s_own[:256, :256] + s_far[512:]).astype(BF)
    co_ref[:256, :256] = (c_own[:256, :256] + c_far[512:]).astype(BF)


def induce_kernel(moved_ref, va_ref, vb_ref, fwd_ref, inv_ref, out_ref):
    rows = moved_ref[...].reshape(256, 128)
    turned = pltpu.roll(rows.astype(F32), 96, 1).astype(BF)
    here = nn(fwd_ref[...], rows)
    after = nn(fwd_ref[...], turned)
    cross = va_ref[...] * after - vb_ref[...] * here
    back = nn(inv_ref[...], cross.astype(BF))
    out_ref[...] = back.astype(BF).reshape(16, 16, 128)


def section_rows(refs, mode_ref):
    (field_ref, fp_ref, fn_ref, emf_ref, ep_ref, en_ref, so_ref, sp_ref, co_ref, cp_ref) = refs[:10]
    tr_ref, dtn_ref, wall_ref, mass_ref = refs[10:14]
    order = [3 * p + c for c in range(3) for p in range(2)]
    field = jnp.concatenate([field_ref[s] for s in order], 0)
    f_own = jnp.concatenate([field.astype(BF), unpack(fn_ref, 8)], 1)
    e_own = jnp.concatenate([unpack(emf_ref, 16), unpack(en_ref, 8)], 1)
    total = nn(f_own, so_ref[...]) + nn(e_own, co_ref[...])
    low = nn(unpack(fp_ref, 16), sp_ref[...]) + nn(unpack(ep_ref, 16), cp_ref[...])
    total = jnp.concatenate([total[:, :256] + low, total[:, 256:]], 1)
    whole = jnp.concatenate([tr_ref[2 * a] + tr_ref[2 * a + 1] for a in range(16)], 1)
    every = nt(whole, dtn_ref[...].reshape(512, 2048))
    mine = lax.broadcasted_iota(jnp.int32, (16, 512), 0) % 8
    every = jnp.where(mine == lax.broadcasted_iota(jnp.int32, (16, 512), 1) // 64, every, 0.0)
    flux = every[:, :128] + every[:, 128:256] + every[:, 256:384] + every[:, 384:]
    flux = flux + pltpu.roll(flux, 64, 1)
    onehot = wall_onehot(wall_ref[...])
    upper = flux.astype(BF)
    added = nt(upper, onehot) + nt((flux - upper.astype(F32)).astype(BF), onehot)
    total = jnp.concatenate([total[:32], total[32:] - 0.5 * added], 0)
    number = lax.broadcasted_iota(jnp.int32, (48, 512), 0) % 8 + 8 * mode_ref[0]
    coef = (number.astype(F32) / 128.0) ** 2
    rate = total / mass_ref[...] - 4.0 * coef * field
    return rate, field, flux, onehot


def first_kernel(mode_ref, *refs):
    sect_ref, pack_ref, trace_ref, flux_ref = refs[14:]
    rate, field, flux, onehot = section_rows(refs, mode_ref)
    sect = field + 0.2 * rate
    flux_ref[...] = flux
    rows = {(c, p): sect[16 * c + 8 * p : 16 * c + 8 * p + 8] for c in range(3) for p in range(2)}
    for (c, p), r in rows.items():
        sect_ref[3 * p + c] = r
    pack(rows, pack_ref)
    tr = nn(sect[32:].astype(BF), onehot).astype(BF)
    for j in range(trace_ref.shape[0]):
        trace_ref[j] = tr


def second_kernel(mode_ref, *refs):
    start_ref, first_flux_ref, out_ref, flux_ref = refs[14:]
    rate, sect, flux, onehot = section_rows(refs, mode_ref)
    for c in range(3):
        for p in range(2):
            at = slice(16 * c + 8 * p, 16 * c + 8 * p + 8)
            out_ref[3 * p + c] = 0.5 * (start_ref[3 * p + c] + sect[at] + 0.2 * rate[at])
    for p in range(2):
        flux_ref[0, :, p, :] = first_flux_ref[8 * p : 8 * p + 8, :64]
        flux_ref[1, :, p, :] = flux[8 * p : 8 * p + 8, :64]


def shapes(*items):
    return [jax.ShapeDtypeStruct(s, d) for s, d in items]


def call(kernel, out, scratch=(), scalars=0, n_in=0, cost=None):
    vmem = pl.BlockSpec(memory_space=pltpu.VMEM)
    smem = pl.BlockSpec(memory_space=pltpu.SMEM)
    return pl.pallas_call(
        kernel,
        out_shape=out,
        in_specs=[smem] * scalars + [vmem] * (n_in - scalars),
        out_specs=jax.tree.map(lambda _: vmem, out),
        scratch_shapes=list(scratch),
        compiler_params=PARAMS,
        cost_estimate=cost,
    )


def body(field, velocity, stiffness, curl_matrix, mass, connect, wall_index, dtn):
    fwd, inv = tables(128, 256, 8)
    spots = lax.axis_size("mer")
    mine = lax.axis_index("mer")
    mode = lax.axis_index("mode").astype(jnp.int32).reshape(1)
    up = [(i, i + 1) for i in range(spots - 1)]
    down = [(i + 1, i) for i in range(spots - 1)]
    start = jnp.transpose(field, (1, 0, 2))
    conn = connect.reshape(8, 128)
    conn_far = lax.ppermute(conn, "mer", up)
    twice = jnp.concatenate([wall_index, wall_index])
    wall = jnp.where(jnp.arange(128) // 64 == mine % 2, twice, -1).reshape(1, 128)
    row = mass.reshape(1, 512)

    packed = call(pack_kernel, shapes(((16, 16, 128), BF))[0], n_in=1)(start)
    trace = call(trace_kernel, shapes(((spots, 16, 128), BF))[0], n_in=2)(start, wall)
    va, vb, s_own, s_far, c_own, c_far = call(
        prep_kernel,
        shapes(
            ((256, 128), F32), ((256, 128), F32),
            ((768, 512), BF), ((512, 256), BF), ((768, 512), BF), ((512, 256), BF),
        ),
        scratch=[pltpu.VMEM((768, 1024), BF)] + [pltpu.VMEM((1024, 512), BF)] * 3,
        n_in=5,
    )(jnp.transpose(velocity, (0, 2, 1)), stiffness, curl_matrix, conn, conn_far)

    def section(now, packed, trace, last):
        moved = lax.all_to_all(packed, "mode", 0, 0, tiled=True)
        f_prev = lax.ppermute(packed, "mer", up)
        f_next = lax.ppermute(packed, "mer", down)
        back = call(induce_kernel, shapes(((16, 16, 128), BF))[0], n_in=5)(moved, va, vb, fwd, inv)
        emf = lax.all_to_all(back, "mode", 0, 0, tiled=True)
        e_prev = lax.ppermute(emf, "mer", up)
        e_next = lax.ppermute(emf, "mer", down)
        whole = lax.all_to_all(trace, "mer", 0, 0, tiled=True)
        args = (mode, now, f_prev, f_next, emf, e_prev, e_next, s_own, s_far, c_own, c_far)
        args += (whole, dtn, wall, row)
        if last is None:
            out = shapes(((6, 8, 512), F32), ((16, 16, 128), BF), ((spots, 16, 128), BF), ((16, 128), F32))
            return call(first_kernel, out, scalars=1, n_in=len(args))(*args)
        out = shapes(((6, 8, 512), F32), ((2, 8, 2, 64), F32))
        return call(second_kernel, out, scalars=1, n_in=len(args) + 2)(*args, *last)

    sect, packed, trace, flux = section(start, packed, trace, None)
    done, fluxes = section(sect, packed, trace, (start, flux))
    return (jnp.transpose(done, (1, 0, 2)), fluxes)


def solution(mesh):
    placed = (
        P("mode", None, "mer"),
        P(None, None, ("mer", "mode")),
        P(),
        P(),
        P("mer"),
        P("mer", None),
        P("mer"),
        P("mode", "mer", None),
    )
    return jax.shard_map(
        body,
        mesh=mesh,
        in_specs=placed,
        out_specs=(P("mode", None, "mer"), P(None, "mode", None, "mer")),
        check_vma=False,
    )
```

```python
import numpy as np
import jax
import jax.numpy as jnp
from jax import lax
from jax.experimental import pallas as pl
from jax.experimental.pallas import tpu as pltpu
from jax.sharding import PartitionSpec as P


BF = jnp.bfloat16
F32 = jnp.float32


def nt(a, b):
    return lax.dot_general(a, b, (((1,), (1,)), ((), ())), preferred_element_type=F32)


def nn(a, b):
    return jnp.dot(a, b, preferred_element_type=F32)


def tables(modes, nphi, mode_dev):
    mode = np.arange(modes).reshape(-1, 1, mode_dev)
    k = np.arange(nphi).reshape(-1, 1, 1, 1)
    angle = 2.0 * np.pi * ((mode[None] * k) % nphi) / nphi
    fwd = np.concatenate([np.cos(angle), -np.sin(angle)], 2).reshape(nphi, 2 * modes)
    return fwd.astype(BF), (fwd.T / nphi).astype(BF)


def lane_group(shape):
    return lax.broadcasted_iota(jnp.int32, shape, len(shape) - 1) // 32


def pick(group, parts):
    out = parts[0]
    for g, part in enumerate(parts[1:], 1):
        out = jnp.where(group == g, part, out)
    return out


def shift(x, groups):
    return x if groups % 4 == 0 else pltpu.roll(x, 32 * (groups % 4), 1)


def pack(rows, out_ref):
    group = lane_group((8, 128))
    for v in range(4):
        tiles = {cp: r[:, 128 * v : 128 * v + 128] for cp, r in rows.items()}
        for q in range(4):
            halves = [
                pick(group, [shift(tiles[c % 3, p], c - q) for c in range(4)]) for p in range(2)
            ]
            out_ref[4 * v + q] = jnp.concatenate(halves, 0).astype(BF)


def unpack(tile, slots):
    group = lane_group((16, 128))
    cols = []
    for v in range(slots // 4):
        tiles = [tile(4 * v + q).astype(F32) for q in range(4)]
        cols.append(
            jnp.concatenate(
                [pick(group, [shift(tiles[q], q - c) for q in range(4)]) for c in range(3)], 0
            ).astype(BF)
        )
    return jnp.concatenate(cols, 1)


def wall_onehot(wall_ref, mer):
    twice = jnp.concatenate([wall_ref[...], wall_ref[...]], 1)
    nodes = lax.broadcasted_iota(jnp.int32, (512, 128), 0)
    half = lax.broadcasted_iota(jnp.int32, (512, 128), 1) // 64
    return jnp.where(half == mer % 2, (nodes == twice).astype(F32), 0.0).astype(BF)


def two_by_two(conn_ref):
    return jnp.concatenate([conn_ref[pl.ds(0, 8, 2), :], conn_ref[pl.ds(1, 8, 2), :]], 1)


def open_kernel(mer_ref, field_ref, wall_ref, conn_ref, pack_ref, out_ref):
    pack({(c, p): field_ref[3 * p + c] for c in range(3) for p in range(2)}, pack_ref)
    last = jnp.concatenate([field_ref[2], field_ref[5]], 0).astype(BF)
    tr = nn(last, wall_onehot(wall_ref, mer_ref[0]))
    conn = two_by_two(conn_ref)
    parts = [tr, (conn // 32).astype(F32), (conn % 32).astype(F32)]
    parts = jnp.concatenate(parts, 0).astype(BF)
    for j in range(out_ref.shape[0]):
        out_ref[j] = parts


def element_blocks(ref, sign):
    row = lax.broadcasted_iota(jnp.int32, (256, 64), 0)
    col = lax.broadcasted_iota(jnp.int32, (256, 64), 1)
    spread = (row % 64 == col).astype(F32).astype(BF)
    near = lax.broadcasted_iota(jnp.int32, (256, 256), 0) // 64
    same = near == lax.broadcasted_iota(jnp.int32, (256, 256), 1) // 64
    once = nt(spread, ref[...].astype(BF)).astype(BF)
    return jnp.where(same, sign * nt(once, spread), 0.0).astype(BF)


def operators(conn, first, width, stiff_ref, curl_ref, tall_ref, work_ref):
    across = conn.T
    nodes = lax.broadcasted_iota(jnp.int32, (768, 128), 0).astype(F32)
    lanes = lax.broadcasted_iota(jnp.int32, (128, width), 1).astype(F32) + first
    mats = [element_blocks(stiff_ref, -1.0), element_blocks(curl_ref, 1.0)]
    for t in range(8):
        tall_ref[:, 128 * t : 128 * t + 128] = (nodes == conn[t : t + 1]).astype(F32).astype(BF)
    for u in range(4):
        picks = [
            (lanes == across[:, t : t + 1]).astype(F32).astype(BF) for t in (2 * u, 2 * u + 1)
        ]
        picks = jnp.concatenate(picks, 0)
        for k, mat in enumerate(mats):
            work_ref[k, 256 * u : 256 * u + 256] = nn(mat, picks).astype(BF)
    return nn(tall_ref[...], work_ref[0]), nn(tall_ref[...], work_ref[1])


def own_kernel(vel_ref, stiff_ref, curl_ref, conn_ref, va_ref, vb_ref, s_ref, near_ref, tall_ref, work_ref):
    vel = [vel_ref[c].astype(F32) for c in range(3)]
    zero = jnp.zeros_like(vel[0])
    va_ref[...] = jnp.concatenate([vel[0], vel[1], vel[2], zero], 0).T.astype(BF)
    vb_ref[...] = jnp.concatenate([vel[1], vel[2], vel[0], zero], 0).T.astype(BF)
    conn = two_by_two(conn_ref).astype(F32)
    s, c = operators(conn, 0.0, 512, stiff_ref, curl_ref, tall_ref, work_ref)
    s_ref[...] = s[:512].astype(BF)
    near_ref[:768] = c.astype(BF)
    near_ref[768:] = s[512:].astype(BF)


def far_kernel(mer_ref, whole_ref, stiff_ref, curl_ref, far_ref, tall_ref, work_ref):
    code = whole_ref[jnp.maximum(mer_ref[0] - 1, 0)].astype(F32)
    conn = 32.0 * code[16:24] + code[24:32]
    s, c = operators(conn, 512.0, 256, stiff_ref, curl_ref, tall_ref, work_ref)
    there = jnp.where(mer_ref[0] > 0, 1.0, 0.0)
    far_ref[:768] = (c * there).astype(BF)
    far_ref[768:] = (s * there).astype(BF)


def induce_kernel(moved_ref, va_ref, vb_ref, fwd_ref, inv_ref, out_ref):
    moved = moved_ref[...]
    rows = moved.reshape(256, 128)
    turned = pltpu.roll(rows.astype(F32), 96, 1).astype(BF)
    here = nn(fwd_ref[...], rows)
    after = nn(fwd_ref[...], turned)
    cross = va_ref[...].astype(F32) * after - vb_ref[...].astype(F32) * here
    back = nn(inv_ref[...], cross.astype(BF))
    out_ref[:, :16] = back.astype(BF).reshape(16, 16, 128)
    out_ref[:, 16:] = moved


ORDER = [3 * p + c for c in range(3) for p in range(2)]


def stiff_kernel(field_ref, s_ref, out_ref):
    field = jnp.concatenate([field_ref[s] for s in ORDER], 0)
    out_ref[...] = nn(field.astype(BF), s_ref[...])


def section_rows(refs, scratch):
    mode_ref, mer_ref, field_ref, part_ref, emf_ref, pa_ref, pb_ref, whole_ref, wall_ref, mass_ref = refs[:10]
    near_ref, far_ref, dtn_ref = refs[10:13]
    near_buf, far_buf, dtn_buf, sems = scratch
    copies = [
        pltpu.make_async_copy(a, b, sems.at[k])
        for k, (a, b) in enumerate(((near_ref, near_buf), (far_ref, far_buf), (dtn_ref, dtn_buf)))
    ]
    for copy in copies:
        copy.start()
    odd = (jnp.zeros((16, 128), jnp.int32) + mer_ref[0] % 2) == 1

    def before(part):
        rows = slice(16 * part, 16 * part + 16)
        return lambda s: jnp.where(odd, pa_ref[s, rows].astype(F32), pb_ref[s, rows].astype(F32))

    def behind(part):
        rows = slice(16 * part, 16 * part + 16)
        return lambda s: jnp.where(odd, pb_ref[s, rows].astype(F32), pa_ref[s, rows].astype(F32))

    field = jnp.concatenate([field_ref[s] for s in ORDER], 0)
    own = unpack(lambda s: emf_ref[s, :16], 16)
    near = jnp.concatenate([own, unpack(behind(0), 8), unpack(behind(1), 8)], 1)
    far = jnp.concatenate([unpack(before(0), 16), own[:, :256], unpack(before(1), 16), field[:, :256].astype(BF)], 1)
    copies[0].wait()
    total = part_ref[...] + nn(near, near_buf[...])
    copies[1].wait()
    low = nn(far, far_buf[...])
    total = jnp.concatenate([total[:, :256] + low, total[:, 256:]], 1)
    whole = jnp.concatenate([whole_ref[2 * a, :16] + whole_ref[2 * a + 1, :16] for a in range(16)], 1)
    copies[2].wait()
    every = nt(whole, dtn_buf[...].reshape(512, 2048))
    mine = lax.broadcasted_iota(jnp.int32, (16, 512), 0) % 8
    every = jnp.where(mine == lax.broadcasted_iota(jnp.int32, (16, 512), 1) // 64, every, 0.0)
    flux = every[:, :128] + every[:, 128:256] + every[:, 256:384] + every[:, 384:]
    flux = flux + pltpu.roll(flux, 64, 1)
    onehot = wall_onehot(wall_ref, mer_ref[0])
    upper = flux.astype(BF)
    added = nt(upper, onehot) + nt((flux - upper.astype(F32)).astype(BF), onehot)
    total = jnp.concatenate([total[:32], total[32:] - 0.5 * added], 0)
    number = lax.broadcasted_iota(jnp.int32, (48, 512), 0) % 8 + 8 * mode_ref[0]
    coef = (number.astype(F32) / 128.0) ** 2
    rate = total / mass_ref[...] - 4.0 * coef * field
    return rate, field, flux, onehot


def first_kernel(*refs):
    sect_ref, pack_ref, trace_ref, flux_ref = refs[13:17]
    rate, field, flux, onehot = section_rows(refs, refs[17:])
    sect = field + 0.2 * rate
    flux_ref[...] = flux
    rows = {(c, p): sect[16 * c + 8 * p : 16 * c + 8 * p + 8] for c in range(3) for p in range(2)}
    for (c, p), r in rows.items():
        sect_ref[3 * p + c] = r
    pack(rows, pack_ref)
    tr = nn(sect[32:].astype(BF), onehot).astype(BF)
    for j in range(trace_ref.shape[0]):
        trace_ref[j] = tr


def second_kernel(*refs):
    start_ref, first_flux_ref, out_ref, flux_ref = refs[13:17]
    rate, sect, flux, onehot = section_rows(refs, refs[17:])
    for c in range(3):
        for p in range(2):
            at = slice(16 * c + 8 * p, 16 * c + 8 * p + 8)
            out_ref[3 * p + c] = 0.5 * (start_ref[3 * p + c] + sect[at] + 0.2 * rate[at])
    for p in range(2):
        flux_ref[0, :, p, :] = first_flux_ref[8 * p : 8 * p + 8, :64]
        flux_ref[1, :, p, :] = flux[8 * p : 8 * p + 8, :64]


def call(kernel, out, where, scratch=(), limit=16):
    spec = {k: pl.BlockSpec(memory_space=pltpu.VMEM) for k in "vc"}
    spec["s"] = pl.BlockSpec(memory_space=pltpu.SMEM)
    spec["h"] = pl.BlockSpec(memory_space=pl.ANY)
    made = pl.pallas_call(
        kernel,
        out_shape=[pltpu.VMEM(s, d) if near else jax.ShapeDtypeStruct(s, d) for s, d, near in out],
        in_specs=[spec[k] for k in where],
        out_specs=[spec["v"]] * len(out),
        scratch_shapes=list(scratch),
        compiler_params=pltpu.CompilerParams(vmem_limit_bytes=limit * 2**20),
    )

    def run(*args):
        return made(
            *[
                pltpu.with_memory_space_constraint(a, pltpu.VMEM) if k == "v" else a
                for k, a in zip(where, args, strict=True)
            ]
        )

    return run


def body(field, velocity, stiffness, curl_matrix, mass, connect, wall_index, dtn):
    fwd, inv = tables(128, 256, 8)
    spots = lax.axis_size("mer")
    mer = lax.axis_index("mer").astype(jnp.int32).reshape(1)
    mode = lax.axis_index("mode").astype(jnp.int32).reshape(1)
    start = jnp.transpose(field, (1, 0, 2))
    wall = wall_index.reshape(1, 64)
    row = mass.reshape(1, 512)
    works = [pltpu.VMEM((768, 1024), BF), pltpu.VMEM((2, 1024, 512), BF)]

    packed, trace = call(
        open_kernel, [((16, 16, 128), BF, True), ((spots, 32, 128), BF, True)], "sccc"
    )(mer, start, wall, connect)
    va, vb, s_own, near = call(
        own_kernel,
        [((256, 128), BF, False)] * 2 + [((512, 512), BF, False), ((1024, 512), BF, False)],
        "cccc",
        works,
        32,
    )(jnp.transpose(velocity, (0, 2, 1)), stiffness, curl_matrix, connect)

    twins = [(i, i ^ 1) for i in range(spots)]
    others = [(i, ((i + 1) ^ 1) - 1) for i in range(1, spots - 1)]

    def section(now, packed, trace, far, last):
        whole = lax.all_to_all(trace, "mer", 0, 0, tiled=True)
        if far is None:
            works[1] = pltpu.VMEM((2, 1024, 256), BF)
            (far,) = call(far_kernel, [((1536, 256), BF, False)], "sccc", works, 32)(
                mer, whole, stiffness, curl_matrix
            )
        moved = lax.all_to_all(packed, "mode", 0, 0, tiled=True)
        (back,) = call(induce_kernel, [((16, 32, 128), BF, True)], "vvvvv")(moved, va, vb, fwd, inv)
        emf = lax.all_to_all(back, "mode", 0, 0, tiled=True)
        (part,) = call(stiff_kernel, [((48, 512), F32, True)], "cc")(now, s_own)
        e_twin = lax.ppermute(emf, "mer", twins)
        e_other = lax.ppermute(emf, "mer", others)
        args = (mode, mer, now, part, emf, e_twin, e_other, whole, wall, row, near, far, dtn)
        kinds = "ss" + ("c" if last is None else "v") + "vvvvvcchhh"
        bufs = [
            pltpu.VMEM((1024, 512), BF),
            pltpu.VMEM((1536, 256), BF),
            pltpu.VMEM((8, 64, 2048), BF),
            pltpu.SemaphoreType.DMA((3,)),
        ]
        if last is None:
            out = [((6, 8, 512), F32, True), ((16, 16, 128), BF, True)]
            out += [((spots, 16, 128), BF, True), ((16, 128), F32, False)]
            return far, call(first_kernel, out, kinds, bufs)(*args)
        out = [((6, 8, 512), F32, False), ((2, 8, 2, 64), F32, False)]
        return far, call(second_kernel, out, kinds + "cc", bufs)(*args, *last)

    far, (sect, packed, trace, flux) = section(start, packed, trace, None, None)
    far, (done, fluxes) = section(sect, packed, trace, far, (start, flux))
    return (jnp.transpose(done, (1, 0, 2)), fluxes)


def solution(mesh):
    placed = (
        P("mode", None, "mer"),
        P(None, None, ("mer", "mode")),
        P(),
        P(),
        P("mer"),
        P("mer", None),
        P("mer"),
        P("mode", "mer", None),
    )
    return jax.shard_map(
        body,
        mesh=mesh,
        in_specs=placed,
        out_specs=(P("mode", None, "mer"), P(None, "mode", None, "mer")),
        check_vma=False,
    )
```

```python
import numpy as np
import jax
import jax.numpy as jnp
from jax import lax
from jax.experimental import pallas as pl
from jax.experimental.pallas import tpu as pltpu
from jax.sharding import PartitionSpec as P


BF = jnp.bfloat16
F32 = jnp.float32


def nt(a, b):
    return lax.dot_general(a, b, (((1,), (1,)), ((), ())), preferred_element_type=F32)


def nn(a, b):
    return jnp.dot(a, b, preferred_element_type=F32)


def tables(modes, nphi, mode_dev):
    mode = np.arange(modes).reshape(-1, 1, mode_dev)
    k = np.arange(nphi).reshape(-1, 1, 1, 1)
    angle = 2.0 * np.pi * ((mode[None] * k) % nphi) / nphi
    fwd = np.concatenate([np.cos(angle), -np.sin(angle)], 2).reshape(nphi, 2 * modes)
    return fwd.astype(BF), (fwd.T / nphi).astype(BF)


def lane_group(shape):
    return lax.broadcasted_iota(jnp.int32, shape, len(shape) - 1) // 32


def pick(group, parts):
    out = parts[0]
    for g, part in enumerate(parts[1:], 1):
        out = jnp.where(group == g, part, out)
    return out


def shift(x, groups):
    return x if groups % 4 == 0 else pltpu.roll(x, 32 * (groups % 4), 1)


def pack(rows, out_ref):
    group = lane_group((8, 128))
    for v in range(4):
        tiles = {cp: r[:, 128 * v : 128 * v + 128] for cp, r in rows.items()}
        for q in range(4):
            halves = [
                pick(group, [shift(tiles[c % 3, p], c - q) for c in range(4)]) for p in range(2)
            ]
            out_ref[4 * v + q] = jnp.concatenate(halves, 0).astype(BF)


def unpack(tile, slots):
    group = lane_group((16, 128))
    cols = []
    for v in range(slots // 4):
        tiles = [tile(4 * v + q).astype(F32) for q in range(4)]
        cols.append(
            jnp.concatenate(
                [pick(group, [shift(tiles[q], q - c) for q in range(4)]) for c in range(3)], 0
            ).astype(BF)
        )
    return jnp.concatenate(cols, 1)


def wall_onehot(wall_ref, mer):
    twice = jnp.concatenate([wall_ref[...], wall_ref[...]], 1)
    nodes = lax.broadcasted_iota(jnp.int32, (512, 128), 0)
    half = lax.broadcasted_iota(jnp.int32, (512, 128), 1) // 64
    return jnp.where(half == mer % 2, (nodes == twice).astype(F32), 0.0).astype(BF)


def two_by_two(conn_ref):
    return jnp.concatenate([conn_ref[pl.ds(0, 8, 2), :], conn_ref[pl.ds(1, 8, 2), :]], 1)


def open_kernel(mer_ref, field, wall, conn, pack_ref, out_ref):
    onehot = wall_onehot(wall(), mer_ref[0])
    conn = two_by_two(conn())
    field_ref = field()
    pack({(c, p): field_ref[3 * p + c] for c in range(3) for p in range(2)}, pack_ref)
    last = jnp.concatenate([field_ref[2], field_ref[5]], 0).astype(BF)
    tr = nn(last, onehot)
    parts = [tr, (conn // 32).astype(F32), (conn % 32).astype(F32)]
    parts = jnp.concatenate(parts, 0).astype(BF)
    for j in range(out_ref.shape[0]):
        out_ref[j] = parts


def gate_kernel(packed_ref, whole_ref, near_ref, out_ref):
    out_ref[...] = packed_ref[...]


def element_blocks(ref, sign):
    row = lax.broadcasted_iota(jnp.int32, (256, 64), 0)
    col = lax.broadcasted_iota(jnp.int32, (256, 64), 1)
    spread = (row % 64 == col).astype(F32).astype(BF)
    near = lax.broadcasted_iota(jnp.int32, (256, 256), 0) // 64
    same = near == lax.broadcasted_iota(jnp.int32, (256, 256), 1) // 64
    once = nt(spread, ref[...].astype(BF)).astype(BF)
    return jnp.where(same, sign * nt(once, spread), 0.0).astype(BF)


def operators(conn, first, width, stiff_ref, curl_ref, tall_ref, work_ref):
    across = conn.T
    nodes = lax.broadcasted_iota(jnp.int32, (768, 128), 0).astype(F32)
    lanes = lax.broadcasted_iota(jnp.int32, (128, width), 1).astype(F32) + first
    mats = [element_blocks(stiff_ref, -1.0), element_blocks(curl_ref, 1.0)]
    for t in range(8):
        tall_ref[:, 128 * t : 128 * t + 128] = (nodes == conn[t : t + 1]).astype(F32).astype(BF)
    for u in range(4):
        picks = [
            (lanes == across[:, t : t + 1]).astype(F32).astype(BF) for t in (2 * u, 2 * u + 1)
        ]
        picks = jnp.concatenate(picks, 0)
        for k, mat in enumerate(mats):
            work_ref[k, 256 * u : 256 * u + 256] = nn(mat, picks).astype(BF)
    return nn(tall_ref[...], work_ref[0]), nn(tall_ref[...], work_ref[1])


def own_kernel(vel, stiff, curl, conn, fwd, inv, *refs):
    va_ref, vb_ref, fwd_ref, inv_ref, near_out, near_ref, tall_ref, work_ref, sem = refs
    conn = two_by_two(conn()).astype(F32)
    s, c = operators(conn, 0.0, 512, stiff(), curl(), tall_ref, work_ref)
    near_ref[:768] = c.astype(BF)
    near_ref[768:] = s.astype(BF)
    copy = pltpu.make_async_copy(near_ref, near_out, sem)
    copy.start()
    vel_ref = vel()
    vel = [vel_ref[c].astype(F32) for c in range(3)]
    zero = jnp.zeros_like(vel[0])
    va_ref[...] = jnp.concatenate([vel[0], vel[1], vel[2], zero], 0).T.astype(BF)
    vb_ref[...] = jnp.concatenate([vel[1], vel[2], vel[0], zero], 0).T.astype(BF)
    fwd_ref[...] = fwd()[...]
    inv_ref[...] = inv()[...]
    copy.wait()


def far_kernel(mer_ref, whole_ref, stiff, curl, far_out, far_ref, tall_ref, work_ref, sem):
    code = whole_ref[jnp.maximum(mer_ref[0] - 1, 0)].astype(F32)
    conn = 32.0 * code[16:24] + code[24:32]
    s, c = operators(conn, 512.0, 256, stiff(), curl(), tall_ref, work_ref)
    there = jnp.where(mer_ref[0] > 0, 1.0, 0.0)
    far_ref[:768] = (c * there).astype(BF)
    far_ref[768:] = (s * there).astype(BF)
    copy = pltpu.make_async_copy(far_ref, far_out, sem)
    copy.start()
    copy.wait()


def induce_kernel(moved_ref, va_ref, vb_ref, fwd_ref, inv_ref, far_ref, out_ref):
    moved = moved_ref[...]
    rows = moved.reshape(256, 128)
    turned = pltpu.roll(rows.astype(F32), 96, 1).astype(BF)
    here = nn(fwd_ref[...], rows)
    after = nn(fwd_ref[...], turned)
    cross = va_ref[...].astype(F32) * after - vb_ref[...].astype(F32) * here
    back = nn(inv_ref[...], cross.astype(BF))
    out_ref[:, :16] = back.astype(BF).reshape(16, 16, 128)
    out_ref[:, 16:] = moved


ORDER = [3 * p + c for c in range(3) for p in range(2)]


def rows_of(field):
    field_ref = field() if callable(field) else field
    return jnp.concatenate([field_ref[s] for s in ORDER], 0)


def operator_kernel(mer_ref, now, emf_ref, pa_ref, pb_ref, near, far, out_ref):
    odd = (jnp.zeros((16, 128), jnp.int32) + mer_ref[0] % 2) == 1

    def before(part):
        rows = slice(16 * part, 16 * part + 16)
        return lambda s: jnp.where(odd, pa_ref[s, rows].astype(F32), pb_ref[s, rows].astype(F32))

    def behind(part):
        rows = slice(16 * part, 16 * part + 16)
        return lambda s: jnp.where(odd, pb_ref[s, rows].astype(F32), pa_ref[s, rows].astype(F32))

    own = unpack(lambda s: emf_ref[s, :16], 16)
    e_next, f_next = unpack(behind(0), 8), unpack(behind(1), 8)
    e_prev, f_prev = unpack(before(0), 16), unpack(before(1), 16)
    field = rows_of(now).astype(BF)
    total = nn(jnp.concatenate([own, e_next, field, f_next], 1), near()[...])
    low = nn(jnp.concatenate([e_prev, own[:, :256], f_prev, field[:, :256]], 1), far()[...])
    out_ref[...] = jnp.concatenate([total[:, :256] + low, total[:, 256:]], 1)


def finish(mode_ref, mer_ref, now, total_ref, whole_ref, wall, mass, dtn):
    onehot = wall_onehot(wall(), mer_ref[0])
    field = rows_of(now)
    number = lax.broadcasted_iota(jnp.int32, (48, 512), 0) % 8 + 8 * mode_ref[0]
    coef = (number.astype(F32) / 128.0) ** 2
    whole = jnp.concatenate([whole_ref[2 * a, :16] + whole_ref[2 * a + 1, :16] for a in range(16)], 1)
    weight = 1.0 / mass()[...]
    every = nt(whole, dtn()[...].reshape(512, 2048))
    mine = lax.broadcasted_iota(jnp.int32, (16, 512), 0) % 8
    every = jnp.where(mine == lax.broadcasted_iota(jnp.int32, (16, 512), 1) // 64, every, 0.0)
    flux = every[:, :128] + every[:, 128:256] + every[:, 256:384] + every[:, 384:]
    flux = flux + pltpu.roll(flux, 64, 1)
    upper = flux.astype(BF)
    added = nt(upper, onehot) + nt((flux - upper.astype(F32)).astype(BF), onehot)
    total = total_ref[...]
    total = jnp.concatenate([total[:32], total[32:] - 0.5 * added], 0)
    rate = total * weight - 4.0 * coef * field
    return rate, field, flux, onehot


def first_kernel(*refs):
    sect_ref, pack_ref, trace_ref, flux_ref = refs[8:]
    rate, field, flux, onehot = finish(*refs[:8])
    sect = field + 0.2 * rate
    flux_ref[...] = flux
    rows = {(c, p): sect[16 * c + 8 * p : 16 * c + 8 * p + 8] for c in range(3) for p in range(2)}
    for (c, p), r in rows.items():
        sect_ref[3 * p + c] = r
    pack(rows, pack_ref)
    tr = nn(sect[32:].astype(BF), onehot).astype(BF)
    for j in range(trace_ref.shape[0]):
        trace_ref[j] = tr


def second_kernel(*refs):
    start, first_flux_ref, out_ref, flux_ref = refs[8:]
    rate, sect, flux, onehot = finish(*refs[:8])
    start_ref = start()
    for c in range(3):
        for p in range(2):
            at = slice(16 * c + 8 * p, 16 * c + 8 * p + 8)
            out_ref[3 * p + c] = 0.5 * (start_ref[3 * p + c] + sect[at] + 0.2 * rate[at])
    for p in range(2):
        flux_ref[0, :, p, :] = first_flux_ref[8 * p : 8 * p + 8, :64]
        flux_ref[1, :, p, :] = flux[8 * p : 8 * p + 8, :64]


def call(kernel, out, where, args, scratch=(), limit=16):
    count = len(where)
    brought = [a for a, k in zip(args, where, strict=True) if k == "c"]

    def run(*refs):
        inner, sems, bufs = refs, None, []
        if brought:
            inner, sems = refs[: -len(brought) - 1], refs[-len(brought) - 1]
            bufs = refs[-len(brought) :]
        near, copies = [], []
        for ref, k in zip(inner[:count], where, strict=True):
            if k == "c":
                n = len(copies)
                copies.append(pltpu.make_async_copy(ref, bufs[n], sems.at[n]))
                copies[n].start()
                near.append(later(copies[n], bufs[n]))
            else:
                near.append(ref)
        kernel(*near, *inner[count:])

    spaces = {"s": pltpu.SMEM, "v": pltpu.VMEM, "c": pltpu.HBM, "h": pltpu.HBM}
    extra = [pltpu.SemaphoreType.DMA((len(brought),))] if brought else []
    extra += [pltpu.VMEM(a.shape, a.dtype) for a in brought]
    return pl.pallas_call(
        run,
        out_shape=[space(s, d) if space else jax.ShapeDtypeStruct(s, d) for s, d, space in out],
        in_specs=[pl.BlockSpec(memory_space=spaces[k]) for k in where],
        out_specs=[pl.BlockSpec(memory_space=space or pltpu.VMEM) for _, _, space in out],
        scratch_shapes=[*scratch, *extra],
        compiler_params=pltpu.CompilerParams(vmem_limit_bytes=limit * 2**20),
    )(
        *[
            a if k == "s" else pltpu.with_memory_space_constraint(a, spaces[k])
            for k, a in zip(where, args, strict=True)
        ]
    )


def later(copy, buf):
    arrived = []

    def get():
        if not arrived:
            copy.wait()
            arrived.append(True)
        return buf

    return get


def body(field, velocity, stiffness, curl_matrix, mass, connect, wall_index, dtn):
    fwd, inv = tables(128, 256, 8)
    near_space, far_space = pltpu.VMEM, pltpu.HBM
    spots = lax.axis_size("mer")
    mer = lax.axis_index("mer").astype(jnp.int32).reshape(1)
    mode = lax.axis_index("mode").astype(jnp.int32).reshape(1)
    start = jnp.transpose(field, (1, 0, 2))
    wall = wall_index.reshape(1, 64)
    row = mass.reshape(1, 512)
    chunk = ((16, 16, 128), BF, near_space)

    def works(rows, width):
        return [
            pltpu.VMEM((rows, width), BF),
            pltpu.VMEM((768, 1024), BF),
            pltpu.VMEM((2, 1024, width), BF),
            pltpu.SemaphoreType.DMA,
        ]

    packed, trace = call(
        open_kernel, [chunk, ((spots, 32, 128), BF, near_space)], "sccc", (mer, start, wall, connect)
    )
    table = [((256, 128), BF, near_space)] * 2 + [((256, 256), BF, near_space)] * 2
    *table, near = call(
        own_kernel,
        table + [((1536, 512), BF, far_space)],
        "cccccc",
        (jnp.transpose(velocity, (0, 2, 1)), stiffness, curl_matrix, connect, fwd, inv),
        works(1536, 512),
        32,
    )

    twins = [(i, i ^ 1) for i in range(spots)]
    others = [(i, ((i + 1) ^ 1) - 1) for i in range(1, spots - 1)]

    def section(now, packed, whole, far, last):
        moved = lax.all_to_all(packed, "mode", 0, 0, tiled=True)
        (back,) = call(
            induce_kernel, [((16, 32, 128), BF, near_space)], "vvvvvh", (moved, *table, far)
        )
        emf = lax.all_to_all(back, "mode", 0, 0, tiled=True)
        e_twin = lax.ppermute(emf, "mer", twins)
        e_other = lax.ppermute(emf, "mer", others)
        held = "c" if last is None else "v"
        if last is not None:
            whole = lax.all_to_all(whole, "mer", 0, 0, tiled=True)
        (total,) = call(
            operator_kernel,
            [((48, 512), F32, near_space)],
            "s" + held + "vvvcc",
            (mer, now, emf, e_twin, e_other, near, far),
        )
        args = (mode, mer, now, total, whole, wall, row, dtn)
        kinds = "ss" + held + "vvccc"
        if last is None:
            out = [((6, 8, 512), F32, near_space), chunk]
            out += [((spots, 16, 128), BF, near_space), ((16, 128), F32, near_space)]
            return call(first_kernel, out, kinds, args)
        out = [((6, 8, 512), F32, None), ((2, 8, 2, 64), F32, None)]
        return call(second_kernel, out, kinds + "cv", (*args, *last))

    whole = lax.all_to_all(trace, "mer", 0, 0, tiled=True)
    (far,) = call(
        far_kernel,
        [((1536, 256), BF, far_space)],
        "svcc",
        (mer, whole, stiffness, curl_matrix),
        works(1536, 256),
        32,
    )
    (packed,) = call(gate_kernel, [chunk], "vvh", (packed, whole, near))
    sect, packed, trace, flux = section(start, packed, whole, far, None)
    done, fluxes = section(sect, packed, trace, far, (start, flux))
    return (jnp.transpose(done, (1, 0, 2)), fluxes)


def solution(mesh):
    placed = (
        P("mode", None, "mer"),
        P(None, None, ("mer", "mode")),
        P(),
        P(),
        P("mer"),
        P("mer", None),
        P("mer"),
        P("mode", "mer", None),
    )
    return jax.shard_map(
        body,
        mesh=mesh,
        in_specs=placed,
        out_specs=(P("mode", None, "mer"), P(None, "mode", None, "mer")),
        check_vma=False,
    )
```

```python
import numpy as np
import jax
import jax.numpy as jnp
from jax import lax
from jax.experimental import pallas as pl
from jax.experimental.pallas import tpu as pltpu
from jax.sharding import PartitionSpec as P


BF = jnp.bfloat16
F32 = jnp.float32


def nt(a, b):
    return lax.dot_general(a, b, (((1,), (1,)), ((), ())), preferred_element_type=F32)


def nn(a, b):
    return jnp.dot(a, b, preferred_element_type=F32)


def tables(modes, nphi, mode_dev):
    mode = np.arange(modes).reshape(-1, 1, mode_dev)
    k = np.arange(nphi).reshape(-1, 1, 1, 1)
    angle = 2.0 * np.pi * ((mode[None] * k) % nphi) / nphi
    fwd = np.concatenate([np.cos(angle), -np.sin(angle)], 2).reshape(nphi, 2 * modes)
    return fwd.astype(BF), (fwd.T / nphi).astype(BF)


def lane_group(shape):
    return lax.broadcasted_iota(jnp.int32, shape, len(shape) - 1) // 32


def pick(group, parts):
    out = parts[0]
    for g, part in enumerate(parts[1:], 1):
        out = jnp.where(group == g, part, out)
    return out


def shift(x, groups):
    return x if groups % 4 == 0 else pltpu.roll(x, 32 * (groups % 4), 1)


def pack(rows, out_ref):
    group = lane_group((8, 128))
    for v in range(4):
        tiles = {cp: r[:, 128 * v : 128 * v + 128] for cp, r in rows.items()}
        for q in range(4):
            halves = [
                pick(group, [shift(tiles[c % 3, p], c - q) for c in range(4)]) for p in range(2)
            ]
            out_ref[4 * v + q] = jnp.concatenate(halves, 0).astype(BF)


def unpack(tile, slots):
    group = lane_group((16, 128))
    cols = []
    for v in range(slots // 4):
        tiles = [tile(4 * v + q).astype(F32) for q in range(4)]
        cols.append(
            jnp.concatenate(
                [pick(group, [shift(tiles[q], q - c) for q in range(4)]) for c in range(3)], 0
            ).astype(BF)
        )
    return jnp.concatenate(cols, 1)


def wall_onehot(wall_ref, mer):
    twice = jnp.concatenate([wall_ref[...], wall_ref[...]], 1)
    nodes = lax.broadcasted_iota(jnp.int32, (512, 128), 0)
    half = lax.broadcasted_iota(jnp.int32, (512, 128), 1) // 64
    return jnp.where(half == mer % 2, (nodes == twice).astype(F32), 0.0).astype(BF)


def two_by_two(conn_ref):
    return jnp.concatenate([conn_ref[pl.ds(0, 8, 2), :], conn_ref[pl.ds(1, 8, 2), :]], 1)


def open_kernel(mer_ref, field, wall, conn, vel, fwd, inv, pack_ref, out_ref, va_ref, vb_ref, fwd_ref, inv_ref):
    onehot = wall_onehot(wall(), mer_ref[0])
    conn = two_by_two(conn())
    field_ref = field()
    pack({(c, p): field_ref[3 * p + c] for c in range(3) for p in range(2)}, pack_ref)
    vel_ref = vel()
    vel = [vel_ref[c].astype(F32) for c in range(3)]
    zero = jnp.zeros_like(vel[0])
    va_ref[...] = jnp.concatenate([vel[0], vel[1], vel[2], zero], 0).T.astype(BF)
    vb_ref[...] = jnp.concatenate([vel[1], vel[2], vel[0], zero], 0).T.astype(BF)
    fwd_ref[...] = fwd()[...]
    inv_ref[...] = inv()[...]
    last = jnp.concatenate([field_ref[2], field_ref[5]], 0).astype(BF)
    tr = nn(last, onehot)
    parts = [tr, (conn // 32).astype(F32), (conn % 32).astype(F32)]
    parts = jnp.concatenate(parts, 0).astype(BF)
    for j in range(out_ref.shape[0]):
        out_ref[j] = parts


def element_blocks(ref, sign):
    row = lax.broadcasted_iota(jnp.int32, (256, 64), 0)
    col = lax.broadcasted_iota(jnp.int32, (256, 64), 1)
    spread = (row % 64 == col).astype(F32).astype(BF)
    near = lax.broadcasted_iota(jnp.int32, (256, 256), 0) // 64
    same = near == lax.broadcasted_iota(jnp.int32, (256, 256), 1) // 64
    once = nt(spread, ref[...].astype(BF)).astype(BF)
    return jnp.where(same, sign * nt(once, spread), 0.0).astype(BF)


def operators(conn, first, width, stiff_ref, curl_ref, tall_ref, work_ref):
    across = conn.T
    nodes = lax.broadcasted_iota(jnp.int32, (768, 128), 0).astype(F32)
    lanes = lax.broadcasted_iota(jnp.int32, (128, width), 1).astype(F32) + first
    mats = [element_blocks(stiff_ref, -1.0), element_blocks(curl_ref, 1.0)]
    for t in range(8):
        tall_ref[:, 128 * t : 128 * t + 128] = (nodes == conn[t : t + 1]).astype(F32).astype(BF)
    for u in range(4):
        picks = [
            (lanes == across[:, t : t + 1]).astype(F32).astype(BF) for t in (2 * u, 2 * u + 1)
        ]
        picks = jnp.concatenate(picks, 0)
        for k, mat in enumerate(mats):
            work_ref[k, 256 * u : 256 * u + 256] = nn(mat, picks).astype(BF)
    return nn(tall_ref[...], work_ref[0]), nn(tall_ref[...], work_ref[1])


def own_kernel(stiff, curl, conn, emf_ref, near_out, near_ref, tall_ref, work_ref, sem):
    conn = two_by_two(conn()).astype(F32)
    s, c = operators(conn, 0.0, 512, stiff(), curl(), tall_ref, work_ref)
    near_ref[:768] = c.astype(BF)
    near_ref[768:] = s.astype(BF)
    copy = pltpu.make_async_copy(near_ref, near_out, sem)
    copy.start()
    copy.wait()


def induce_kernel(moved_ref, va_ref, vb_ref, fwd_ref, inv_ref, out_ref):
    moved = moved_ref[...]
    rows = moved.reshape(256, 128)
    turned = pltpu.roll(rows.astype(F32), 96, 1).astype(BF)
    here = nn(fwd_ref[...], rows)
    after = nn(fwd_ref[...], turned)
    cross = va_ref[...].astype(F32) * after - vb_ref[...].astype(F32) * here
    back = nn(inv_ref[...], cross.astype(BF))
    out_ref[:, :16] = back.astype(BF).reshape(16, 16, 128)
    out_ref[:, 16:] = moved


ORDER = [3 * p + c for c in range(3) for p in range(2)]


def rows_of(field):
    field_ref = field() if callable(field) else field
    return jnp.concatenate([field_ref[s] for s in ORDER], 0)


def operator_rows(mer_ref, now, emf_ref, pa_ref, pb_ref, near, far):
    odd = (jnp.zeros((16, 128), jnp.int32) + mer_ref[0] % 2) == 1

    def before(part):
        rows = slice(16 * part, 16 * part + 16)
        return lambda s: jnp.where(odd, pa_ref[s, rows].astype(F32), pb_ref[s, rows].astype(F32))

    def behind(part):
        rows = slice(16 * part, 16 * part + 16)
        return lambda s: jnp.where(odd, pb_ref[s, rows].astype(F32), pa_ref[s, rows].astype(F32))

    own = unpack(lambda s: emf_ref[s, :16], 16)
    e_next, f_next = unpack(behind(0), 8), unpack(behind(1), 8)
    e_prev, f_prev = unpack(before(0), 16), unpack(before(1), 16)
    field = rows_of(now).astype(BF)
    total = nn(jnp.concatenate([own, e_next, field, f_next], 1), near()[...])
    low = nn(jnp.concatenate([e_prev, own[:, :256], f_prev, field[:, :256]], 1), far()[...])
    return jnp.concatenate([total[:, :256] + low, total[:, 256:]], 1)


def first_operator_kernel(mer_ref, now, emf_ref, pa_ref, pb_ref, near, whole_ref, stiff, curl, *refs):
    out_ref, far_out, far_ref, tall_ref, work_ref, sem = refs
    code = whole_ref[jnp.maximum(mer_ref[0] - 1, 0)].astype(F32)
    conn = 32.0 * code[16:24] + code[24:32]
    s, c = operators(conn, 512.0, 256, stiff(), curl(), tall_ref, work_ref)
    there = jnp.where(mer_ref[0] > 0, 1.0, 0.0)
    far_ref[:768] = (c * there).astype(BF)
    far_ref[768:] = (s * there).astype(BF)
    copy = pltpu.make_async_copy(far_ref, far_out, sem)
    copy.start()
    out_ref[...] = operator_rows(mer_ref, now, emf_ref, pa_ref, pb_ref, near, lambda: far_ref)
    copy.wait()


def operator_kernel(mer_ref, now, emf_ref, pa_ref, pb_ref, near, far, out_ref):
    out_ref[...] = operator_rows(mer_ref, now, emf_ref, pa_ref, pb_ref, near, far)


def finish(mode_ref, mer_ref, now, total_ref, whole_ref, wall, mass, dtn):
    onehot = wall_onehot(wall(), mer_ref[0])
    field = rows_of(now)
    number = lax.broadcasted_iota(jnp.int32, (48, 512), 0) % 8 + 8 * mode_ref[0]
    coef = (number.astype(F32) / 128.0) ** 2
    whole = jnp.concatenate([whole_ref[2 * a, :16] + whole_ref[2 * a + 1, :16] for a in range(16)], 1)
    weight = 1.0 / mass()[...]
    every = [nt(whole, dtn(k)[2 * k : 2 * k + 2].reshape(128, 2048)) for k in range(4)]
    every = jnp.concatenate(every, 1)
    mine = lax.broadcasted_iota(jnp.int32, (16, 512), 0) % 8
    every = jnp.where(mine == lax.broadcasted_iota(jnp.int32, (16, 512), 1) // 64, every, 0.0)
    flux = every[:, :128] + every[:, 128:256] + every[:, 256:384] + every[:, 384:]
    flux = flux + pltpu.roll(flux, 64, 1)
    upper = flux.astype(BF)
    added = nt(upper, onehot) + nt((flux - upper.astype(F32)).astype(BF), onehot)
    total = total_ref[...]
    total = jnp.concatenate([total[:32], total[32:] - 0.5 * added], 0)
    rate = total * weight - 4.0 * coef * field
    return rate, field, flux, onehot


def first_kernel(*refs):
    sect_ref, pack_ref, trace_ref, flux_ref = refs[8:]
    rate, field, flux, onehot = finish(*refs[:8])
    sect = field + 0.2 * rate
    flux_ref[...] = flux
    rows = {(c, p): sect[16 * c + 8 * p : 16 * c + 8 * p + 8] for c in range(3) for p in range(2)}
    for (c, p), r in rows.items():
        sect_ref[3 * p + c] = r
    pack(rows, pack_ref)
    tr = nn(sect[32:].astype(BF), onehot).astype(BF)
    for j in range(trace_ref.shape[0]):
        trace_ref[j] = tr


def second_kernel(*refs):
    start, first_flux_ref, out_ref, flux_ref = refs[8:]
    rate, sect, flux, onehot = finish(*refs[:8])
    start_ref = start()
    for c in range(3):
        for p in range(2):
            at = slice(16 * c + 8 * p, 16 * c + 8 * p + 8)
            out_ref[3 * p + c] = 0.5 * (start_ref[3 * p + c] + sect[at] + 0.2 * rate[at])
    for p in range(2):
        flux_ref[0, :, p, :] = first_flux_ref[8 * p : 8 * p + 8, :64]
        flux_ref[1, :, p, :] = flux[8 * p : 8 * p + 8, :64]


def call(kernel, out, where, args, scratch=(), limit=16):
    count = len(where)
    brought = [(a, k) for a, k in zip(args, where, strict=True) if k in "cd"]

    def run(*refs):
        inner, sems, bufs = refs, None, []
        if brought:
            inner, sems = refs[: -len(brought) - 1], refs[-len(brought) - 1]
            bufs = list(refs[-len(brought) :])
        near, used = [], 0
        for ref, k in zip(inner[:count], where, strict=True):
            if k not in "cd":
                near.append(ref)
                continue
            buf, copies = bufs.pop(0), []
            for part in range(4 if k == "d" else 1):
                piece = pl.ds(2 * part, 2) if k == "d" else Ellipsis
                src, dst = (ref.at[piece], buf.at[piece]) if k == "d" else (ref, buf)
                copies.append(pltpu.make_async_copy(src, dst, sems.at[used]))
                copies[-1].start()
                used += 1
            near.append(later(copies, buf))
        kernel(*near, *inner[count:])

    spaces = {"s": pltpu.SMEM, "v": pltpu.VMEM, "c": pltpu.HBM, "d": pltpu.HBM}
    waits = sum(4 if k == "d" else 1 for _, k in brought)
    extra = [pltpu.SemaphoreType.DMA((waits,))] if brought else []
    extra += [pltpu.VMEM(a.shape, a.dtype) for a, _ in brought]
    return pl.pallas_call(
        run,
        out_shape=[space(s, d) if space else jax.ShapeDtypeStruct(s, d) for s, d, space in out],
        in_specs=[pl.BlockSpec(memory_space=spaces[k]) for k in where],
        out_specs=[pl.BlockSpec(memory_space=space or pltpu.VMEM) for _, _, space in out],
        scratch_shapes=[*scratch, *extra],
        compiler_params=pltpu.CompilerParams(vmem_limit_bytes=limit * 2**20),
    )(
        *[
            a if k == "s" else pltpu.with_memory_space_constraint(a, spaces[k])
            for k, a in zip(where, args, strict=True)
        ]
    )


def later(copies, buf):
    arrived = set()

    def get(part=0):
        if part not in arrived:
            copies[part].wait()
            arrived.add(part)
        return buf

    return get


def body(field, velocity, stiffness, curl_matrix, mass, connect, wall_index, dtn):
    fwd, inv = tables(128, 256, 8)
    near_space, far_space = pltpu.VMEM, pltpu.HBM
    spots = lax.axis_size("mer")
    mer = lax.axis_index("mer").astype(jnp.int32).reshape(1)
    mode = lax.axis_index("mode").astype(jnp.int32).reshape(1)
    start = jnp.transpose(field, (1, 0, 2))
    wall = wall_index.reshape(1, 64)
    row = mass.reshape(1, 512)
    chunk = ((16, 16, 128), BF, near_space)

    def works(rows, width):
        return [
            pltpu.VMEM((rows, width), BF),
            pltpu.VMEM((768, 1024), BF),
            pltpu.VMEM((2, 1024, width), BF),
            pltpu.SemaphoreType.DMA,
        ]

    table = [((256, 128), BF, near_space)] * 2 + [((256, 256), BF, near_space)] * 2
    packed, trace, *table = call(
        open_kernel,
        [chunk, ((spots, 32, 128), BF, near_space), *table],
        "scccccc",
        (mer, start, wall, connect, jnp.transpose(velocity, (0, 2, 1)), fwd, inv),
    )
    twins = [(i, i ^ 1) for i in range(spots)]
    others = [(i, ((i + 1) ^ 1) - 1) for i in range(1, spots - 1)]

    def exchange(packed, trace):
        moved = lax.all_to_all(packed, "mode", 0, 0, tiled=True)
        (back,) = call(
            induce_kernel, [((16, 32, 128), BF, near_space)], "vvvvv", (moved, *table)
        )
        emf = lax.all_to_all(back, "mode", 0, 0, tiled=True)
        e_twin = lax.ppermute(emf, "mer", twins)
        e_other = lax.ppermute(emf, "mer", others)
        return emf, e_twin, e_other, lax.all_to_all(trace, "mer", 0, 0, tiled=True)

    rows = ((48, 512), F32, near_space)
    emf, e_twin, e_other, whole = exchange(packed, trace)
    (near,) = call(
        own_kernel,
        [((1536, 512), BF, far_space)],
        "cccv",
        (stiffness, curl_matrix, connect, emf),
        works(1536, 512),
        32,
    )
    total, far = call(
        first_operator_kernel,
        [rows, ((1536, 256), BF, far_space)],
        "scvvvcvcc",
        (mer, start, emf, e_twin, e_other, near, whole, stiffness, curl_matrix),
        works(1536, 256),
        32,
    )
    out = [((6, 8, 512), F32, near_space), chunk]
    out += [((spots, 16, 128), BF, near_space), ((16, 128), F32, near_space)]
    sect, packed, trace, flux = call(
        first_kernel, out, "sscvvccd", (mode, mer, start, total, whole, wall, row, dtn)
    )
    emf, e_twin, e_other, whole = exchange(packed, trace)
    (total,) = call(
        operator_kernel, [rows], "svvvvcc", (mer, sect, emf, e_twin, e_other, near, far)
    )
    out = [((6, 8, 512), F32, None), ((2, 8, 2, 64), F32, None)]
    done, fluxes = call(
        second_kernel, out, "ssvvvccdcv", (mode, mer, sect, total, whole, wall, row, dtn, start, flux)
    )
    return (jnp.transpose(done, (1, 0, 2)), fluxes)


def solution(mesh):
    placed = (
        P("mode", None, "mer"),
        P(None, None, ("mer", "mode")),
        P(),
        P(),
        P("mer"),
        P("mer", None),
        P("mer"),
        P("mode", "mer", None),
    )
    return jax.shard_map(
        body,
        mesh=mesh,
        in_specs=placed,
        out_specs=(P("mode", None, "mer"), P(None, "mode", None, "mer")),
        check_vma=False,
    )
```

```python
import numpy as np
import jax
import jax.numpy as jnp
from jax import lax
from jax.experimental import pallas as pl
from jax.experimental.pallas import tpu as pltpu
from jax.sharding import PartitionSpec as P


BF = jnp.bfloat16
F32 = jnp.float32


def nt(a, b):
    return lax.dot_general(a, b, (((1,), (1,)), ((), ())), preferred_element_type=F32)


def nn(a, b):
    return jnp.dot(a, b, preferred_element_type=F32)


def tables(modes, nphi, mode_dev):
    mode = np.arange(modes).reshape(-1, 1, mode_dev)
    k = np.arange(nphi).reshape(-1, 1, 1, 1)
    angle = 2.0 * np.pi * ((mode[None] * k) % nphi) / nphi
    fwd = np.concatenate([np.cos(angle), -np.sin(angle)], 2).reshape(nphi, 2 * modes)
    return fwd.astype(BF), (fwd.T / nphi).astype(BF)


def lane_group(shape):
    return lax.broadcasted_iota(jnp.int32, shape, len(shape) - 1) // 32


def pick(group, parts):
    out = parts[0]
    for g, part in enumerate(parts[1:], 1):
        out = jnp.where(group == g, part, out)
    return out


def shift(x, groups):
    return x if groups % 4 == 0 else pltpu.roll(x, 32 * (groups % 4), 1)


def pack(rows, out_ref):
    group = lane_group((8, 128))
    for v in range(4):
        tiles = {cp: r[:, 128 * v : 128 * v + 128] for cp, r in rows.items()}
        for q in range(4):
            halves = [
                pick(group, [shift(tiles[c % 3, p], c - q) for c in range(4)]) for p in range(2)
            ]
            out_ref[4 * v + q] = jnp.concatenate(halves, 0).astype(BF)


def unpack(tile, slots):
    group = lane_group((16, 128))
    cols = []
    for v in range(slots // 4):
        tiles = [tile(4 * v + q).astype(F32) for q in range(4)]
        cols.append(
            jnp.concatenate(
                [pick(group, [shift(tiles[q], q - c) for q in range(4)]) for c in range(3)], 0
            ).astype(BF)
        )
    return jnp.concatenate(cols, 1)


def wall_onehot(wall_ref):
    twice = jnp.concatenate([wall_ref[...], wall_ref[...]], 1)
    nodes = lax.broadcasted_iota(jnp.int32, (512, 128), 0)
    return (nodes == twice).astype(F32).astype(BF)


def trace_rows(rows, onehot):
    both = nn(rows, onehot)
    return jnp.where(low_lanes((8, 128)), both[:8], both[8:]).astype(BF)


def low_lanes(shape):
    return lax.broadcasted_iota(jnp.int32, shape, len(shape) - 1) < 64


def two_by_two(conn_ref):
    return jnp.concatenate([conn_ref[pl.ds(0, 8, 2), :], conn_ref[pl.ds(1, 8, 2), :]], 1)


def open_kernel(mode_ref, field, wall, conn, vel, fwd, inv, pack_ref, out_ref, mark_ref, va_ref, vb_ref, fwd_ref, inv_ref):
    onehot = wall_onehot(wall())
    conn = conn()[...]
    field_ref = field()
    pack({(c, p): field_ref[3 * p + c] for c in range(3) for p in range(2)}, pack_ref)
    tr = trace_rows(jnp.concatenate([field_ref[2], field_ref[5]], 0).astype(BF), onehot)
    for j in range(out_ref.shape[0]):
        out_ref[j] = tr
    part = jnp.zeros((16, 64), jnp.int32) + mode_ref[0] % 4
    code = jnp.where(part < 2, conn // 32, conn % 32).astype(F32)
    code = jnp.concatenate([code, code], 1)
    even = (jnp.zeros((16, 128), jnp.int32) + mode_ref[0] % 2) == 0
    code = jnp.where(even, pltpu.roll(code, 32, 1), code)
    mark_ref[...] = jnp.where(lane_group((16, 128)) == 3, code, 0.0)
    vel_ref = vel()
    vel = [vel_ref[c].astype(F32) for c in range(3)]
    zero = jnp.zeros_like(vel[0])
    va_ref[...] = jnp.concatenate([vel[0], vel[1], vel[2], zero], 0).T.astype(BF)
    vb_ref[...] = jnp.concatenate([vel[1], vel[2], vel[0], zero], 0).T.astype(BF)
    fwd_ref[...] = fwd()[...]
    inv_ref[...] = inv()[...]


def element_blocks(ref, sign):
    row = lax.broadcasted_iota(jnp.int32, (256, 64), 0)
    col = lax.broadcasted_iota(jnp.int32, (256, 64), 1)
    spread = (row % 64 == col).astype(F32).astype(BF)
    near = lax.broadcasted_iota(jnp.int32, (256, 256), 0) // 64
    same = near == lax.broadcasted_iota(jnp.int32, (256, 256), 1) // 64
    once = nt(spread, ref[...].astype(BF)).astype(BF)
    return jnp.where(same, sign * nt(once, spread), 0.0).astype(BF)


def operators(conn, first, width, stiff_ref, curl_ref, tall_ref, work_ref):
    across = conn.T
    nodes = lax.broadcasted_iota(jnp.int32, (768, 128), 0).astype(F32)
    lanes = lax.broadcasted_iota(jnp.int32, (128, width), 1).astype(F32) + first
    mats = [element_blocks(stiff_ref, -1.0), element_blocks(curl_ref, 1.0)]
    for t in range(8):
        tall_ref[:, 128 * t : 128 * t + 128] = (nodes == conn[t : t + 1]).astype(F32).astype(BF)
    for u in range(4):
        picks = [
            (lanes == across[:, t : t + 1]).astype(F32).astype(BF) for t in (2 * u, 2 * u + 1)
        ]
        picks = jnp.concatenate(picks, 0)
        for k, mat in enumerate(mats):
            work_ref[k, 256 * u : 256 * u + 256] = nn(mat, picks).astype(BF)
    return nn(tall_ref[...], work_ref[0]), nn(tall_ref[...], work_ref[1])


def own_kernel(stiff, curl, conn, emf_ref, near_out, near_ref, tall_ref, work_ref, sem):
    conn = two_by_two(conn()).astype(F32)
    s, c = operators(conn, 0.0, 512, stiff(), curl(), tall_ref, work_ref)
    near_ref[:768] = c.astype(BF)
    near_ref[768:] = s.astype(BF)
    copy = pltpu.make_async_copy(near_ref, near_out, sem)
    copy.start()
    copy.wait()


def induce_kernel(moved_ref, mark_ref, va_ref, vb_ref, fwd_ref, inv_ref, out_ref):
    moved = moved_ref[...]
    rows = moved.reshape(256, 128)
    turned = pltpu.roll(rows.astype(F32), 96, 1).astype(BF)
    here = nn(fwd_ref[...], rows)
    after = nn(fwd_ref[...], turned)
    cross = va_ref[...].astype(F32) * after - vb_ref[...].astype(F32) * here
    back = nn(inv_ref[...], cross.astype(BF))
    out_ref[:, :16] = (back.reshape(16, 16, 128) + mark_ref[...][None]).astype(BF)
    out_ref[:, 16:] = moved


ORDER = [3 * p + c for c in range(3) for p in range(2)]


def rows_of(field):
    field_ref = field() if callable(field) else field
    return jnp.concatenate([field_ref[s] for s in ORDER], 0)


def side(mer_ref, a_ref, b_ref, odd_takes, part):
    rows = slice(16 * part, 16 * part + 16)
    odd = (jnp.zeros((16, 128), jnp.int32) + mer_ref[0] % 2) == 1
    first, second = (a_ref, b_ref) if odd_takes == 0 else (b_ref, a_ref)
    return lambda s: jnp.where(odd, first[s, rows], second[s, rows])


def operator_rows(mer_ref, now, emf_ref, pa_ref, pb_ref, near, far):
    own = unpack(lambda s: emf_ref[s, :16], 16)
    e_next, f_next = [unpack(side(mer_ref, pa_ref, pb_ref, 1, part), 8) for part in range(2)]
    e_prev, f_prev = [unpack(side(mer_ref, pa_ref, pb_ref, 0, part), 16) for part in range(2)]
    field = rows_of(now).astype(BF)
    total = nn(jnp.concatenate([own, e_next, field, f_next], 1), near()[...])
    low = nn(jnp.concatenate([e_prev, own[:, :256], f_prev, field[:, :256]], 1), far()[...])
    return jnp.concatenate([total[:, :256] + low, total[:, 256:]], 1)


def first_operator_kernel(mer_ref, now, emf_ref, pa_ref, pb_ref, near, stiff, curl, *refs):
    out_ref, far_out, far_ref, tall_ref, work_ref, conn_ref, sem = refs
    tile = side(mer_ref, pa_ref, pb_ref, 0, 0)
    code = [pltpu.roll(tile(s).astype(F32), 32 + 32 * (s % 2), 1) for s in range(4)]
    first = lane_group((16, 128)) == 0
    conn_ref[...] = 32.0 * jnp.where(first, code[0], code[1]) + jnp.where(first, code[2], code[3])
    conn = [conn_ref[pl.ds(k, 8, 2), :] for k in range(2)]
    conn = jnp.where(low_lanes((8, 128)), conn[0], pltpu.roll(conn[1], 64, 1))
    s, c = operators(conn, 512.0, 256, stiff(), curl(), tall_ref, work_ref)
    there = jnp.where(mer_ref[0] > 0, 1.0, 0.0)
    far_ref[:768] = (c * there).astype(BF)
    far_ref[768:] = (s * there).astype(BF)
    copy = pltpu.make_async_copy(far_ref, far_out, sem)
    copy.start()
    out_ref[...] = operator_rows(mer_ref, now, emf_ref, pa_ref, pb_ref, near, lambda: far_ref)
    copy.wait()


def operator_kernel(mer_ref, now, emf_ref, pa_ref, pb_ref, near, far, out_ref):
    out_ref[...] = operator_rows(mer_ref, now, emf_ref, pa_ref, pb_ref, near, far)


def finish(mode_ref, now, total_ref, whole_ref, wall, mass, dtn):
    onehot = wall_onehot(wall())
    field = rows_of(now)
    number = lax.broadcasted_iota(jnp.int32, (48, 512), 0) % 8 + 8 * mode_ref[0]
    coef = (number.astype(F32) / 128.0) ** 2
    low = low_lanes((8, 128))
    parts = [], []
    for a in range(whole_ref.shape[0] // 2):
        x, y = whole_ref[2 * a].astype(F32), whole_ref[2 * a + 1].astype(F32)
        parts[0].append(jnp.where(low, x, pltpu.roll(y, 64, 1)))
        parts[1].append(jnp.where(low, pltpu.roll(x, 64, 1), y))
    whole = jnp.concatenate([jnp.concatenate(p, 1) for p in parts], 0).astype(BF)
    weight = 1.0 / mass()[...]
    every = [nt(whole, dtn(k)[2 * k : 2 * k + 2].reshape(128, 2048)) for k in range(4)]
    every = jnp.concatenate(every, 1)
    mine = lax.broadcasted_iota(jnp.int32, (16, 512), 0) % 8
    every = jnp.where(mine == lax.broadcasted_iota(jnp.int32, (16, 512), 1) // 64, every, 0.0)
    flux = every[:, :128] + every[:, 128:256] + every[:, 256:384] + every[:, 384:]
    flux = jnp.where(low_lanes((16, 128)), flux + pltpu.roll(flux, 64, 1), 0.0)
    upper = flux.astype(BF)
    added = nt(upper, onehot) + nt((flux - upper.astype(F32)).astype(BF), onehot)
    total = total_ref[...]
    total = jnp.concatenate([total[:32], total[32:] - 0.5 * added], 0)
    rate = total * weight - 4.0 * coef * field
    return rate, field, flux, onehot


def first_kernel(*refs):
    sect_ref, pack_ref, trace_ref, flux_ref = refs[7:]
    rate, field, flux, onehot = finish(*refs[:7])
    sect = field + 0.2 * rate
    flux_ref[...] = flux
    rows = {(c, p): sect[16 * c + 8 * p : 16 * c + 8 * p + 8] for c in range(3) for p in range(2)}
    for (c, p), r in rows.items():
        sect_ref[3 * p + c] = r
    pack(rows, pack_ref)
    tr = trace_rows(sect[32:].astype(BF), onehot)
    for j in range(trace_ref.shape[0]):
        trace_ref[j] = tr


def second_kernel(*refs):
    start, first_flux_ref, out_ref, flux_ref = refs[7:]
    rate, sect, flux, onehot = finish(*refs[:7])
    start_ref = start()
    for c in range(3):
        for p in range(2):
            at = slice(16 * c + 8 * p, 16 * c + 8 * p + 8)
            out_ref[3 * p + c] = 0.5 * (start_ref[3 * p + c] + sect[at] + 0.2 * rate[at])
    for p in range(2):
        flux_ref[0, :, p, :] = first_flux_ref[8 * p : 8 * p + 8, :64]
        flux_ref[1, :, p, :] = flux[8 * p : 8 * p + 8, :64]


def call(kernel, out, where, args, scratch=(), limit=16):
    count = len(where)
    brought = [(a, k) for a, k in zip(args, where, strict=True) if k in "cd"]

    def run(*refs):
        inner, sems, bufs = refs, None, []
        if brought:
            inner, sems = refs[: -len(brought) - 1], refs[-len(brought) - 1]
            bufs = list(refs[-len(brought) :])
        near, used = [], 0
        for ref, k in zip(inner[:count], where, strict=True):
            if k not in "cd":
                near.append(ref)
                continue
            buf, copies = bufs.pop(0), []
            for part in range(4 if k == "d" else 1):
                piece = pl.ds(2 * part, 2) if k == "d" else Ellipsis
                src, dst = (ref.at[piece], buf.at[piece]) if k == "d" else (ref, buf)
                copies.append(pltpu.make_async_copy(src, dst, sems.at[used]))
                copies[-1].start()
                used += 1
            near.append(later(copies, buf))
        kernel(*near, *inner[count:])

    spaces = {"s": pltpu.SMEM, "v": pltpu.VMEM, "c": pltpu.HBM, "d": pltpu.HBM}
    waits = sum(4 if k == "d" else 1 for _, k in brought)
    extra = [pltpu.SemaphoreType.DMA((waits,))] if brought else []
    extra += [pltpu.VMEM(a.shape, a.dtype) for a, _ in brought]
    return pl.pallas_call(
        run,
        out_shape=[space(s, d) if space else jax.ShapeDtypeStruct(s, d) for s, d, space in out],
        in_specs=[pl.BlockSpec(memory_space=spaces[k]) for k in where],
        out_specs=[pl.BlockSpec(memory_space=space or pltpu.VMEM) for _, _, space in out],
        scratch_shapes=[*scratch, *extra],
        compiler_params=pltpu.CompilerParams(vmem_limit_bytes=limit * 2**20),
    )(
        *[
            a if k == "s" else pltpu.with_memory_space_constraint(a, spaces[k])
            for k, a in zip(where, args, strict=True)
        ]
    )


def later(copies, buf):
    arrived = set()

    def get(part=0):
        if part not in arrived:
            copies[part].wait()
            arrived.add(part)
        return buf

    return get


def body(field, velocity, stiffness, curl_matrix, mass, connect, wall_index, dtn):
    fwd, inv = tables(128, 256, 8)
    near_space, far_space = pltpu.VMEM, pltpu.HBM
    spots = lax.axis_size("mer")
    mer = lax.axis_index("mer").astype(jnp.int32).reshape(1)
    mode = lax.axis_index("mode").astype(jnp.int32).reshape(1)
    start = jnp.transpose(field, (1, 0, 2))
    wall = wall_index.reshape(1, 64)
    row = mass.reshape(1, 512)
    chunk = ((16, 16, 128), BF, near_space)

    def works(rows, width):
        return [
            pltpu.VMEM((rows, width), BF),
            pltpu.VMEM((768, 1024), BF),
            pltpu.VMEM((2, 1024, width), BF),
            pltpu.SemaphoreType.DMA,
        ]

    table = [((256, 128), BF, near_space)] * 2 + [((256, 256), BF, near_space)] * 2
    packed, trace, *table = call(
        open_kernel,
        [chunk, ((spots, 8, 128), BF, near_space), ((16, 128), F32, near_space), *table],
        "scccccc",
        (mode, start, wall, connect, jnp.transpose(velocity, (0, 2, 1)), fwd, inv),
    )
    twins = [(i, i ^ 1) for i in range(spots)]
    others = [(i, ((i + 1) ^ 1) - 1) for i in range(1, spots - 1)]

    def exchange(packed, trace):
        moved = lax.all_to_all(packed, "mode", 0, 0, tiled=True)
        (back,) = call(
            induce_kernel, [((16, 32, 128), BF, near_space)], "vvvvvv", (moved, *table)
        )
        emf = lax.all_to_all(back, "mode", 0, 0, tiled=True)
        e_twin = lax.ppermute(emf, "mer", twins)
        e_other = lax.ppermute(emf, "mer", others)
        return emf, e_twin, e_other, lax.all_to_all(trace, "mer", 0, 0, tiled=True)

    rows = ((48, 512), F32, near_space)
    emf, e_twin, e_other, whole = exchange(packed, trace)
    (near,) = call(
        own_kernel,
        [((1536, 512), BF, far_space)],
        "cccv",
        (stiffness, curl_matrix, connect, emf),
        works(1536, 512),
        32,
    )
    total, far = call(
        first_operator_kernel,
        [rows, ((1536, 256), BF, far_space)],
        "scvvvccc",
        (mer, start, emf, e_twin, e_other, near, stiffness, curl_matrix),
        [*works(1536, 256)[:3], pltpu.VMEM((16, 128), F32), pltpu.SemaphoreType.DMA],
        32,
    )
    out = [((6, 8, 512), F32, near_space), chunk]
    out += [((spots, 8, 128), BF, near_space), ((16, 128), F32, near_space)]
    sect, packed, trace, flux = call(
        first_kernel, out, "scvvccd", (mode, start, total, whole, wall, row, dtn)
    )
    emf, e_twin, e_other, whole = exchange(packed, trace)
    (total,) = call(
        operator_kernel, [rows], "svvvvcc", (mer, sect, emf, e_twin, e_other, near, far)
    )
    out = [((6, 8, 512), F32, None), ((2, 8, 2, 64), F32, None)]
    done, fluxes = call(
        second_kernel, out, "svvvccdcv", (mode, sect, total, whole, wall, row, dtn, start, flux)
    )
    return (jnp.transpose(done, (1, 0, 2)), fluxes)


def solution(mesh):
    placed = (
        P("mode", None, "mer"),
        P(None, None, ("mer", "mode")),
        P(),
        P(),
        P("mer"),
        P("mer", None),
        P("mer"),
        P("mode", "mer", None),
    )
    return jax.shard_map(
        body,
        mesh=mesh,
        in_specs=placed,
        out_specs=(P("mode", None, "mer"), P(None, "mode", None, "mer")),
        check_vma=False,
    )
```

```python
import numpy as np
import jax
import jax.numpy as jnp
from jax import lax
from jax.experimental import pallas as pl
from jax.experimental.pallas import tpu as pltpu
from jax.sharding import PartitionSpec as P


BF = jnp.bfloat16
F32 = jnp.float32


def nt(a, b):
    return lax.dot_general(a, b, (((1,), (1,)), ((), ())), preferred_element_type=F32)


def nn(a, b):
    return jnp.dot(a, b, preferred_element_type=F32)


def tables(modes, nphi, mode_dev):
    mode = np.arange(modes).reshape(-1, 1, mode_dev)
    k = np.arange(nphi).reshape(-1, 1, 1, 1)
    angle = 2.0 * np.pi * ((mode[None] * k) % nphi) / nphi
    fwd = np.concatenate([np.cos(angle), -np.sin(angle)], 2).reshape(nphi, 2 * modes)
    return fwd.astype(BF), (fwd.T / nphi).astype(BF)


def lane_group(shape):
    return lax.broadcasted_iota(jnp.int32, shape, len(shape) - 1) // 32


def pick(group, parts):
    out = parts[0]
    for g, part in enumerate(parts[1:], 1):
        out = jnp.where(group == g, part, out)
    return out


def shift(x, groups):
    return x if groups % 4 == 0 else pltpu.roll(x, 32 * (groups % 4), 1)


def pack(rows, out_ref):
    group = lane_group((8, 128))
    for v in range(4):
        tiles = {cp: r[:, 128 * v : 128 * v + 128] for cp, r in rows.items()}
        for q in range(4):
            halves = [
                pick(group, [shift(tiles[c % 3, p], c - q) for c in range(4)]) for p in range(2)
            ]
            out_ref[4 * v + q] = jnp.concatenate(halves, 0).astype(BF)


def unpack(tile, slots):
    group = lane_group((16, 128))
    cols = []
    for v in range(slots // 4):
        tiles = [tile(4 * v + q).astype(F32) for q in range(4)]
        cols.append(
            jnp.concatenate(
                [pick(group, [shift(tiles[q], q - c) for q in range(4)]) for c in range(3)], 0
            ).astype(BF)
        )
    return jnp.concatenate(cols, 1)


def wall_onehot(wall_ref):
    twice = jnp.concatenate([wall_ref[...], wall_ref[...]], 1)
    nodes = lax.broadcasted_iota(jnp.int32, (512, 128), 0)
    return (nodes == twice).astype(F32).astype(BF)


def trace_rows(rows, onehot):
    both = nn(rows, onehot)
    return jnp.where(low_lanes((8, 128)), both[:8], both[8:])


def low_lanes(shape):
    return lax.broadcasted_iota(jnp.int32, shape, len(shape) - 1) < 64


def two_by_two(conn_ref):
    return jnp.concatenate([conn_ref[pl.ds(0, 8, 2), :], conn_ref[pl.ds(1, 8, 2), :]], 1)


def open_kernel(mode_ref, field, wall, conn, vel, fwd, inv, pack_ref, out_ref, mark_ref, va_ref, vb_ref, fwd_ref, inv_ref):
    onehot = wall_onehot(wall())
    conn = conn()[...]
    field_ref = field()
    pack({(c, p): field_ref[3 * p + c] for c in range(3) for p in range(2)}, pack_ref)
    tr = trace_rows(jnp.concatenate([field_ref[2], field_ref[5]], 0).astype(BF), onehot)
    for j in range(out_ref.shape[0]):
        out_ref[j] = tr
    part = jnp.zeros((16, 64), jnp.int32) + mode_ref[0] % 4
    code = jnp.where(part < 2, conn // 32, conn % 32).astype(F32)
    code = jnp.concatenate([code, code], 1)
    even = (jnp.zeros((16, 128), jnp.int32) + mode_ref[0] % 2) == 0
    code = jnp.where(even, pltpu.roll(code, 32, 1), code)
    mark_ref[...] = jnp.where(lane_group((16, 128)) == 3, code, 0.0)
    vel_ref = vel()
    vel = [vel_ref[c].astype(F32) for c in range(3)]
    zero = jnp.zeros_like(vel[0])
    va_ref[...] = jnp.concatenate([vel[0], vel[1], vel[2], zero], 0).T.astype(BF)
    vb_ref[...] = jnp.concatenate([vel[1], vel[2], vel[0], zero], 0).T.astype(BF)
    fwd_ref[...] = fwd()[...]
    inv_ref[...] = inv()[...]


def element_blocks(ref, sign):
    row = lax.broadcasted_iota(jnp.int32, (256, 64), 0)
    col = lax.broadcasted_iota(jnp.int32, (256, 64), 1)
    spread = (row % 64 == col).astype(F32).astype(BF)
    near = lax.broadcasted_iota(jnp.int32, (256, 256), 0) // 64
    same = near == lax.broadcasted_iota(jnp.int32, (256, 256), 1) // 64
    once = nt(spread, ref[...].astype(BF)).astype(BF)
    return jnp.where(same, sign * nt(once, spread), 0.0).astype(BF)


def operators(conn, first, width, stiff_ref, curl_ref, tall_ref, work_ref):
    across = conn.T
    nodes = lax.broadcasted_iota(jnp.int32, (768, 128), 0).astype(F32)
    lanes = lax.broadcasted_iota(jnp.int32, (128, width), 1).astype(F32) + first
    mats = [element_blocks(stiff_ref, -1.0), element_blocks(curl_ref, 1.0)]
    for t in range(8):
        tall_ref[:, 128 * t : 128 * t + 128] = (nodes == conn[t : t + 1]).astype(F32).astype(BF)
    for u in range(4):
        picks = [
            (lanes == across[:, t : t + 1]).astype(F32).astype(BF) for t in (2 * u, 2 * u + 1)
        ]
        picks = jnp.concatenate(picks, 0)
        for k, mat in enumerate(mats):
            work_ref[k, 256 * u : 256 * u + 256, :width] = nn(mat, picks).astype(BF)
    return [nn(tall_ref[...], work_ref[k, :, :width]) for k in range(2)]


def induce_kernel(moved_ref, mark_ref, va_ref, vb_ref, fwd_ref, inv_ref, out_ref):
    moved = moved_ref[...]
    rows = moved.reshape(256, 128)
    turned = pltpu.roll(rows.astype(F32), 96, 1).astype(BF)
    here = nn(fwd_ref[...], rows)
    after = nn(fwd_ref[...], turned)
    cross = va_ref[...].astype(F32) * after - vb_ref[...].astype(F32) * here
    back = nn(inv_ref[...], cross.astype(BF))
    out_ref[:, :16] = (back.reshape(16, 16, 128) + mark_ref[...][None]).astype(BF)
    out_ref[:, 16:] = moved


ORDER = [3 * p + c for c in range(3) for p in range(2)]


def rows_of(field):
    field_ref = field() if callable(field) else field
    return jnp.concatenate([field_ref[s] for s in ORDER], 0)


def side(mer_ref, a_ref, b_ref, odd_takes, part):
    rows = slice(16 * part, 16 * part + 16)
    odd = (jnp.zeros((16, 128), jnp.int32) + mer_ref[0] % 2) == 1
    first, second = (a_ref, b_ref) if odd_takes == 0 else (b_ref, a_ref)
    return lambda s: jnp.where(odd, first[s, rows], second[s, rows])


def operator_rows(mer_ref, now, emf_ref, pa_ref, pb_ref, near, far):
    own = unpack(lambda s: emf_ref[s, :16], 16)
    e_next, f_next = [unpack(side(mer_ref, pa_ref, pb_ref, 1, part), 8) for part in range(2)]
    e_prev, f_prev = [unpack(side(mer_ref, pa_ref, pb_ref, 0, part), 16) for part in range(2)]
    field = rows_of(now).astype(BF)
    total = nn(jnp.concatenate([own, e_next, field, f_next], 1), near()[...])
    low = nn(jnp.concatenate([e_prev, own[:, :256], f_prev, field[:, :256]], 1), far()[...])
    return jnp.concatenate([total[:, :256] + low, total[:, 256:]], 1)


def first_operator_kernel(mer_ref, now, emf_ref, pa_ref, pb_ref, conn, stiff, curl, *refs):
    out_ref, near_out, far_out, near_ref, far_ref, tall_ref, work_ref, conn_ref, sems = refs
    tile = side(mer_ref, pa_ref, pb_ref, 0, 0)
    code = [pltpu.roll(tile(s).astype(F32), 32 + 32 * (s % 2), 1) for s in range(4)]
    first = lane_group((16, 128)) == 0
    conn_ref[...] = 32.0 * jnp.where(first, code[0], code[1]) + jnp.where(first, code[2], code[3])
    there = [conn_ref[pl.ds(k, 8, 2), :] for k in range(2)]
    there = jnp.where(low_lanes((8, 128)), there[0], pltpu.roll(there[1], 64, 1))
    here = two_by_two(conn()).astype(F32)
    has = jnp.where(mer_ref[0] > 0, 1.0, 0.0)
    jobs = ((here, 0.0, 512, near_ref, near_out, 1.0), (there, 512.0, 256, far_ref, far_out, has))
    copies = []
    for conn, start, width, ref, out, gain in jobs:
        s, c = operators(conn, start, width, stiff(), curl(), tall_ref, work_ref)
        ref[:768] = (c * gain).astype(BF)
        ref[768:] = (s * gain).astype(BF)
        copies.append(pltpu.make_async_copy(ref, out, sems.at[len(copies)]))
        copies[-1].start()
    out_ref[...] = operator_rows(mer_ref, now, emf_ref, pa_ref, pb_ref, lambda: near_ref, lambda: far_ref)
    for copy in copies:
        copy.wait()


def operator_kernel(mer_ref, now, emf_ref, pa_ref, pb_ref, near, far, out_ref):
    out_ref[...] = operator_rows(mer_ref, now, emf_ref, pa_ref, pb_ref, near, far)


def finish(mode_ref, now, total_ref, whole_ref, wall, mass, dtn):
    onehot = wall_onehot(wall())
    field = rows_of(now)
    number = lax.broadcasted_iota(jnp.int32, (48, 512), 0) % 8 + 8 * mode_ref[0]
    coef = (number.astype(F32) / 128.0) ** 2
    low = low_lanes((8, 128))
    parts = [], []
    for a in range(whole_ref.shape[0] // 2):
        x, y = whole_ref[2 * a], whole_ref[2 * a + 1]
        parts[0].append(jnp.where(low, x, pltpu.roll(y, 64, 1)))
        parts[1].append(jnp.where(low, pltpu.roll(x, 64, 1), y))
    whole = jnp.concatenate([jnp.concatenate(p, 1) for p in parts], 0).astype(BF)
    weight = 1.0 / mass()[...]
    every = [nt(whole, dtn(k)[2 * k : 2 * k + 2].reshape(128, 2048)) for k in range(4)]
    every = jnp.concatenate(every, 1)
    mine = lax.broadcasted_iota(jnp.int32, (16, 512), 0) % 8
    every = jnp.where(mine == lax.broadcasted_iota(jnp.int32, (16, 512), 1) // 64, every, 0.0)
    flux = every[:, :128] + every[:, 128:256] + every[:, 256:384] + every[:, 384:]
    flux = jnp.where(low_lanes((16, 128)), flux + pltpu.roll(flux, 64, 1), 0.0)
    upper = flux.astype(BF)
    added = nt(upper, onehot) + nt((flux - upper.astype(F32)).astype(BF), onehot)
    total = total_ref[...]
    total = jnp.concatenate([total[:32], total[32:] - 0.5 * added], 0)
    rate = total * weight - 4.0 * coef * field
    return rate, field, flux, onehot


def first_kernel(*refs):
    sect_ref, pack_ref, trace_ref, flux_ref = refs[7:]
    rate, field, flux, onehot = finish(*refs[:7])
    sect = field + 0.2 * rate
    flux_ref[...] = flux
    rows = {(c, p): sect[16 * c + 8 * p : 16 * c + 8 * p + 8] for c in range(3) for p in range(2)}
    for (c, p), r in rows.items():
        sect_ref[3 * p + c] = r
    pack(rows, pack_ref)
    tr = trace_rows(sect[32:].astype(BF), onehot)
    for j in range(trace_ref.shape[0]):
        trace_ref[j] = tr


def second_kernel(*refs):
    start, first_flux_ref, out_ref, flux_ref = refs[7:]
    rate, sect, flux, onehot = finish(*refs[:7])
    start_ref = start()
    for c in range(3):
        for p in range(2):
            at = slice(16 * c + 8 * p, 16 * c + 8 * p + 8)
            out_ref[3 * p + c] = 0.5 * (start_ref[3 * p + c] + sect[at] + 0.2 * rate[at])
    for p in range(2):
        flux_ref[0, :, p, :] = first_flux_ref[8 * p : 8 * p + 8, :64]
        flux_ref[1, :, p, :] = flux[8 * p : 8 * p + 8, :64]


def call(kernel, out, where, args, scratch=(), limit=16):
    count = len(where)
    brought = [(a, k) for a, k in zip(args, where, strict=True) if k in "cd"]

    def run(*refs):
        inner, sems, bufs = refs, None, []
        if brought:
            inner, sems = refs[: -len(brought) - 1], refs[-len(brought) - 1]
            bufs = list(refs[-len(brought) :])
        near, used = [], 0
        for ref, k in zip(inner[:count], where, strict=True):
            if k not in "cd":
                near.append(ref)
                continue
            buf, copies = bufs.pop(0), []
            for part in range(4 if k == "d" else 1):
                piece = pl.ds(2 * part, 2) if k == "d" else Ellipsis
                src, dst = (ref.at[piece], buf.at[piece]) if k == "d" else (ref, buf)
                copies.append(pltpu.make_async_copy(src, dst, sems.at[used]))
                copies[-1].start()
                used += 1
            near.append(later(copies, buf))
        kernel(*near, *inner[count:])

    spaces = {"s": pltpu.SMEM, "v": pltpu.VMEM, "c": pltpu.HBM, "d": pltpu.HBM}
    waits = sum(4 if k == "d" else 1 for _, k in brought)
    extra = [pltpu.SemaphoreType.DMA((waits,))] if brought else []
    extra += [pltpu.VMEM(a.shape, a.dtype) for a, _ in brought]
    return pl.pallas_call(
        run,
        out_shape=[space(s, d) if space else jax.ShapeDtypeStruct(s, d) for s, d, space in out],
        in_specs=[pl.BlockSpec(memory_space=spaces[k]) for k in where],
        out_specs=[pl.BlockSpec(memory_space=space or pltpu.VMEM) for _, _, space in out],
        scratch_shapes=[*scratch, *extra],
        compiler_params=pltpu.CompilerParams(vmem_limit_bytes=limit * 2**20),
    )(
        *[
            a if k == "s" else pltpu.with_memory_space_constraint(a, spaces[k])
            for k, a in zip(where, args, strict=True)
        ]
    )


def later(copies, buf):
    arrived = set()

    def get(part=0):
        if part not in arrived:
            copies[part].wait()
            arrived.add(part)
        return buf

    return get


def body(field, velocity, stiffness, curl_matrix, mass, connect, wall_index, dtn):
    fwd, inv = tables(128, 256, 8)
    near_space, far_space = pltpu.VMEM, pltpu.HBM
    spots = lax.axis_size("mer")
    mer = lax.axis_index("mer").astype(jnp.int32).reshape(1)
    mode = lax.axis_index("mode").astype(jnp.int32).reshape(1)
    start = jnp.transpose(field, (1, 0, 2))
    wall = wall_index.reshape(1, 64)
    row = mass.reshape(1, 512)
    chunk = ((16, 16, 128), BF, near_space)

    table = [((256, 128), BF, near_space)] * 2 + [((256, 256), BF, near_space)] * 2
    packed, trace, *table = call(
        open_kernel,
        [chunk, ((spots, 8, 128), F32, near_space), ((16, 128), F32, near_space), *table],
        "scccccc",
        (mode, start, wall, connect, jnp.transpose(velocity, (0, 2, 1)), fwd, inv),
    )
    twins = [(i, i ^ 1) for i in range(spots)]
    others = [(i, ((i + 1) ^ 1) - 1) for i in range(1, spots - 1)]

    def exchange(packed, trace):
        moved = lax.all_to_all(packed, "mode", 0, 0, tiled=True)
        (back,) = call(
            induce_kernel, [((16, 32, 128), BF, near_space)], "vvvvvv", (moved, *table)
        )
        emf = lax.all_to_all(back, "mode", 0, 0, tiled=True)
        e_twin = lax.ppermute(emf, "mer", twins)
        e_other = lax.ppermute(emf, "mer", others)
        return emf, e_twin, e_other, lax.all_to_all(trace, "mer", 0, 0, tiled=True)

    rows = ((48, 512), F32, near_space)
    emf, e_twin, e_other, whole = exchange(packed, trace)
    works = [
        pltpu.VMEM((1536, 512), BF),
        pltpu.VMEM((1536, 256), BF),
        pltpu.VMEM((768, 1024), BF),
        pltpu.VMEM((2, 1024, 512), BF),
        pltpu.VMEM((16, 128), F32),
        pltpu.SemaphoreType.DMA((2,)),
    ]
    total, near, far = call(
        first_operator_kernel,
        [rows, ((1536, 512), BF, far_space), ((1536, 256), BF, far_space)],
        "scvvvccc",
        (mer, start, emf, e_twin, e_other, connect, stiffness, curl_matrix),
        works,
        32,
    )
    out = [((6, 8, 512), F32, near_space), chunk]
    out += [((spots, 8, 128), F32, near_space), ((16, 128), F32, near_space)]
    sect, packed, trace, flux = call(
        first_kernel, out, "scvvccd", (mode, start, total, whole, wall, row, dtn)
    )
    emf, e_twin, e_other, whole = exchange(packed, trace)
    (total,) = call(
        operator_kernel, [rows], "svvvvcc", (mer, sect, emf, e_twin, e_other, near, far)
    )
    out = [((6, 8, 512), F32, None), ((2, 8, 2, 64), F32, None)]
    done, fluxes = call(
        second_kernel, out, "svvvccdcv", (mode, sect, total, whole, wall, row, dtn, start, flux)
    )
    return (jnp.transpose(done, (1, 0, 2)), fluxes)


def solution(mesh):
    placed = (
        P("mode", None, "mer"),
        P(None, None, ("mer", "mode")),
        P(),
        P(),
        P("mer"),
        P("mer", None),
        P("mer"),
        P("mode", "mer", None),
    )
    return jax.shard_map(
        body,
        mesh=mesh,
        in_specs=placed,
        out_specs=(P("mode", None, "mer"), P(None, "mode", None, "mer")),
        check_vma=False,
    )
```

```python
import numpy as np
import jax
import jax.numpy as jnp
from jax import lax
from jax.experimental import pallas as pl
from jax.experimental.pallas import tpu as pltpu
from jax.sharding import PartitionSpec as P


BF = jnp.bfloat16
F32 = jnp.float32


def nt(a, b):
    return lax.dot_general(a, b, (((1,), (1,)), ((), ())), preferred_element_type=F32)


def nn(a, b):
    return jnp.dot(a, b, preferred_element_type=F32)


def tables(modes, nphi, mode_dev):
    mode = np.arange(modes).reshape(-1, 1, mode_dev)
    k = np.arange(nphi).reshape(-1, 1, 1, 1)
    angle = 2.0 * np.pi * ((mode[None] * k) % nphi) / nphi
    fwd = np.concatenate([np.cos(angle), -np.sin(angle)], 2).reshape(nphi, 2 * modes)
    return fwd.astype(BF), (fwd.T / nphi).astype(BF)


def lane_group(shape):
    return lax.broadcasted_iota(jnp.int32, shape, len(shape) - 1) // 32


def pick(group, parts):
    out = parts[0]
    for g, part in enumerate(parts[1:], 1):
        out = jnp.where(group == g, part, out)
    return out


def shift(x, groups):
    return x if groups % 4 == 0 else pltpu.roll(x, 32 * (groups % 4), 1)


def pack(rows, out_ref):
    group = lane_group((8, 128))
    for v in range(4):
        tiles = {cp: r[:, 128 * v : 128 * v + 128] for cp, r in rows.items()}
        for q in range(4):
            halves = [
                pick(group, [shift(tiles[c % 3, p], c - q) for c in range(4)]) for p in range(2)
            ]
            out_ref[4 * v + q] = jnp.concatenate(halves, 0).astype(BF)


def unpack(tile, slots):
    group = lane_group((16, 128))
    cols = []
    for v in range(slots // 4):
        tiles = [tile(4 * v + q).astype(F32) for q in range(4)]
        cols.append(
            jnp.concatenate(
                [pick(group, [shift(tiles[q], q - c) for q in range(4)]) for c in range(3)], 0
            ).astype(BF)
        )
    return jnp.concatenate(cols, 1)


def wall_onehot(wall_ref, mer):
    twice = jnp.concatenate([wall_ref[...], wall_ref[...]], 1)
    nodes = lax.broadcasted_iota(jnp.int32, (512, 128), 0)
    half = lax.broadcasted_iota(jnp.int32, (512, 128), 1) // 64
    return jnp.where(half == mer % 2, (nodes == twice).astype(F32), 0.0).astype(BF)


def low_lanes(shape):
    return lax.broadcasted_iota(jnp.int32, shape, len(shape) - 1) < 64


def two_by_two(conn_ref):
    return jnp.concatenate([conn_ref[pl.ds(0, 8, 2), :], conn_ref[pl.ds(1, 8, 2), :]], 1)


def open_kernel(mode_ref, mer_ref, field, wall, conn, vel, fwd, inv, pack_ref, out_ref, mark_ref, va_ref, vb_ref, fwd_ref, inv_ref):
    onehot = wall_onehot(wall(), mer_ref[0])
    conn = conn()[...]
    field_ref = field()
    pack({(c, p): field_ref[3 * p + c] for c in range(3) for p in range(2)}, pack_ref)
    tr = nn(jnp.concatenate([field_ref[2], field_ref[5]], 0).astype(BF), onehot).astype(BF)
    for j in range(out_ref.shape[0]):
        out_ref[j] = tr
    part = jnp.zeros((16, 64), jnp.int32) + mode_ref[0] % 4
    code = jnp.where(part < 2, conn // 32, conn % 32).astype(F32)
    code = jnp.concatenate([code, code], 1)
    even = (jnp.zeros((16, 128), jnp.int32) + mode_ref[0] % 2) == 0
    code = jnp.where(even, pltpu.roll(code, 32, 1), code)
    mark_ref[...] = jnp.where(lane_group((16, 128)) == 3, code, 0.0)
    vel_ref = vel()
    vel = [vel_ref[c].astype(F32) for c in range(3)]
    zero = jnp.zeros_like(vel[0])
    va_ref[...] = jnp.concatenate([vel[0], vel[1], vel[2], zero], 0).T.astype(BF)
    vb_ref[...] = jnp.concatenate([vel[1], vel[2], vel[0], zero], 0).T.astype(BF)
    fwd_ref[...] = fwd()[...]
    inv_ref[...] = inv()[...]


def element_blocks(ref, sign):
    row = lax.broadcasted_iota(jnp.int32, (256, 64), 0)
    col = lax.broadcasted_iota(jnp.int32, (256, 64), 1)
    spread = (row % 64 == col).astype(F32).astype(BF)
    near = lax.broadcasted_iota(jnp.int32, (256, 256), 0) // 64
    same = near == lax.broadcasted_iota(jnp.int32, (256, 256), 1) // 64
    once = nt(spread, ref[...].astype(BF)).astype(BF)
    return jnp.where(same, sign * nt(once, spread), 0.0).astype(BF)


def operators(conn, first, width, stiff_ref, curl_ref, tall_ref, work_ref):
    across = conn.T
    nodes = lax.broadcasted_iota(jnp.int32, (768, 128), 0).astype(F32)
    lanes = lax.broadcasted_iota(jnp.int32, (128, width), 1).astype(F32) + first
    mats = [element_blocks(stiff_ref, -1.0), element_blocks(curl_ref, 1.0)]
    for t in range(8):
        tall_ref[:, 128 * t : 128 * t + 128] = (nodes == conn[t : t + 1]).astype(F32).astype(BF)
    for u in range(4):
        picks = [
            (lanes == across[:, t : t + 1]).astype(F32).astype(BF) for t in (2 * u, 2 * u + 1)
        ]
        picks = jnp.concatenate(picks, 0)
        for k, mat in enumerate(mats):
            work_ref[k, 256 * u : 256 * u + 256, :width] = nn(mat, picks).astype(BF)
    return [nn(tall_ref[...], work_ref[k, :, :width]) for k in range(2)]


def induce_kernel(moved_ref, mark_ref, va_ref, vb_ref, fwd_ref, inv_ref, out_ref):
    moved = moved_ref[...]
    rows = moved.reshape(256, 128)
    turned = pltpu.roll(rows.astype(F32), 96, 1).astype(BF)
    here = nn(fwd_ref[...], rows)
    after = nn(fwd_ref[...], turned)
    cross = va_ref[...].astype(F32) * after - vb_ref[...].astype(F32) * here
    back = nn(inv_ref[...], cross.astype(BF))
    out_ref[:, :16] = (back.reshape(16, 16, 128) + mark_ref[...][None]).astype(BF)
    out_ref[:, 16:] = moved


ORDER = [3 * p + c for c in range(3) for p in range(2)]


def rows_of(field):
    field_ref = field() if callable(field) else field
    return jnp.concatenate([field_ref[s] for s in ORDER], 0)


def side(mer_ref, a_ref, b_ref, odd_takes, part):
    rows = slice(16 * part, 16 * part + 16)
    odd = (jnp.zeros((16, 128), jnp.int32) + mer_ref[0] % 2) == 1
    first, second = (a_ref, b_ref) if odd_takes == 0 else (b_ref, a_ref)
    return lambda s: jnp.where(odd, first[s, rows], second[s, rows])


def operator_rows(mer_ref, now, emf_ref, pa_ref, pb_ref, near, far):
    own = unpack(lambda s: emf_ref[s, :16], 16)
    e_next, f_next = [unpack(side(mer_ref, pa_ref, pb_ref, 1, part), 8) for part in range(2)]
    e_prev, f_prev = [unpack(side(mer_ref, pa_ref, pb_ref, 0, part), 16) for part in range(2)]
    field = rows_of(now).astype(BF)
    total = nn(jnp.concatenate([own, e_next, field, f_next], 1), near()[...])
    low = nn(jnp.concatenate([e_prev, own[:, :256], f_prev, field[:, :256]], 1), far()[...])
    return jnp.concatenate([total[:, :256] + low, total[:, 256:]], 1)


def first_operator_kernel(mer_ref, now, emf_ref, pa_ref, pb_ref, conn, stiff, curl, dtn_ref, *refs):
    out_ref, half_ref, near_out, far_out, near_ref, far_ref, tall_ref, work_ref, conn_ref, sems = refs
    bring = pltpu.make_async_copy(dtn_ref.at[pl.ds(0, 4)], half_ref, sems.at[2])
    bring.start()
    tile = side(mer_ref, pa_ref, pb_ref, 0, 0)
    code = [pltpu.roll(tile(s).astype(F32), 32 + 32 * (s % 2), 1) for s in range(4)]
    first = lane_group((16, 128)) == 0
    conn_ref[...] = 32.0 * jnp.where(first, code[0], code[1]) + jnp.where(first, code[2], code[3])
    there = [conn_ref[pl.ds(k, 8, 2), :] for k in range(2)]
    there = jnp.where(low_lanes((8, 128)), there[0], pltpu.roll(there[1], 64, 1))
    here = two_by_two(conn()).astype(F32)
    has = jnp.where(mer_ref[0] > 0, 1.0, 0.0)
    jobs = ((here, 0.0, 512, near_ref, near_out, 1.0), (there, 512.0, 256, far_ref, far_out, has))
    copies = []
    for conn, start, width, ref, out, gain in jobs:
        s, c = operators(conn, start, width, stiff(), curl(), tall_ref, work_ref)
        ref[:768] = (c * gain).astype(BF)
        ref[768:] = (s * gain).astype(BF)
        copies.append(pltpu.make_async_copy(ref, out, sems.at[len(copies)]))
        copies[-1].start()
    out_ref[...] = operator_rows(mer_ref, now, emf_ref, pa_ref, pb_ref, lambda: near_ref, lambda: far_ref)
    for copy in [*copies, bring]:
        copy.wait()


def operator_kernel(mer_ref, now, emf_ref, pa_ref, pb_ref, near, far, dtn_ref, out_ref, half_ref, sem):
    bring = pltpu.make_async_copy(dtn_ref.at[pl.ds(0, 4)], half_ref, sem)
    bring.start()
    out_ref[...] = operator_rows(mer_ref, now, emf_ref, pa_ref, pb_ref, near, far)
    bring.wait()


def finish(mode_ref, mer_ref, now, total_ref, whole_ref, wall, mass, half_ref, dtn):
    whole = jnp.concatenate([whole_ref[2 * a] + whole_ref[2 * a + 1] for a in range(16)], 1)
    every = [nt(whole, half_ref[2 * k : 2 * k + 2].reshape(128, 2048)) for k in range(2)]
    onehot = wall_onehot(wall(), mer_ref[0])
    field = rows_of(now)
    number = lax.broadcasted_iota(jnp.int32, (48, 512), 0) % 8 + 8 * mode_ref[0]
    coef = (number.astype(F32) / 128.0) ** 2
    weight = 1.0 / mass()[...]
    every += [nt(whole, dtn(k)[2 * k : 2 * k + 2].reshape(128, 2048)) for k in range(2)]
    every = jnp.concatenate(every, 1)
    mine = lax.broadcasted_iota(jnp.int32, (16, 512), 0) % 8
    every = jnp.where(mine == lax.broadcasted_iota(jnp.int32, (16, 512), 1) // 64, every, 0.0)
    flux = every[:, :128] + every[:, 128:256] + every[:, 256:384] + every[:, 384:]
    flux = flux + pltpu.roll(flux, 64, 1)
    upper = flux.astype(BF)
    added = nt(upper, onehot) + nt((flux - upper.astype(F32)).astype(BF), onehot)
    total = total_ref[...]
    total = jnp.concatenate([total[:32], total[32:] - 0.5 * added], 0)
    rate = total * weight - 4.0 * coef * field
    return rate, field, flux, onehot


def first_kernel(*refs):
    sect_ref, pack_ref, trace_ref, flux_ref = refs[9:]
    rate, field, flux, onehot = finish(*refs[:9])
    sect = field + 0.2 * rate
    flux_ref[...] = flux
    rows = {(c, p): sect[16 * c + 8 * p : 16 * c + 8 * p + 8] for c in range(3) for p in range(2)}
    for (c, p), r in rows.items():
        sect_ref[3 * p + c] = r
    pack(rows, pack_ref)
    tr = nn(sect[32:].astype(BF), onehot).astype(BF)
    for j in range(trace_ref.shape[0]):
        trace_ref[j] = tr


def second_kernel(*refs):
    start, first_flux_ref, out_ref, flux_ref = refs[9:]
    rate, sect, flux, onehot = finish(*refs[:9])
    start_ref = start()
    for c in range(3):
        for p in range(2):
            at = slice(16 * c + 8 * p, 16 * c + 8 * p + 8)
            out_ref[3 * p + c] = 0.5 * (start_ref[3 * p + c] + sect[at] + 0.2 * rate[at])
    for p in range(2):
        flux_ref[0, :, p, :] = first_flux_ref[8 * p : 8 * p + 8, :64]
        flux_ref[1, :, p, :] = flux[8 * p : 8 * p + 8, :64]


def call(kernel, out, where, args, scratch=(), limit=16):
    count = len(where)
    brought = [(a, k) for a, k in zip(args, where, strict=True) if k in "cd"]

    def run(*refs):
        inner, sems, bufs = refs, None, []
        if brought:
            inner, sems = refs[: -len(brought) - 1], refs[-len(brought) - 1]
            bufs = list(refs[-len(brought) :])
        near, used = [], 0
        for ref, k in zip(inner[:count], where, strict=True):
            if k not in "cd":
                near.append(ref)
                continue
            buf, copies = bufs.pop(0), []
            for part in range(2 if k == "d" else 1):
                src, dst = ref, buf
                if k == "d":
                    src, dst = ref.at[pl.ds(4 + 2 * part, 2)], buf.at[pl.ds(2 * part, 2)]
                copies.append(pltpu.make_async_copy(src, dst, sems.at[used]))
                copies[-1].start()
                used += 1
            near.append(later(copies, buf))
        kernel(*near, *inner[count:])

    spaces = {"s": pltpu.SMEM, "v": pltpu.VMEM, "c": pltpu.HBM, "d": pltpu.HBM, "h": pltpu.HBM}
    waits = sum(2 if k == "d" else 1 for _, k in brought)
    extra = [pltpu.SemaphoreType.DMA((waits,))] if brought else []
    extra += [pltpu.VMEM((4,) + a.shape[1:] if k == "d" else a.shape, a.dtype) for a, k in brought]
    return pl.pallas_call(
        run,
        out_shape=[space(s, d) if space else jax.ShapeDtypeStruct(s, d) for s, d, space in out],
        in_specs=[pl.BlockSpec(memory_space=spaces[k]) for k in where],
        out_specs=[pl.BlockSpec(memory_space=space or pltpu.VMEM) for _, _, space in out],
        scratch_shapes=[*scratch, *extra],
        compiler_params=pltpu.CompilerParams(vmem_limit_bytes=limit * 2**20),
    )(
        *[
            a if k == "s" else pltpu.with_memory_space_constraint(a, spaces[k])
            for k, a in zip(where, args, strict=True)
        ]
    )


def later(copies, buf):
    arrived = set()

    def get(part=0):
        if part not in arrived:
            copies[part].wait()
            arrived.add(part)
        return buf

    return get


def body(field, velocity, stiffness, curl_matrix, mass, connect, wall_index, dtn):
    fwd, inv = tables(128, 256, 8)
    near_space, far_space = pltpu.VMEM, pltpu.HBM
    spots = lax.axis_size("mer")
    mer = lax.axis_index("mer").astype(jnp.int32).reshape(1)
    mode = lax.axis_index("mode").astype(jnp.int32).reshape(1)
    start = jnp.transpose(field, (1, 0, 2))
    wall = wall_index.reshape(1, 64)
    row = mass.reshape(1, 512)
    chunk = ((16, 16, 128), BF, near_space)

    table = [((256, 128), BF, near_space)] * 2 + [((256, 256), BF, near_space)] * 2
    packed, trace, *table = call(
        open_kernel,
        [chunk, ((spots, 16, 128), BF, near_space), ((16, 128), F32, near_space), *table],
        "sscccccc",
        (mode, mer, start, wall, connect, jnp.transpose(velocity, (0, 2, 1)), fwd, inv),
    )
    twins = [(i, i ^ 1) for i in range(spots)]
    others = [(i, ((i + 1) ^ 1) - 1) for i in range(1, spots - 1)]

    def exchange(packed, trace):
        moved = lax.all_to_all(packed, "mode", 0, 0, tiled=True)
        (back,) = call(
            induce_kernel, [((16, 32, 128), BF, near_space)], "vvvvvv", (moved, *table)
        )
        emf = lax.all_to_all(back, "mode", 0, 0, tiled=True)
        e_twin = lax.ppermute(emf, "mer", twins)
        e_other = lax.ppermute(emf, "mer", others)
        return emf, e_twin, e_other, lax.all_to_all(trace, "mer", 0, 0, tiled=True)

    rows = ((48, 512), F32, near_space)
    emf, e_twin, e_other, whole = exchange(packed, trace)
    works = [
        pltpu.VMEM((1536, 512), BF),
        pltpu.VMEM((1536, 256), BF),
        pltpu.VMEM((768, 1024), BF),
        pltpu.VMEM((2, 1024, 512), BF),
        pltpu.VMEM((16, 128), F32),
        pltpu.SemaphoreType.DMA((3,)),
    ]
    some = ((4, 64, 2048), BF, near_space)
    total, half, near, far = call(
        first_operator_kernel,
        [rows, some, ((1536, 512), BF, far_space), ((1536, 256), BF, far_space)],
        "scvvvccch",
        (mer, start, emf, e_twin, e_other, connect, stiffness, curl_matrix, dtn),
        works,
        32,
    )
    out = [((6, 8, 512), F32, near_space), chunk]
    out += [((spots, 16, 128), BF, near_space), ((16, 128), F32, near_space)]
    sect, packed, trace, flux = call(
        first_kernel, out, "sscvvccvd", (mode, mer, start, total, whole, wall, row, half, dtn)
    )
    emf, e_twin, e_other, whole = exchange(packed, trace)
    total, half = call(
        operator_kernel,
        [rows, some],
        "svvvvcch",
        (mer, sect, emf, e_twin, e_other, near, far, dtn),
        [pltpu.SemaphoreType.DMA],
    )
    out = [((6, 8, 512), F32, None), ((2, 8, 2, 64), F32, None)]
    done, fluxes = call(
        second_kernel,
        out,
        "ssvvvccvdcv",
        (mode, mer, sect, total, whole, wall, row, half, dtn, start, flux),
    )
    return (jnp.transpose(done, (1, 0, 2)), fluxes)


def solution(mesh):
    placed = (
        P("mode", None, "mer"),
        P(None, None, ("mer", "mode")),
        P(),
        P(),
        P("mer"),
        P("mer", None),
        P("mer"),
        P("mode", "mer", None),
    )
    return jax.shard_map(
        body,
        mesh=mesh,
        in_specs=placed,
        out_specs=(P("mode", None, "mer"), P(None, "mode", None, "mer")),
        check_vma=False,
    )
```

```python
import numpy as np
import jax
import jax.numpy as jnp
from jax import lax
from jax.experimental import pallas as pl
from jax.experimental.pallas import tpu as pltpu
from jax.sharding import PartitionSpec as P


BF = jnp.bfloat16
F32 = jnp.float32


def nt(a, b):
    return lax.dot_general(a, b, (((1,), (1,)), ((), ())), preferred_element_type=F32)


def nn(a, b):
    return jnp.dot(a, b, preferred_element_type=F32)


def tables(modes, nphi, mode_dev):
    mode = np.arange(modes).reshape(-1, 1, mode_dev)
    k = np.arange(nphi).reshape(-1, 1, 1, 1)
    angle = 2.0 * np.pi * ((mode[None] * k) % nphi) / nphi
    fwd = np.concatenate([np.cos(angle), -np.sin(angle)], 2).reshape(nphi, 2 * modes)
    return fwd.astype(BF), (fwd.T / nphi).astype(BF)


def lane_group(shape):
    return lax.broadcasted_iota(jnp.int32, shape, len(shape) - 1) // 32


def pick(group, parts):
    out = parts[0]
    for g, part in enumerate(parts[1:], 1):
        out = jnp.where(group == g, part, out)
    return out


def shift(x, groups):
    return x if groups % 4 == 0 else pltpu.roll(x, 32 * (groups % 4), 1)


def pack(rows, out_ref):
    group = lane_group((8, 128))
    for v in range(4):
        tiles = {cp: r[:, 128 * v : 128 * v + 128] for cp, r in rows.items()}
        for q in range(4):
            halves = [
                pick(group, [shift(tiles[c % 3, p], c - q) for c in range(4)]) for p in range(2)
            ]
            out_ref[4 * v + q] = jnp.concatenate(halves, 0).astype(BF)


def unpack(tile, slots):
    group = lane_group((16, 128))
    cols = []
    for v in range(slots // 4):
        tiles = [tile(4 * v + q).astype(F32) for q in range(4)]
        cols.append(
            jnp.concatenate(
                [pick(group, [shift(tiles[q], q - c) for q in range(4)]) for c in range(3)], 0
            ).astype(BF)
        )
    return jnp.concatenate(cols, 1)


def wall_onehot(wall_ref, mer):
    twice = jnp.concatenate([wall_ref[...], wall_ref[...]], 1)
    nodes = lax.broadcasted_iota(jnp.int32, (512, 128), 0)
    half = lax.broadcasted_iota(jnp.int32, (512, 128), 1) // 64
    return jnp.where(half == mer % 2, (nodes == twice).astype(F32), 0.0).astype(BF)


def low_lanes(shape):
    return lax.broadcasted_iota(jnp.int32, shape, len(shape) - 1) < 64


def two_by_two(conn_ref):
    return jnp.concatenate([conn_ref[pl.ds(0, 8, 2), :], conn_ref[pl.ds(1, 8, 2), :]], 1)


def open_kernel(mode_ref, mer_ref, field, wall, conn, vel, fwd, inv, pack_ref, out_ref, mark_ref, va_ref, vb_ref, fwd_ref, inv_ref):
    onehot = wall_onehot(wall(), mer_ref[0])
    conn = conn()[...]
    field_ref = field()
    pack({(c, p): field_ref[3 * p + c] for c in range(3) for p in range(2)}, pack_ref)
    tr = nn(jnp.concatenate([field_ref[2], field_ref[5]], 0).astype(BF), onehot).astype(BF)
    for j in range(out_ref.shape[0]):
        out_ref[j] = tr
    part = jnp.zeros((16, 64), jnp.int32) + mode_ref[0] % 4
    code = jnp.where(part < 2, conn // 32, conn % 32).astype(F32)
    code = jnp.concatenate([code, code], 1)
    even = (jnp.zeros((16, 128), jnp.int32) + mode_ref[0] % 2) == 0
    code = jnp.where(even, pltpu.roll(code, 32, 1), code)
    mark_ref[...] = jnp.where(lane_group((16, 128)) == 3, code, 0.0)
    vel_ref = vel()
    vel = [vel_ref[c].astype(F32) for c in range(3)]
    zero = jnp.zeros_like(vel[0])
    va_ref[...] = jnp.concatenate([vel[0], vel[1], vel[2], zero], 0).T.astype(BF)
    vb_ref[...] = jnp.concatenate([vel[1], vel[2], vel[0], zero], 0).T.astype(BF)
    fwd_ref[...] = fwd()[...]
    inv_ref[...] = inv()[...]


def element_blocks(ref, sign):
    row = lax.broadcasted_iota(jnp.int32, (256, 64), 0)
    col = lax.broadcasted_iota(jnp.int32, (256, 64), 1)
    spread = (row % 64 == col).astype(F32).astype(BF)
    near = lax.broadcasted_iota(jnp.int32, (256, 256), 0) // 64
    same = near == lax.broadcasted_iota(jnp.int32, (256, 256), 1) // 64
    once = nt(spread, ref[...].astype(BF)).astype(BF)
    return jnp.where(same, sign * nt(once, spread), 0.0).astype(BF)


def operators(conn, first, width, stiff_ref, curl_ref, tall_ref, work_ref):
    across = conn.T
    nodes = lax.broadcasted_iota(jnp.int32, (768, 128), 0).astype(F32)
    lanes = lax.broadcasted_iota(jnp.int32, (128, width), 1).astype(F32) + first
    mats = [element_blocks(stiff_ref, -1.0), element_blocks(curl_ref, 1.0)]
    for t in range(8):
        tall_ref[:, 128 * t : 128 * t + 128] = (nodes == conn[t : t + 1]).astype(F32).astype(BF)
    for u in range(4):
        picks = [
            (lanes == across[:, t : t + 1]).astype(F32).astype(BF) for t in (2 * u, 2 * u + 1)
        ]
        picks = jnp.concatenate(picks, 0)
        for k, mat in enumerate(mats):
            work_ref[k, 256 * u : 256 * u + 256, :width] = nn(mat, picks).astype(BF)
    return [nn(tall_ref[...], work_ref[k, :, :width]) for k in range(2)]


def induce_kernel(moved_ref, mark_ref, va_ref, vb_ref, fwd_ref, inv_ref, out_ref):
    moved = moved_ref[...]
    rows = moved.reshape(256, 128)
    turned = pltpu.roll(rows.astype(F32), 96, 1).astype(BF)
    here = nn(fwd_ref[...], rows)
    after = nn(fwd_ref[...], turned)
    cross = va_ref[...].astype(F32) * after - vb_ref[...].astype(F32) * here
    back = nn(inv_ref[...], cross.astype(BF))
    out_ref[:, :16] = (back.reshape(16, 16, 128) + mark_ref[...][None]).astype(BF)
    out_ref[:, 16:] = moved


ORDER = [3 * p + c for c in range(3) for p in range(2)]


def rows_of(field):
    field_ref = field() if callable(field) else field
    return jnp.concatenate([field_ref[s] for s in ORDER], 0)


def side(mer_ref, a_ref, b_ref, odd_takes, part):
    rows = slice(16 * part, 16 * part + 16)
    odd = (jnp.zeros((16, 128), jnp.int32) + mer_ref[0] % 2) == 1
    first, second = (a_ref, b_ref) if odd_takes == 0 else (b_ref, a_ref)
    return lambda s: jnp.where(odd, first[s, rows], second[s, rows])


def operands(mer_ref, now, emf_ref, pa_ref, pb_ref):
    own = unpack(lambda s: emf_ref[s, :16], 16)
    e_next, f_next = [unpack(side(mer_ref, pa_ref, pb_ref, 1, part), 8) for part in range(2)]
    e_prev, f_prev = [unpack(side(mer_ref, pa_ref, pb_ref, 0, part), 16) for part in range(2)]
    field = rows_of(now).astype(BF)
    near = jnp.concatenate([own, e_next, field, f_next], 1)
    return near, jnp.concatenate([e_prev, own[:, :256], f_prev, field[:, :256]], 1)


def operator_rows(rows, near, far):
    total = sum(nn(rows[0][:, 512 * k : 512 * k + 512], near(k)) for k in range(3))
    low = nn(rows[1], far())
    return jnp.concatenate([total[:, :256] + low, total[:, 256:]], 1)


def first_operator_kernel(mer_ref, now, emf_ref, pa_ref, pb_ref, conn, stiff, curl, dtn_ref, *refs):
    out_ref, half_ref, near_out, far_out, near_ref, far_ref, tall_ref, work_ref, conn_ref, sems = refs
    bring = pltpu.make_async_copy(dtn_ref.at[pl.ds(0, 4)], half_ref, sems.at[2])
    bring.start()
    tile = side(mer_ref, pa_ref, pb_ref, 0, 0)
    code = [pltpu.roll(tile(s).astype(F32), 32 + 32 * (s % 2), 1) for s in range(4)]
    first = lane_group((16, 128)) == 0
    conn_ref[...] = 32.0 * jnp.where(first, code[0], code[1]) + jnp.where(first, code[2], code[3])
    there = [conn_ref[pl.ds(k, 8, 2), :] for k in range(2)]
    there = jnp.where(low_lanes((8, 128)), there[0], pltpu.roll(there[1], 64, 1))
    here = two_by_two(conn()).astype(F32)
    has = jnp.where(mer_ref[0] > 0, 1.0, 0.0)
    jobs = ((here, 0.0, 512, near_ref, near_out, 1.0), (there, 512.0, 256, far_ref, far_out, has))
    copies = []
    for conn, start, width, ref, out, gain in jobs:
        s, c = operators(conn, start, width, stiff(), curl(), tall_ref, work_ref)
        ref[:768] = (c * gain).astype(BF)
        ref[768:] = (s * gain).astype(BF)
        copies.append(pltpu.make_async_copy(ref, out, sems.at[len(copies)]))
        copies[-1].start()
    rows = operands(mer_ref, now, emf_ref, pa_ref, pb_ref)
    out_ref[...] = operator_rows(
        rows, lambda k: near_ref[512 * k : 512 * k + 512], lambda: far_ref[...]
    )
    for copy in [*copies, bring]:
        copy.wait()


def operator_kernel(mer_ref, now, emf_ref, pa_ref, pb_ref, near_ref, far_ref, dtn_ref, *refs):
    out_ref, half_ref, near_buf, far_buf, sems = refs
    pairs = [(near_ref.at[pl.ds(512 * k, 512)], near_buf.at[pl.ds(512 * k, 512)]) for k in range(3)]
    pairs += [(far_ref, far_buf), (dtn_ref.at[pl.ds(0, 4)], half_ref)]
    copies = [pltpu.make_async_copy(a, b, sems.at[k]) for k, (a, b) in enumerate(pairs)]
    for copy in copies:
        copy.start()
    rows = operands(mer_ref, now, emf_ref, pa_ref, pb_ref)

    def near(k):
        copies[k].wait()
        return near_buf[512 * k : 512 * k + 512]

    def far():
        copies[3].wait()
        return far_buf[...]

    out_ref[...] = operator_rows(rows, near, far)
    copies[4].wait()


def finish(mode_ref, mer_ref, now, total_ref, whole_ref, wall, mass, half_ref, dtn):
    whole = jnp.concatenate([whole_ref[2 * a] + whole_ref[2 * a + 1] for a in range(16)], 1)
    every = [nt(whole, half_ref[2 * k : 2 * k + 2].reshape(128, 2048)) for k in range(2)]
    onehot = wall_onehot(wall(), mer_ref[0])
    field = rows_of(now)
    number = lax.broadcasted_iota(jnp.int32, (48, 512), 0) % 8 + 8 * mode_ref[0]
    coef = (number.astype(F32) / 128.0) ** 2
    weight = 1.0 / mass()[...]
    every += [nt(whole, dtn(k)[2 * k : 2 * k + 2].reshape(128, 2048)) for k in range(2)]
    every = jnp.concatenate(every, 1)
    mine = lax.broadcasted_iota(jnp.int32, (16, 512), 0) % 8
    every = jnp.where(mine == lax.broadcasted_iota(jnp.int32, (16, 512), 1) // 64, every, 0.0)
    flux = every[:, :128] + every[:, 128:256] + every[:, 256:384] + every[:, 384:]
    flux = flux + pltpu.roll(flux, 64, 1)
    upper = flux.astype(BF)
    added = nt(upper, onehot) + nt((flux - upper.astype(F32)).astype(BF), onehot)
    total = total_ref[...]
    total = jnp.concatenate([total[:32], total[32:] - 0.5 * added], 0)
    rate = total * weight - 4.0 * coef * field
    return rate, field, flux, onehot


def first_kernel(*refs):
    sect_ref, pack_ref, trace_ref, flux_ref = refs[9:]
    rate, field, flux, onehot = finish(*refs[:9])
    sect = field + 0.2 * rate
    flux_ref[...] = flux
    rows = {(c, p): sect[16 * c + 8 * p : 16 * c + 8 * p + 8] for c in range(3) for p in range(2)}
    for (c, p), r in rows.items():
        sect_ref[3 * p + c] = r
    pack(rows, pack_ref)
    tr = nn(sect[32:].astype(BF), onehot).astype(BF)
    for j in range(trace_ref.shape[0]):
        trace_ref[j] = tr


def second_kernel(*refs):
    start, first_flux_ref, out_ref, flux_ref = refs[9:]
    rate, sect, flux, onehot = finish(*refs[:9])
    start_ref = start()
    for c in range(3):
        for p in range(2):
            at = slice(16 * c + 8 * p, 16 * c + 8 * p + 8)
            out_ref[3 * p + c] = 0.5 * (start_ref[3 * p + c] + sect[at] + 0.2 * rate[at])
    for p in range(2):
        flux_ref[0, :, p, :] = first_flux_ref[8 * p : 8 * p + 8, :64]
        flux_ref[1, :, p, :] = flux[8 * p : 8 * p + 8, :64]


def call(kernel, out, where, args, scratch=(), limit=16):
    count = len(where)
    brought = [(a, k) for a, k in zip(args, where, strict=True) if k in "cd"]

    def run(*refs):
        inner, sems, bufs = refs, None, []
        if brought:
            inner, sems = refs[: -len(brought) - 1], refs[-len(brought) - 1]
            bufs = list(refs[-len(brought) :])
        near, used = [], 0
        for ref, k in zip(inner[:count], where, strict=True):
            if k not in "cd":
                near.append(ref)
                continue
            buf, copies = bufs.pop(0), []
            for part in range(2 if k == "d" else 1):
                src, dst = ref, buf
                if k == "d":
                    src, dst = ref.at[pl.ds(4 + 2 * part, 2)], buf.at[pl.ds(2 * part, 2)]
                copies.append(pltpu.make_async_copy(src, dst, sems.at[used]))
                copies[-1].start()
                used += 1
            near.append(later(copies, buf))
        kernel(*near, *inner[count:])

    spaces = {"s": pltpu.SMEM, "v": pltpu.VMEM, "c": pltpu.HBM, "d": pltpu.HBM, "h": pltpu.HBM}
    waits = sum(2 if k == "d" else 1 for _, k in brought)
    extra = [pltpu.SemaphoreType.DMA((waits,))] if brought else []
    extra += [pltpu.VMEM((4,) + a.shape[1:] if k == "d" else a.shape, a.dtype) for a, k in brought]
    return pl.pallas_call(
        run,
        out_shape=[space(s, d) if space else jax.ShapeDtypeStruct(s, d) for s, d, space in out],
        in_specs=[pl.BlockSpec(memory_space=spaces[k]) for k in where],
        out_specs=[pl.BlockSpec(memory_space=space or pltpu.VMEM) for _, _, space in out],
        scratch_shapes=[*scratch, *extra],
        compiler_params=pltpu.CompilerParams(vmem_limit_bytes=limit * 2**20),
    )(
        *[
            a if k == "s" else pltpu.with_memory_space_constraint(a, spaces[k])
            for k, a in zip(where, args, strict=True)
        ]
    )


def later(copies, buf):
    arrived = set()

    def get(part=0):
        if part not in arrived:
            copies[part].wait()
            arrived.add(part)
        return buf

    return get


def body(field, velocity, stiffness, curl_matrix, mass, connect, wall_index, dtn):
    fwd, inv = tables(128, 256, 8)
    near_space, far_space = pltpu.VMEM, pltpu.HBM
    spots = lax.axis_size("mer")
    mer = lax.axis_index("mer").astype(jnp.int32).reshape(1)
    mode = lax.axis_index("mode").astype(jnp.int32).reshape(1)
    start = jnp.transpose(field, (1, 0, 2))
    wall = wall_index.reshape(1, 64)
    row = mass.reshape(1, 512)
    chunk = ((16, 16, 128), BF, near_space)

    table = [((256, 128), BF, near_space)] * 2 + [((256, 256), BF, near_space)] * 2
    packed, trace, *table = call(
        open_kernel,
        [chunk, ((spots, 16, 128), BF, near_space), ((16, 128), F32, near_space), *table],
        "sscccccc",
        (mode, mer, start, wall, connect, jnp.transpose(velocity, (0, 2, 1)), fwd, inv),
    )
    twins = [(i, i ^ 1) for i in range(spots)]
    others = [(i, ((i + 1) ^ 1) - 1) for i in range(1, spots - 1)]

    def exchange(packed, trace):
        moved = lax.all_to_all(packed, "mode", 0, 0, tiled=True)
        (back,) = call(
            induce_kernel, [((16, 32, 128), BF, near_space)], "vvvvvv", (moved, *table)
        )
        emf = lax.all_to_all(back, "mode", 0, 0, tiled=True)
        e_twin = lax.ppermute(emf, "mer", twins)
        e_other = lax.ppermute(emf, "mer", others)
        return emf, e_twin, e_other, lax.all_to_all(trace, "mer", 0, 0, tiled=True)

    rows = ((48, 512), F32, near_space)
    emf, e_twin, e_other, whole = exchange(packed, trace)
    works = [
        pltpu.VMEM((1536, 512), BF),
        pltpu.VMEM((1536, 256), BF),
        pltpu.VMEM((768, 1024), BF),
        pltpu.VMEM((2, 1024, 512), BF),
        pltpu.VMEM((16, 128), F32),
        pltpu.SemaphoreType.DMA((3,)),
    ]
    some = ((4, 64, 2048), BF, near_space)
    total, half, near, far = call(
        first_operator_kernel,
        [rows, some, ((1536, 512), BF, far_space), ((1536, 256), BF, far_space)],
        "scvvvccch",
        (mer, start, emf, e_twin, e_other, connect, stiffness, curl_matrix, dtn),
        works,
        32,
    )
    out = [((6, 8, 512), F32, near_space), chunk]
    out += [((spots, 16, 128), BF, near_space), ((16, 128), F32, near_space)]
    sect, packed, trace, flux = call(
        first_kernel, out, "sscvvccvd", (mode, mer, start, total, whole, wall, row, half, dtn)
    )
    emf, e_twin, e_other, whole = exchange(packed, trace)
    total, half = call(
        operator_kernel,
        [rows, some],
        "svvvvhhh",
        (mer, sect, emf, e_twin, e_other, near, far, dtn),
        [*works[:2], pltpu.SemaphoreType.DMA((5,))],
    )
    out = [((6, 8, 512), F32, None), ((2, 8, 2, 64), F32, None)]
    done, fluxes = call(
        second_kernel,
        out,
        "ssvvvccvdcv",
        (mode, mer, sect, total, whole, wall, row, half, dtn, start, flux),
    )
    return (jnp.transpose(done, (1, 0, 2)), fluxes)


def solution(mesh):
    placed = (
        P("mode", None, "mer"),
        P(None, None, ("mer", "mode")),
        P(),
        P(),
        P("mer"),
        P("mer", None),
        P("mer"),
        P("mode", "mer", None),
    )
    return jax.shard_map(
        body,
        mesh=mesh,
        in_specs=placed,
        out_specs=(P("mode", None, "mer"), P(None, "mode", None, "mer")),
        check_vma=False,
    )
```

```python
import numpy as np
import jax
import jax.numpy as jnp
from jax import lax
from jax.experimental import pallas as pl
from jax.experimental.pallas import tpu as pltpu
from jax.sharding import PartitionSpec as P


BF = jnp.bfloat16
F32 = jnp.float32


def nt(a, b):
    return lax.dot_general(a, b, (((1,), (1,)), ((), ())), preferred_element_type=F32)


def nn(a, b):
    return jnp.dot(a, b, preferred_element_type=F32)


def tables(modes, nphi, mode_dev):
    mode = np.arange(modes).reshape(-1, 1, mode_dev)
    k = np.arange(nphi).reshape(-1, 1, 1, 1)
    angle = 2.0 * np.pi * ((mode[None] * k) % nphi) / nphi
    fwd = np.concatenate([np.cos(angle), -np.sin(angle)], 2).reshape(nphi, 2 * modes)
    return fwd.astype(BF), (fwd.T / nphi).astype(BF)


def lane_group(shape):
    return lax.broadcasted_iota(jnp.int32, shape, len(shape) - 1) // 32


def pick(group, parts):
    out = parts[0]
    for g, part in enumerate(parts[1:], 1):
        out = jnp.where(group == g, part, out)
    return out


def shift(x, groups):
    return x if groups % 4 == 0 else pltpu.roll(x, 32 * (groups % 4), 1)


def pack(rows, out_ref):
    group = lane_group((8, 128))
    for v in range(4):
        tiles = {cp: r[:, 128 * v : 128 * v + 128] for cp, r in rows.items()}
        for q in range(4):
            halves = [
                pick(group, [shift(tiles[c % 3, p], c - q) for c in range(4)]) for p in range(2)
            ]
            out_ref[4 * v + q] = jnp.concatenate(halves, 0).astype(BF)


def unpack(tile, slots):
    group = lane_group((16, 128))
    cols = []
    for v in range(slots // 4):
        tiles = [tile(4 * v + q).astype(F32) for q in range(4)]
        cols.append(
            jnp.concatenate(
                [pick(group, [shift(tiles[q], q - c) for q in range(4)]) for c in range(3)], 0
            ).astype(BF)
        )
    return jnp.concatenate(cols, 1)


def wall_onehot(wall_ref, mer=None):
    twice = jnp.concatenate([wall_ref[...], wall_ref[...]], 1)
    nodes = lax.broadcasted_iota(jnp.int32, (512, 128), 0)
    hit = (nodes == twice).astype(F32)
    if mer is not None:
        half = lax.broadcasted_iota(jnp.int32, (512, 128), 1) // 64
        hit = jnp.where(half == mer % 2, hit, 0.0)
    return hit.astype(BF)


def all_traces(whole_ref):
    pairs = [(whole_ref[2 * a], whole_ref[2 * a + 1]) for a in range(16)]
    if whole_ref.shape[1] == 16:
        return jnp.concatenate([x + y for x, y in pairs], 1)
    low = low_lanes((8, 128))
    parts = [], []
    for x, y in pairs:
        x, y = x.astype(F32), y.astype(F32)
        parts[0].append(jnp.where(low, x, pltpu.roll(y, 64, 1)))
        parts[1].append(jnp.where(low, pltpu.roll(x, 64, 1), y))
    return jnp.concatenate([jnp.concatenate(p, 1) for p in parts], 0).astype(BF)


def low_lanes(shape):
    return lax.broadcasted_iota(jnp.int32, shape, len(shape) - 1) < 64


def two_by_two(conn_ref):
    return jnp.concatenate([conn_ref[pl.ds(0, 8, 2), :], conn_ref[pl.ds(1, 8, 2), :]], 1)


def open_kernel(mode_ref, field, wall, conn, vel, fwd, inv, pack_ref, out_ref, mark_ref, va_ref, vb_ref, fwd_ref, inv_ref):
    onehot = wall_onehot(wall())
    conn = conn()[...]
    field_ref = field()
    pack({(c, p): field_ref[3 * p + c] for c in range(3) for p in range(2)}, pack_ref)
    tr = nn(jnp.concatenate([field_ref[2], field_ref[5]], 0).astype(BF), onehot)
    tr = jnp.where(low_lanes((8, 128)), tr[:8], tr[8:]).astype(BF)
    for j in range(out_ref.shape[0]):
        out_ref[j] = tr
    part = jnp.zeros((16, 64), jnp.int32) + mode_ref[0] % 4
    code = jnp.where(part < 2, conn // 32, conn % 32).astype(F32)
    code = jnp.concatenate([code, code], 1)
    even = (jnp.zeros((16, 128), jnp.int32) + mode_ref[0] % 2) == 0
    code = jnp.where(even, pltpu.roll(code, 32, 1), code)
    mark_ref[...] = jnp.where(lane_group((16, 128)) == 3, code, 0.0)
    vel_ref = vel()
    vel = [vel_ref[c].astype(F32) for c in range(3)]
    zero = jnp.zeros_like(vel[0])
    va_ref[...] = jnp.concatenate([vel[0], vel[1], vel[2], zero], 0).T.astype(BF)
    vb_ref[...] = jnp.concatenate([vel[1], vel[2], vel[0], zero], 0).T.astype(BF)
    fwd_ref[...] = fwd()[...]
    inv_ref[...] = inv()[...]


def element_blocks(ref, sign):
    row = lax.broadcasted_iota(jnp.int32, (256, 64), 0)
    col = lax.broadcasted_iota(jnp.int32, (256, 64), 1)
    spread = (row % 64 == col).astype(F32).astype(BF)
    near = lax.broadcasted_iota(jnp.int32, (256, 256), 0) // 64
    same = near == lax.broadcasted_iota(jnp.int32, (256, 256), 1) // 64
    once = nt(spread, ref[...].astype(BF)).astype(BF)
    return jnp.where(same, sign * nt(once, spread), 0.0).astype(BF)


def operators(conn, first, width, stiff_ref, curl_ref, tall_ref, work_ref):
    across = conn.T
    nodes = lax.broadcasted_iota(jnp.int32, (768, 128), 0).astype(F32)
    lanes = lax.broadcasted_iota(jnp.int32, (128, width), 1).astype(F32) + first
    mats = [element_blocks(stiff_ref, -1.0), element_blocks(curl_ref, 1.0)]
    for t in range(8):
        tall_ref[:, 128 * t : 128 * t + 128] = (nodes == conn[t : t + 1]).astype(F32).astype(BF)
    for u in range(4):
        picks = [
            (lanes == across[:, t : t + 1]).astype(F32).astype(BF) for t in (2 * u, 2 * u + 1)
        ]
        picks = jnp.concatenate(picks, 0)
        for k, mat in enumerate(mats):
            work_ref[k, 256 * u : 256 * u + 256, :width] = nn(mat, picks).astype(BF)
    return [nn(tall_ref[...], work_ref[k, :, :width]) for k in range(2)]


def induce_kernel(moved_ref, mark_ref, va_ref, vb_ref, fwd_ref, inv_ref, out_ref):
    moved = moved_ref[...]
    rows = moved.reshape(256, 128)
    turned = pltpu.roll(rows.astype(F32), 96, 1).astype(BF)
    here = nn(fwd_ref[...], rows)
    after = nn(fwd_ref[...], turned)
    cross = va_ref[...].astype(F32) * after - vb_ref[...].astype(F32) * here
    back = nn(inv_ref[...], cross.astype(BF))
    out_ref[:, :16] = (back.reshape(16, 16, 128) + mark_ref[...][None]).astype(BF)
    out_ref[:, 16:] = moved


ORDER = [3 * p + c for c in range(3) for p in range(2)]


def rows_of(field):
    field_ref = field() if callable(field) else field
    return jnp.concatenate([field_ref[s] for s in ORDER], 0)


def side(mer_ref, a_ref, b_ref, odd_takes, part):
    rows = slice(16 * part, 16 * part + 16)
    odd = (jnp.zeros((16, 128), jnp.int32) + mer_ref[0] % 2) == 1
    first, second = (a_ref, b_ref) if odd_takes == 0 else (b_ref, a_ref)
    return lambda s: jnp.where(odd, first[s, rows], second[s, rows])


def operands(mer_ref, now, emf_ref, pa_ref, pb_ref):
    own = unpack(lambda s: emf_ref[s, :16], 16)
    e_next, f_next = [unpack(side(mer_ref, pa_ref, pb_ref, 1, part), 8) for part in range(2)]
    e_prev, f_prev = [unpack(side(mer_ref, pa_ref, pb_ref, 0, part), 16) for part in range(2)]
    field = rows_of(now).astype(BF)
    near = jnp.concatenate([own, e_next, field, f_next], 1)
    return near, jnp.concatenate([e_prev, own[:, :256], f_prev, field[:, :256]], 1)


def operator_rows(rows, near, far):
    total = sum(nn(rows[0][:, 512 * k : 512 * k + 512], near(k)) for k in range(3))
    low = nn(rows[1], far())
    return jnp.concatenate([total[:, :256] + low, total[:, 256:]], 1)


def first_operator_kernel(mer_ref, now, emf_ref, pa_ref, pb_ref, conn, stiff, curl, dtn_ref, *refs):
    out_ref, half_ref, near_out, far_out, near_ref, far_ref, tall_ref, work_ref, conn_ref, sems = refs
    bring = pltpu.make_async_copy(dtn_ref.at[pl.ds(0, 4)], half_ref, sems.at[2])
    bring.start()
    tile = side(mer_ref, pa_ref, pb_ref, 0, 0)
    code = [pltpu.roll(tile(s).astype(F32), 32 + 32 * (s % 2), 1) for s in range(4)]
    first = lane_group((16, 128)) == 0
    conn_ref[...] = 32.0 * jnp.where(first, code[0], code[1]) + jnp.where(first, code[2], code[3])
    there = [conn_ref[pl.ds(k, 8, 2), :] for k in range(2)]
    there = jnp.where(low_lanes((8, 128)), there[0], pltpu.roll(there[1], 64, 1))
    here = two_by_two(conn()).astype(F32)
    has = jnp.where(mer_ref[0] > 0, 1.0, 0.0)
    jobs = ((here, 0.0, 512, near_ref, near_out, 1.0), (there, 512.0, 256, far_ref, far_out, has))
    copies = []
    for conn, start, width, ref, out, gain in jobs:
        s, c = operators(conn, start, width, stiff(), curl(), tall_ref, work_ref)
        ref[:768] = (c * gain).astype(BF)
        ref[768:] = (s * gain).astype(BF)
        copies.append(pltpu.make_async_copy(ref, out, sems.at[len(copies)]))
        copies[-1].start()
    rows = operands(mer_ref, now, emf_ref, pa_ref, pb_ref)
    out_ref[...] = operator_rows(
        rows, lambda k: near_ref[512 * k : 512 * k + 512], lambda: far_ref[...]
    )
    for copy in [*copies, bring]:
        copy.wait()


def operator_kernel(mer_ref, now, emf_ref, pa_ref, pb_ref, near_ref, far_ref, dtn_ref, *refs):
    out_ref, half_ref, near_buf, far_buf, sems = refs
    pairs = [(near_ref.at[pl.ds(512 * k, 512)], near_buf.at[pl.ds(512 * k, 512)]) for k in range(3)]
    pairs += [(far_ref, far_buf), (dtn_ref.at[pl.ds(0, 4)], half_ref)]
    copies = [pltpu.make_async_copy(a, b, sems.at[k]) for k, (a, b) in enumerate(pairs)]
    for copy in copies:
        copy.start()
    rows = operands(mer_ref, now, emf_ref, pa_ref, pb_ref)

    def near(k):
        copies[k].wait()
        return near_buf[512 * k : 512 * k + 512]

    def far():
        copies[3].wait()
        return far_buf[...]

    out_ref[...] = operator_rows(rows, near, far)
    copies[4].wait()


def finish(mode_ref, mer_ref, now, total_ref, whole_ref, wall, mass, half_ref, dtn):
    whole = all_traces(whole_ref)
    every = [nt(whole, half_ref[2 * k : 2 * k + 2].reshape(128, 2048)) for k in range(2)]
    onehot = wall_onehot(wall(), mer_ref[0])
    field = rows_of(now)
    number = lax.broadcasted_iota(jnp.int32, (48, 512), 0) % 8 + 8 * mode_ref[0]
    coef = (number.astype(F32) / 128.0) ** 2
    weight = 1.0 / mass()[...]
    every += [nt(whole, dtn(k)[2 * k : 2 * k + 2].reshape(128, 2048)) for k in range(2)]
    every = jnp.concatenate(every, 1)
    mine = lax.broadcasted_iota(jnp.int32, (16, 512), 0) % 8
    every = jnp.where(mine == lax.broadcasted_iota(jnp.int32, (16, 512), 1) // 64, every, 0.0)
    flux = every[:, :128] + every[:, 128:256] + every[:, 256:384] + every[:, 384:]
    flux = flux + pltpu.roll(flux, 64, 1)
    upper = flux.astype(BF)
    added = nt(upper, onehot) + nt((flux - upper.astype(F32)).astype(BF), onehot)
    total = total_ref[...]
    total = jnp.concatenate([total[:32], total[32:] - 0.5 * added], 0)
    rate = total * weight - 4.0 * coef * field
    return rate, field, flux, onehot


def first_kernel(*refs):
    sect_ref, pack_ref, trace_ref, flux_ref = refs[9:]
    rate, field, flux, onehot = finish(*refs[:9])
    sect = field + 0.2 * rate
    flux_ref[...] = flux
    rows = {(c, p): sect[16 * c + 8 * p : 16 * c + 8 * p + 8] for c in range(3) for p in range(2)}
    for (c, p), r in rows.items():
        sect_ref[3 * p + c] = r
    pack(rows, pack_ref)
    tr = nn(sect[32:].astype(BF), onehot).astype(BF)
    for j in range(trace_ref.shape[0]):
        trace_ref[j] = tr


def second_kernel(*refs):
    start, first_flux_ref, out_ref, flux_ref = refs[9:]
    rate, sect, flux, onehot = finish(*refs[:9])
    start_ref = start()
    for c in range(3):
        for p in range(2):
            at = slice(16 * c + 8 * p, 16 * c + 8 * p + 8)
            out_ref[3 * p + c] = 0.5 * (start_ref[3 * p + c] + sect[at] + 0.2 * rate[at])
    for p in range(2):
        flux_ref[0, :, p, :] = first_flux_ref[8 * p : 8 * p + 8, :64]
        flux_ref[1, :, p, :] = flux[8 * p : 8 * p + 8, :64]


def call(kernel, out, where, args, scratch=(), limit=16):
    count = len(where)
    brought = [(a, k) for a, k in zip(args, where, strict=True) if k in "cd"]

    def run(*refs):
        inner, sems, bufs = refs, None, []
        if brought:
            inner, sems = refs[: -len(brought) - 1], refs[-len(brought) - 1]
            bufs = list(refs[-len(brought) :])
        near, used = [], 0
        for ref, k in zip(inner[:count], where, strict=True):
            if k not in "cd":
                near.append(ref)
                continue
            buf, copies = bufs.pop(0), []
            for part in range(2 if k == "d" else 1):
                src, dst = ref, buf
                if k == "d":
                    src, dst = ref.at[pl.ds(4 + 2 * part, 2)], buf.at[pl.ds(2 * part, 2)]
                copies.append(pltpu.make_async_copy(src, dst, sems.at[used]))
                copies[-1].start()
                used += 1
            near.append(later(copies, buf))
        kernel(*near, *inner[count:])

    spaces = {"s": pltpu.SMEM, "v": pltpu.VMEM, "c": pltpu.HBM, "d": pltpu.HBM, "h": pltpu.HBM}
    waits = sum(2 if k == "d" else 1 for _, k in brought)
    extra = [pltpu.SemaphoreType.DMA((waits,))] if brought else []
    extra += [pltpu.VMEM((4,) + a.shape[1:] if k == "d" else a.shape, a.dtype) for a, k in brought]
    return pl.pallas_call(
        run,
        out_shape=[space(s, d) if space else jax.ShapeDtypeStruct(s, d) for s, d, space in out],
        in_specs=[pl.BlockSpec(memory_space=spaces[k]) for k in where],
        out_specs=[pl.BlockSpec(memory_space=space or pltpu.VMEM) for _, _, space in out],
        scratch_shapes=[*scratch, *extra],
        compiler_params=pltpu.CompilerParams(vmem_limit_bytes=limit * 2**20),
    )(
        *[
            a if k == "s" else pltpu.with_memory_space_constraint(a, spaces[k])
            for k, a in zip(where, args, strict=True)
        ]
    )


def later(copies, buf):
    arrived = set()

    def get(part=0):
        if part not in arrived:
            copies[part].wait()
            arrived.add(part)
        return buf

    return get


def body(field, velocity, stiffness, curl_matrix, mass, connect, wall_index, dtn):
    fwd, inv = tables(128, 256, 8)
    near_space, far_space = pltpu.VMEM, pltpu.HBM
    spots = lax.axis_size("mer")
    mer = lax.axis_index("mer").astype(jnp.int32).reshape(1)
    mode = lax.axis_index("mode").astype(jnp.int32).reshape(1)
    start = jnp.transpose(field, (1, 0, 2))
    wall = wall_index.reshape(1, 64)
    row = mass.reshape(1, 512)
    chunk = ((16, 16, 128), BF, near_space)

    table = [((256, 128), BF, near_space)] * 2 + [((256, 256), BF, near_space)] * 2
    packed, trace, *table = call(
        open_kernel,
        [chunk, ((spots, 8, 128), BF, near_space), ((16, 128), F32, near_space), *table],
        "scccccc",
        (mode, start, wall, connect, jnp.transpose(velocity, (0, 2, 1)), fwd, inv),
    )
    twins = [(i, i ^ 1) for i in range(spots)]
    others = [(i, ((i + 1) ^ 1) - 1) for i in range(1, spots - 1)]

    def exchange(packed, trace):
        moved = lax.all_to_all(packed, "mode", 0, 0, tiled=True)
        (back,) = call(
            induce_kernel, [((16, 32, 128), BF, near_space)], "vvvvvv", (moved, *table)
        )
        emf = lax.all_to_all(back, "mode", 0, 0, tiled=True)
        e_twin = lax.ppermute(emf, "mer", twins)
        e_other = lax.ppermute(emf, "mer", others)
        return emf, e_twin, e_other, lax.all_to_all(trace, "mer", 0, 0, tiled=True)

    rows = ((48, 512), F32, near_space)
    emf, e_twin, e_other, whole = exchange(packed, trace)
    works = [
        pltpu.VMEM((1536, 512), BF),
        pltpu.VMEM((1536, 256), BF),
        pltpu.VMEM((768, 1024), BF),
        pltpu.VMEM((2, 1024, 512), BF),
        pltpu.VMEM((16, 128), F32),
        pltpu.SemaphoreType.DMA((3,)),
    ]
    some = ((4, 64, 2048), BF, near_space)
    total, half, near, far = call(
        first_operator_kernel,
        [rows, some, ((1536, 512), BF, far_space), ((1536, 256), BF, far_space)],
        "scvvvccch",
        (mer, start, emf, e_twin, e_other, connect, stiffness, curl_matrix, dtn),
        works,
        32,
    )
    out = [((6, 8, 512), F32, near_space), chunk]
    out += [((spots, 16, 128), BF, near_space), ((16, 128), F32, near_space)]
    sect, packed, trace, flux = call(
        first_kernel, out, "sscvvccvd", (mode, mer, start, total, whole, wall, row, half, dtn)
    )
    emf, e_twin, e_other, whole = exchange(packed, trace)
    total, half = call(
        operator_kernel,
        [rows, some],
        "svvvvhhh",
        (mer, sect, emf, e_twin, e_other, near, far, dtn),
        [*works[:2], pltpu.SemaphoreType.DMA((5,))],
    )
    out = [((6, 8, 512), F32, None), ((2, 8, 2, 64), F32, None)]
    done, fluxes = call(
        second_kernel,
        out,
        "ssvvvccvdcv",
        (mode, mer, sect, total, whole, wall, row, half, dtn, start, flux),
    )
    return (jnp.transpose(done, (1, 0, 2)), fluxes)


def solution(mesh):
    placed = (
        P("mode", None, "mer"),
        P(None, None, ("mer", "mode")),
        P(),
        P(),
        P("mer"),
        P("mer", None),
        P("mer"),
        P("mode", "mer", None),
    )
    return jax.shard_map(
        body,
        mesh=mesh,
        in_specs=placed,
        out_specs=(P("mode", None, "mer"), P(None, "mode", None, "mer")),
        check_vma=False,
    )
```

```python
import numpy as np
import jax
import jax.numpy as jnp
from jax import lax
from jax.experimental import pallas as pl
from jax.experimental.pallas import tpu as pltpu
from jax.sharding import PartitionSpec as P


BF = jnp.bfloat16
F32 = jnp.float32


def nt(a, b):
    return lax.dot_general(a, b, (((1,), (1,)), ((), ())), preferred_element_type=F32)


def nn(a, b):
    return jnp.dot(a, b, preferred_element_type=F32)


def tables(modes, nphi, mode_dev):
    mode = np.arange(modes).reshape(-1, 1, mode_dev)
    k = np.arange(nphi).reshape(-1, 1, 1, 1)
    angle = 2.0 * np.pi * ((mode[None] * k) % nphi) / nphi
    fwd = np.concatenate([np.cos(angle), -np.sin(angle)], 2).reshape(nphi, 2 * modes)
    return fwd.astype(BF), (fwd.T / nphi).astype(BF)


def lane_group(shape):
    return lax.broadcasted_iota(jnp.int32, shape, len(shape) - 1) // 32


def pick(group, parts):
    out = parts[0]
    for g, part in enumerate(parts[1:], 1):
        out = jnp.where(group == g, part, out)
    return out


def shift(x, groups):
    return x if groups % 4 == 0 else pltpu.roll(x, 32 * (groups % 4), 1)


def pack(rows, out_ref):
    group = lane_group((8, 128))
    for v in range(4):
        tiles = {cp: r[:, 128 * v : 128 * v + 128] for cp, r in rows.items()}
        for q in range(4):
            halves = [
                pick(group, [shift(tiles[c % 3, p], c - q) for c in range(4)]) for p in range(2)
            ]
            out_ref[4 * v + q] = jnp.concatenate(halves, 0).astype(BF)


def unpack(tile, slots):
    group = lane_group((16, 128))
    cols = []
    for v in range(slots // 4):
        tiles = [tile(4 * v + q).astype(F32) for q in range(4)]
        cols.append(
            jnp.concatenate(
                [pick(group, [shift(tiles[q], q - c) for q in range(4)]) for c in range(3)], 0
            ).astype(BF)
        )
    return jnp.concatenate(cols, 1)


def wall_onehot(wall_ref, mer=None):
    twice = jnp.concatenate([wall_ref[...], wall_ref[...]], 1)
    nodes = lax.broadcasted_iota(jnp.int32, (512, 128), 0)
    hit = (nodes == twice).astype(F32)
    if mer is not None:
        half = lax.broadcasted_iota(jnp.int32, (512, 128), 1) // 64
        hit = jnp.where(half == mer % 2, hit, 0.0)
    return hit.astype(BF)


def all_traces(whole_ref):
    pairs = [(whole_ref[2 * a], whole_ref[2 * a + 1]) for a in range(16)]
    if whole_ref.shape[1] == 16:
        return jnp.concatenate([x + y for x, y in pairs], 1)
    low = low_lanes((8, 128))
    parts = [], []
    for x, y in pairs:
        x, y = x.astype(F32), y.astype(F32)
        parts[0].append(jnp.where(low, x, pltpu.roll(y, 64, 1)))
        parts[1].append(jnp.where(low, pltpu.roll(x, 64, 1), y))
    return jnp.concatenate([jnp.concatenate(p, 1) for p in parts], 0).astype(BF)


def low_lanes(shape):
    return lax.broadcasted_iota(jnp.int32, shape, len(shape) - 1) < 64


def two_by_two(conn_ref):
    return jnp.concatenate([conn_ref[pl.ds(0, 8, 2), :], conn_ref[pl.ds(1, 8, 2), :]], 1)


def open_kernel(mode_ref, field, wall, conn, vel, fwd, inv, pack_ref, out_ref, mark_ref, va_ref, vb_ref, fwd_ref, inv_ref):
    onehot = wall_onehot(wall())
    conn = conn()[...]
    field_ref = field()
    pack({(c, p): field_ref[3 * p + c] for c in range(3) for p in range(2)}, pack_ref)
    tr = nn(jnp.concatenate([field_ref[2], field_ref[5]], 0).astype(BF), onehot)
    tr = jnp.where(low_lanes((8, 128)), tr[:8], tr[8:]).astype(BF)
    for j in range(out_ref.shape[0]):
        out_ref[j] = tr
    part = jnp.zeros((16, 64), jnp.int32) + mode_ref[0] % 4
    code = jnp.where(part < 2, conn // 32, conn % 32).astype(F32)
    code = jnp.concatenate([code, code], 1)
    even = (jnp.zeros((16, 128), jnp.int32) + mode_ref[0] % 2) == 0
    code = jnp.where(even, pltpu.roll(code, 32, 1), code)
    mark_ref[...] = jnp.where(lane_group((16, 128)) == 3, code, 0.0)
    vel_ref = vel()
    vel = [vel_ref[c].astype(F32) for c in range(3)]
    zero = jnp.zeros_like(vel[0])
    va_ref[...] = jnp.concatenate([vel[0], vel[1], vel[2], zero], 0).T.astype(BF)
    vb_ref[...] = jnp.concatenate([vel[1], vel[2], vel[0], zero], 0).T.astype(BF)
    fwd_ref[...] = fwd()[...]
    inv_ref[...] = inv()[...]


def element_blocks(ref, sign):
    row = lax.broadcasted_iota(jnp.int32, (256, 64), 0)
    col = lax.broadcasted_iota(jnp.int32, (256, 64), 1)
    spread = (row % 64 == col).astype(F32).astype(BF)
    near = lax.broadcasted_iota(jnp.int32, (256, 256), 0) // 64
    same = near == lax.broadcasted_iota(jnp.int32, (256, 256), 1) // 64
    once = nt(spread, ref[...].astype(BF)).astype(BF)
    return jnp.where(same, sign * nt(once, spread), 0.0).astype(BF)


def operators(conn, first, width, stiff_ref, curl_ref, tall_ref, work_ref):
    across = conn.T
    nodes = lax.broadcasted_iota(jnp.int32, (768, 128), 0).astype(F32)
    lanes = lax.broadcasted_iota(jnp.int32, (128, width), 1).astype(F32) + first
    mats = [element_blocks(stiff_ref, -1.0), element_blocks(curl_ref, 1.0)]
    for t in range(8):
        tall_ref[:, 128 * t : 128 * t + 128] = (nodes == conn[t : t + 1]).astype(F32).astype(BF)
    for u in range(4):
        picks = [
            (lanes == across[:, t : t + 1]).astype(F32).astype(BF) for t in (2 * u, 2 * u + 1)
        ]
        picks = jnp.concatenate(picks, 0)
        for k, mat in enumerate(mats):
            work_ref[k, 256 * u : 256 * u + 256, :width] = nn(mat, picks).astype(BF)
    return [nn(tall_ref[...], work_ref[k, :, :width]) for k in range(2)]


def induce_kernel(moved_ref, mark_ref, va_ref, vb_ref, fwd_ref, inv_ref, out_ref):
    moved = moved_ref[...]
    rows = moved.reshape(256, 128)
    turned = pltpu.roll(rows.astype(F32), 96, 1).astype(BF)
    here = nn(fwd_ref[...], rows)
    after = nn(fwd_ref[...], turned)
    cross = va_ref[...].astype(F32) * after - vb_ref[...].astype(F32) * here
    back = nn(inv_ref[...], cross.astype(BF))
    out_ref[:, :16] = (back.reshape(16, 16, 128) + mark_ref[...][None]).astype(BF)
    out_ref[:, 16:] = moved


ORDER = [3 * p + c for c in range(3) for p in range(2)]


def rows_of(field):
    field_ref = field() if callable(field) else field
    return jnp.concatenate([field_ref[s] for s in ORDER], 0)


def side(mer_ref, a_ref, b_ref, odd_takes, part):
    rows = slice(16 * part, 16 * part + 16)
    odd = (jnp.zeros((16, 128), jnp.int32) + mer_ref[0] % 2) == 1
    first, second = (a_ref, b_ref) if odd_takes == 0 else (b_ref, a_ref)
    return lambda s: jnp.where(odd, first[s, rows], second[s, rows])


def operands(mer_ref, now, emf_ref, pa_ref, pb_ref):
    own = unpack(lambda s: emf_ref[s, :16], 16)
    e_next, f_next = [unpack(side(mer_ref, pa_ref, pb_ref, 1, part), 8) for part in range(2)]
    e_prev, f_prev = [unpack(side(mer_ref, pa_ref, pb_ref, 0, part), 16) for part in range(2)]
    field = rows_of(now).astype(BF)
    near = jnp.concatenate([own, e_next, field, f_next], 1)
    return near, jnp.concatenate([e_prev, own[:, :256], f_prev, field[:, :256]], 1)


def operator_rows(rows, near, far):
    total = sum(nn(rows[0][:, 512 * k : 512 * k + 512], near(k)) for k in range(3))
    low = nn(rows[1], far())
    return jnp.concatenate([total[:, :256] + low, total[:, 256:]], 1)


def first_operator_kernel(mer_ref, now, emf_ref, pa_ref, pb_ref, conn, stiff, curl, dtn_ref, *refs):
    out_ref, half_ref, near_out, far_out, near_ref, far_ref, tall_ref, work_ref, conn_ref, sems = refs
    bring = pltpu.make_async_copy(dtn_ref.at[pl.ds(0, 6)], half_ref, sems.at[2])
    bring.start()
    tile = side(mer_ref, pa_ref, pb_ref, 0, 0)
    code = [pltpu.roll(tile(s).astype(F32), 32 + 32 * (s % 2), 1) for s in range(4)]
    first = lane_group((16, 128)) == 0
    conn_ref[...] = 32.0 * jnp.where(first, code[0], code[1]) + jnp.where(first, code[2], code[3])
    there = [conn_ref[pl.ds(k, 8, 2), :] for k in range(2)]
    there = jnp.where(low_lanes((8, 128)), there[0], pltpu.roll(there[1], 64, 1))
    here = two_by_two(conn()).astype(F32)
    has = jnp.where(mer_ref[0] > 0, 1.0, 0.0)
    jobs = ((here, 0.0, 512, near_ref, near_out, 1.0), (there, 512.0, 256, far_ref, far_out, has))
    copies = []
    for conn, start, width, ref, out, gain in jobs:
        s, c = operators(conn, start, width, stiff(), curl(), tall_ref, work_ref)
        ref[:768] = (c * gain).astype(BF)
        ref[768:] = (s * gain).astype(BF)
        copies.append(pltpu.make_async_copy(ref, out, sems.at[len(copies)]))
        copies[-1].start()
    rows = operands(mer_ref, now, emf_ref, pa_ref, pb_ref)
    out_ref[...] = operator_rows(
        rows, lambda k: near_ref[512 * k : 512 * k + 512], lambda: far_ref[...]
    )
    for copy in [*copies, bring]:
        copy.wait()


def operator_kernel(mer_ref, now, emf_ref, pa_ref, pb_ref, near_ref, far_ref, dtn_ref, *refs):
    out_ref, half_ref, near_buf, far_buf, sems = refs
    pairs = [(near_ref.at[pl.ds(512 * k, 512)], near_buf.at[pl.ds(512 * k, 512)]) for k in range(3)]
    pairs += [(far_ref, far_buf), (dtn_ref.at[pl.ds(0, 6)], half_ref)]
    copies = [pltpu.make_async_copy(a, b, sems.at[k]) for k, (a, b) in enumerate(pairs)]
    for copy in copies:
        copy.start()
    rows = operands(mer_ref, now, emf_ref, pa_ref, pb_ref)

    def near(k):
        copies[k].wait()
        return near_buf[512 * k : 512 * k + 512]

    def far():
        copies[3].wait()
        return far_buf[...]

    out_ref[...] = operator_rows(rows, near, far)
    copies[4].wait()


def finish(mode_ref, mer_ref, now, total_ref, whole_ref, wall, mass, half_ref, dtn):
    whole = all_traces(whole_ref)
    every = [nt(whole, half_ref[2 * k : 2 * k + 2].reshape(128, 2048)) for k in range(3)]
    onehot = wall_onehot(wall(), mer_ref[0])
    field = rows_of(now)
    number = lax.broadcasted_iota(jnp.int32, (48, 512), 0) % 8 + 8 * mode_ref[0]
    coef = (number.astype(F32) / 128.0) ** 2
    weight = 1.0 / mass()[...]
    every.append(nt(whole, dtn()[...].reshape(128, 2048)))
    every = jnp.concatenate(every, 1)
    mine = lax.broadcasted_iota(jnp.int32, (16, 512), 0) % 8
    every = jnp.where(mine == lax.broadcasted_iota(jnp.int32, (16, 512), 1) // 64, every, 0.0)
    flux = every[:, :128] + every[:, 128:256] + every[:, 256:384] + every[:, 384:]
    flux = flux + pltpu.roll(flux, 64, 1)
    upper = flux.astype(BF)
    added = nt(upper, onehot) + nt((flux - upper.astype(F32)).astype(BF), onehot)
    total = total_ref[...]
    total = jnp.concatenate([total[:32], total[32:] - 0.5 * added], 0)
    rate = total * weight - 4.0 * coef * field
    return rate, field, flux, onehot


def first_kernel(*refs):
    sect_ref, pack_ref, trace_ref, flux_ref = refs[9:]
    rate, field, flux, onehot = finish(*refs[:9])
    sect = field + 0.2 * rate
    flux_ref[...] = flux
    rows = {(c, p): sect[16 * c + 8 * p : 16 * c + 8 * p + 8] for c in range(3) for p in range(2)}
    for (c, p), r in rows.items():
        sect_ref[3 * p + c] = r
    pack(rows, pack_ref)
    tr = nn(sect[32:].astype(BF), onehot).astype(BF)
    for j in range(trace_ref.shape[0]):
        trace_ref[j] = tr


def second_kernel(*refs):
    start, first_flux_ref, out_ref, flux_ref = refs[9:]
    rate, sect, flux, onehot = finish(*refs[:9])
    start_ref = start()
    for c in range(3):
        for p in range(2):
            at = slice(16 * c + 8 * p, 16 * c + 8 * p + 8)
            out_ref[3 * p + c] = 0.5 * (start_ref[3 * p + c] + sect[at] + 0.2 * rate[at])
    for p in range(2):
        flux_ref[0, :, p, :] = first_flux_ref[8 * p : 8 * p + 8, :64]
        flux_ref[1, :, p, :] = flux[8 * p : 8 * p + 8, :64]


def call(kernel, out, where, args, scratch=(), limit=16):
    count = len(where)
    brought = [(a, k) for a, k in zip(args, where, strict=True) if k in "cd"]

    def run(*refs):
        inner, sems, bufs = refs, None, []
        if brought:
            inner, sems = refs[: -len(brought) - 1], refs[-len(brought) - 1]
            bufs = list(refs[-len(brought) :])
        near, used = [], 0
        for ref, k in zip(inner[:count], where, strict=True):
            if k not in "cd":
                near.append(ref)
                continue
            buf, copies = bufs.pop(0), []
            src = ref.at[pl.ds(6, 2)] if k == "d" else ref
            copies.append(pltpu.make_async_copy(src, buf, sems.at[used]))
            copies[-1].start()
            used += 1
            near.append(later(copies, buf))
        kernel(*near, *inner[count:])

    spaces = {"s": pltpu.SMEM, "v": pltpu.VMEM, "c": pltpu.HBM, "d": pltpu.HBM, "h": pltpu.HBM}
    extra = [pltpu.SemaphoreType.DMA((len(brought),))] if brought else []
    extra += [pltpu.VMEM((2,) + a.shape[1:] if k == "d" else a.shape, a.dtype) for a, k in brought]
    return pl.pallas_call(
        run,
        out_shape=[space(s, d) if space else jax.ShapeDtypeStruct(s, d) for s, d, space in out],
        in_specs=[pl.BlockSpec(memory_space=spaces[k]) for k in where],
        out_specs=[pl.BlockSpec(memory_space=space or pltpu.VMEM) for _, _, space in out],
        scratch_shapes=[*scratch, *extra],
        compiler_params=pltpu.CompilerParams(vmem_limit_bytes=limit * 2**20),
    )(
        *[
            a if k == "s" else pltpu.with_memory_space_constraint(a, spaces[k])
            for k, a in zip(where, args, strict=True)
        ]
    )


def later(copies, buf):
    arrived = set()

    def get(part=0):
        if part not in arrived:
            copies[part].wait()
            arrived.add(part)
        return buf

    return get


def body(field, velocity, stiffness, curl_matrix, mass, connect, wall_index, dtn):
    fwd, inv = tables(128, 256, 8)
    near_space, far_space = pltpu.VMEM, pltpu.HBM
    spots = lax.axis_size("mer")
    mer = lax.axis_index("mer").astype(jnp.int32).reshape(1)
    mode = lax.axis_index("mode").astype(jnp.int32).reshape(1)
    start = jnp.transpose(field, (1, 0, 2))
    wall = wall_index.reshape(1, 64)
    row = mass.reshape(1, 512)
    chunk = ((16, 16, 128), BF, near_space)

    table = [((256, 128), BF, near_space)] * 2 + [((256, 256), BF, near_space)] * 2
    packed, trace, *table = call(
        open_kernel,
        [chunk, ((spots, 8, 128), BF, near_space), ((16, 128), F32, near_space), *table],
        "scccccc",
        (mode, start, wall, connect, jnp.transpose(velocity, (0, 2, 1)), fwd, inv),
    )
    twins = [(i, i ^ 1) for i in range(spots)]
    others = [(i, ((i + 1) ^ 1) - 1) for i in range(1, spots - 1)]

    def exchange(packed, trace):
        moved = lax.all_to_all(packed, "mode", 0, 0, tiled=True)
        (back,) = call(
            induce_kernel, [((16, 32, 128), BF, near_space)], "vvvvvv", (moved, *table)
        )
        emf = lax.all_to_all(back, "mode", 0, 0, tiled=True)
        e_twin = lax.ppermute(emf, "mer", twins)
        e_other = lax.ppermute(emf, "mer", others)
        return emf, e_twin, e_other, lax.all_to_all(trace, "mer", 0, 0, tiled=True)

    rows = ((48, 512), F32, near_space)
    emf, e_twin, e_other, whole = exchange(packed, trace)
    works = [
        pltpu.VMEM((1536, 512), BF),
        pltpu.VMEM((1536, 256), BF),
        pltpu.VMEM((768, 1024), BF),
        pltpu.VMEM((2, 1024, 512), BF),
        pltpu.VMEM((16, 128), F32),
        pltpu.SemaphoreType.DMA((3,)),
    ]
    some = ((6, 64, 2048), BF, near_space)
    total, half, near, far = call(
        first_operator_kernel,
        [rows, some, ((1536, 512), BF, far_space), ((1536, 256), BF, far_space)],
        "scvvvccch",
        (mer, start, emf, e_twin, e_other, connect, stiffness, curl_matrix, dtn),
        works,
        32,
    )
    out = [((6, 8, 512), F32, near_space), chunk]
    out += [((spots, 16, 128), BF, near_space), ((16, 128), F32, near_space)]
    sect, packed, trace, flux = call(
        first_kernel, out, "sscvvccvd", (mode, mer, start, total, whole, wall, row, half, dtn)
    )
    emf, e_twin, e_other, whole = exchange(packed, trace)
    total, half = call(
        operator_kernel,
        [rows, some],
        "svvvvhhh",
        (mer, sect, emf, e_twin, e_other, near, far, dtn),
        [*works[:2], pltpu.SemaphoreType.DMA((5,))],
    )
    out = [((6, 8, 512), F32, None), ((2, 8, 2, 64), F32, None)]
    done, fluxes = call(
        second_kernel,
        out,
        "ssvvvccvdcv",
        (mode, mer, sect, total, whole, wall, row, half, dtn, start, flux),
    )
    return (jnp.transpose(done, (1, 0, 2)), fluxes)


def solution(mesh):
    placed = (
        P("mode", None, "mer"),
        P(None, None, ("mer", "mode")),
        P(),
        P(),
        P("mer"),
        P("mer", None),
        P("mer"),
        P("mode", "mer", None),
    )
    return jax.shard_map(
        body,
        mesh=mesh,
        in_specs=placed,
        out_specs=(P("mode", None, "mer"), P(None, "mode", None, "mer")),
        check_vma=False,
    )
```

```python
import numpy as np
import jax
import jax.numpy as jnp
from jax import lax
from jax.experimental import pallas as pl
from jax.experimental.pallas import tpu as pltpu
from jax.sharding import PartitionSpec as P


BF = jnp.bfloat16
F32 = jnp.float32


def nt(a, b):
    return lax.dot_general(a, b, (((1,), (1,)), ((), ())), preferred_element_type=F32)


def nn(a, b):
    return jnp.dot(a, b, preferred_element_type=F32)


def tables(modes, nphi, mode_dev):
    mode = np.arange(modes).reshape(-1, 1, mode_dev)
    k = np.arange(nphi).reshape(-1, 1, 1, 1)
    angle = 2.0 * np.pi * ((mode[None] * k) % nphi) / nphi
    fwd = np.concatenate([np.cos(angle), -np.sin(angle)], 2).reshape(nphi, 2 * modes)
    return fwd.astype(BF), (fwd.T / nphi).astype(BF)


def lane_group(shape):
    return lax.broadcasted_iota(jnp.int32, shape, len(shape) - 1) // 32


def pick(group, parts):
    out = parts[0]
    for g, part in enumerate(parts[1:], 1):
        out = jnp.where(group == g, part, out)
    return out


def shift(x, groups):
    return x if groups % 4 == 0 else pltpu.roll(x, 32 * (groups % 4), 1)


def pack(rows, out_ref):
    group = lane_group((8, 128))
    for v in range(4):
        tiles = {cp: r[:, 128 * v : 128 * v + 128] for cp, r in rows.items()}
        for q in range(4):
            halves = [
                pick(group, [shift(tiles[c % 3, p], c - q) for c in range(4)]) for p in range(2)
            ]
            out_ref[4 * v + q] = jnp.concatenate(halves, 0).astype(BF)


def unpack(tile, slots):
    group = lane_group((16, 128))
    cols = []
    for v in range(slots // 4):
        tiles = [tile(4 * v + q).astype(F32) for q in range(4)]
        cols.append(
            jnp.concatenate(
                [pick(group, [shift(tiles[q], q - c) for q in range(4)]) for c in range(3)], 0
            ).astype(BF)
        )
    return jnp.concatenate(cols, 1)


def wall_onehot(wall_ref, mer=None):
    twice = jnp.concatenate([wall_ref[...], wall_ref[...]], 1)
    nodes = lax.broadcasted_iota(jnp.int32, (512, 128), 0)
    hit = (nodes == twice).astype(F32)
    if mer is not None:
        half = lax.broadcasted_iota(jnp.int32, (512, 128), 1) // 64
        hit = jnp.where(half == mer % 2, hit, 0.0)
    return hit.astype(BF)


def all_traces(whole_ref):
    pairs = [(whole_ref[2 * a], whole_ref[2 * a + 1]) for a in range(16)]
    if whole_ref.shape[1] == 16:
        return jnp.concatenate([x + y for x, y in pairs], 1)
    low = low_lanes((8, 128))
    parts = [], []
    for x, y in pairs:
        x, y = x.astype(F32), y.astype(F32)
        parts[0].append(jnp.where(low, x, pltpu.roll(y, 64, 1)))
        parts[1].append(jnp.where(low, pltpu.roll(x, 64, 1), y))
    return jnp.concatenate([jnp.concatenate(p, 1) for p in parts], 0).astype(BF)


def low_lanes(shape):
    return lax.broadcasted_iota(jnp.int32, shape, len(shape) - 1) < 64


def two_by_two(conn_ref):
    return jnp.concatenate([conn_ref[pl.ds(0, 8, 2), :], conn_ref[pl.ds(1, 8, 2), :]], 1)


def open_kernel(mode_ref, field, wall, conn, vel, fwd, inv, pack_ref, out_ref, mark_ref, va_ref, vb_ref, fwd_ref, inv_ref, sems):
    tables = [pltpu.make_async_copy(a, b, sems.at[k]) for k, (a, b) in enumerate(((fwd, fwd_ref), (inv, inv_ref)))]
    for copy in tables:
        copy.start()
    onehot = wall_onehot(wall())
    conn = conn()[...]
    field_ref = field()
    pack({(c, p): field_ref[3 * p + c] for c in range(3) for p in range(2)}, pack_ref)
    tr = nn(jnp.concatenate([field_ref[2], field_ref[5]], 0).astype(BF), onehot)
    tr = jnp.where(low_lanes((8, 128)), tr[:8], tr[8:]).astype(BF)
    for j in range(out_ref.shape[0]):
        out_ref[j] = tr
    part = jnp.zeros((16, 64), jnp.int32) + mode_ref[0] % 4
    code = jnp.where(part < 2, conn // 32, conn % 32).astype(F32)
    code = jnp.concatenate([code, code], 1)
    even = (jnp.zeros((16, 128), jnp.int32) + mode_ref[0] % 2) == 0
    code = jnp.where(even, pltpu.roll(code, 32, 1), code)
    mark_ref[...] = jnp.where(lane_group((16, 128)) == 3, code, 0.0)
    vel_ref = vel()
    vel = [vel_ref[c].astype(F32) for c in range(3)]
    zero = jnp.zeros_like(vel[0])
    va_ref[...] = jnp.concatenate([vel[0], vel[1], vel[2], zero], 0).T.astype(BF)
    vb_ref[...] = jnp.concatenate([vel[1], vel[2], vel[0], zero], 0).T.astype(BF)
    for copy in tables:
        copy.wait()


def element_blocks(ref, sign):
    row = lax.broadcasted_iota(jnp.int32, (256, 64), 0)
    col = lax.broadcasted_iota(jnp.int32, (256, 64), 1)
    spread = (row % 64 == col).astype(F32).astype(BF)
    near = lax.broadcasted_iota(jnp.int32, (256, 256), 0) // 64
    same = near == lax.broadcasted_iota(jnp.int32, (256, 256), 1) // 64
    once = nt(spread, ref[...].astype(BF)).astype(BF)
    return jnp.where(same, sign * nt(once, spread), 0.0).astype(BF)


def operators(conn, first, width, stiff_ref, curl_ref, tall_ref, work_ref):
    across = conn.T
    nodes = lax.broadcasted_iota(jnp.int32, (768, 128), 0).astype(F32)
    lanes = lax.broadcasted_iota(jnp.int32, (128, width), 1).astype(F32) + first
    mats = [element_blocks(stiff_ref, -1.0), element_blocks(curl_ref, 1.0)]
    for t in range(8):
        tall_ref[:, 128 * t : 128 * t + 128] = (nodes == conn[t : t + 1]).astype(F32).astype(BF)
    for u in range(4):
        picks = [
            (lanes == across[:, t : t + 1]).astype(F32).astype(BF) for t in (2 * u, 2 * u + 1)
        ]
        picks = jnp.concatenate(picks, 0)
        for k, mat in enumerate(mats):
            work_ref[k, 256 * u : 256 * u + 256, :width] = nn(mat, picks).astype(BF)
    return [nn(tall_ref[...], work_ref[k, :, :width]) for k in range(2)]


def induce_kernel(moved_ref, mark_ref, va_ref, vb_ref, fwd_ref, inv_ref, out_ref):
    moved = moved_ref[...]
    rows = moved.reshape(256, 128)
    turned = pltpu.roll(rows.astype(F32), 96, 1).astype(BF)
    here = nn(fwd_ref[...], rows)
    after = nn(fwd_ref[...], turned)
    cross = va_ref[...].astype(F32) * after - vb_ref[...].astype(F32) * here
    back = nn(inv_ref[...], cross.astype(BF))
    out_ref[:, :16] = (back.reshape(16, 16, 128) + mark_ref[...][None]).astype(BF)
    out_ref[:, 16:] = moved


ORDER = [3 * p + c for c in range(3) for p in range(2)]


def rows_of(field):
    field_ref = field() if callable(field) else field
    return jnp.concatenate([field_ref[s] for s in ORDER], 0)


def side(mer_ref, a_ref, b_ref, odd_takes, part):
    rows = slice(16 * part, 16 * part + 16)
    odd = (jnp.zeros((16, 128), jnp.int32) + mer_ref[0] % 2) == 1
    first, second = (a_ref, b_ref) if odd_takes == 0 else (b_ref, a_ref)
    return lambda s: jnp.where(odd, first[s, rows], second[s, rows])


def operands(mer_ref, now, emf_ref, pa_ref, pb_ref):
    own = unpack(lambda s: emf_ref[s, :16], 16)
    e_next, f_next = [unpack(side(mer_ref, pa_ref, pb_ref, 1, part), 8) for part in range(2)]
    e_prev, f_prev = [unpack(side(mer_ref, pa_ref, pb_ref, 0, part), 16) for part in range(2)]
    field = rows_of(now).astype(BF)
    near = jnp.concatenate([own, e_next, field, f_next], 1)
    return near, jnp.concatenate([e_prev, own[:, :256], f_prev, field[:, :256]], 1)


def operator_rows(rows, near, far):
    total = sum(nn(rows[0][:, 512 * k : 512 * k + 512], near(k)) for k in range(3))
    low = nn(rows[1], far())
    return jnp.concatenate([total[:, :256] + low, total[:, 256:]], 1)


def first_operator_kernel(mer_ref, now, emf_ref, pa_ref, pb_ref, conn, stiff, curl, dtn_ref, *refs):
    out_ref, half_ref, near_out, far_out, near_ref, far_ref, tall_ref, work_ref, conn_ref, sems = refs
    bring = pltpu.make_async_copy(dtn_ref.at[pl.ds(0, 6)], half_ref, sems.at[2])
    bring.start()
    tile = side(mer_ref, pa_ref, pb_ref, 0, 0)
    code = [pltpu.roll(tile(s).astype(F32), 32 + 32 * (s % 2), 1) for s in range(4)]
    first = lane_group((16, 128)) == 0
    conn_ref[...] = 32.0 * jnp.where(first, code[0], code[1]) + jnp.where(first, code[2], code[3])
    there = [conn_ref[pl.ds(k, 8, 2), :] for k in range(2)]
    there = jnp.where(low_lanes((8, 128)), there[0], pltpu.roll(there[1], 64, 1))
    here = two_by_two(conn()).astype(F32)
    has = jnp.where(mer_ref[0] > 0, 1.0, 0.0)
    jobs = ((here, 0.0, 512, near_ref, near_out, 1.0), (there, 512.0, 256, far_ref, far_out, has))
    copies = []
    for conn, start, width, ref, out, gain in jobs:
        s, c = operators(conn, start, width, stiff(), curl(), tall_ref, work_ref)
        ref[:768] = (c * gain).astype(BF)
        ref[768:] = (s * gain).astype(BF)
        copies.append(pltpu.make_async_copy(ref, out, sems.at[len(copies)]))
        copies[-1].start()
    rows = operands(mer_ref, now, emf_ref, pa_ref, pb_ref)
    out_ref[...] = operator_rows(
        rows, lambda k: near_ref[512 * k : 512 * k + 512], lambda: far_ref[...]
    )
    for copy in [*copies, bring]:
        copy.wait()


def operator_kernel(mer_ref, now, emf_ref, pa_ref, pb_ref, near_ref, far_ref, dtn_ref, *refs):
    out_ref, half_ref, near_buf, far_buf, sems = refs
    pairs = [(near_ref.at[pl.ds(512 * k, 512)], near_buf.at[pl.ds(512 * k, 512)]) for k in range(3)]
    pairs += [(far_ref, far_buf), (dtn_ref.at[pl.ds(0, 6)], half_ref)]
    copies = [pltpu.make_async_copy(a, b, sems.at[k]) for k, (a, b) in enumerate(pairs)]
    for copy in copies:
        copy.start()
    rows = operands(mer_ref, now, emf_ref, pa_ref, pb_ref)

    def near(k):
        copies[k].wait()
        return near_buf[512 * k : 512 * k + 512]

    def far():
        copies[3].wait()
        return far_buf[...]

    out_ref[...] = operator_rows(rows, near, far)
    copies[4].wait()


def finish(mode_ref, mer_ref, now, total_ref, whole_ref, wall, mass, half_ref, dtn):
    whole = all_traces(whole_ref)
    every = [nt(whole, half_ref[2 * k : 2 * k + 2].reshape(128, 2048)) for k in range(3)]
    onehot = wall_onehot(wall(), mer_ref[0])
    field = rows_of(now)
    number = lax.broadcasted_iota(jnp.int32, (48, 512), 0) % 8 + 8 * mode_ref[0]
    coef = (number.astype(F32) / 128.0) ** 2
    weight = 1.0 / mass()[...]
    every.append(nt(whole, dtn()[...].reshape(128, 2048)))
    every = jnp.concatenate(every, 1)
    mine = lax.broadcasted_iota(jnp.int32, (16, 512), 0) % 8
    every = jnp.where(mine == lax.broadcasted_iota(jnp.int32, (16, 512), 1) // 64, every, 0.0)
    flux = every[:, :128] + every[:, 128:256] + every[:, 256:384] + every[:, 384:]
    flux = flux + pltpu.roll(flux, 64, 1)
    upper = flux.astype(BF)
    added = nt(upper, onehot) + nt((flux - upper.astype(F32)).astype(BF), onehot)
    total = total_ref[...]
    total = jnp.concatenate([total[:32], total[32:] - 0.5 * added], 0)
    rate = total * weight - 4.0 * coef * field
    return rate, field, flux, onehot


def first_kernel(*refs):
    sect_ref, pack_ref, trace_ref, flux_ref = refs[9:]
    rate, field, flux, onehot = finish(*refs[:9])
    sect = field + 0.2 * rate
    flux_ref[...] = flux
    rows = {(c, p): sect[16 * c + 8 * p : 16 * c + 8 * p + 8] for c in range(3) for p in range(2)}
    for (c, p), r in rows.items():
        sect_ref[3 * p + c] = r
    pack(rows, pack_ref)
    tr = nn(sect[32:].astype(BF), onehot).astype(BF)
    for j in range(trace_ref.shape[0]):
        trace_ref[j] = tr


def second_kernel(*refs):
    start, first_flux_ref, out_ref, flux_ref = refs[9:]
    rate, sect, flux, onehot = finish(*refs[:9])
    start_ref = start()
    for c in range(3):
        for p in range(2):
            at = slice(16 * c + 8 * p, 16 * c + 8 * p + 8)
            out_ref[3 * p + c] = 0.5 * (start_ref[3 * p + c] + sect[at] + 0.2 * rate[at])
    for p in range(2):
        flux_ref[0, :, p, :] = first_flux_ref[8 * p : 8 * p + 8, :64]
        flux_ref[1, :, p, :] = flux[8 * p : 8 * p + 8, :64]


def call(kernel, out, where, args, scratch=(), limit=16):
    count = len(where)
    brought = [(a, k) for a, k in zip(args, where, strict=True) if k in "cd"]

    def run(*refs):
        inner, sems, bufs = refs, None, []
        if brought:
            inner, sems = refs[: -len(brought) - 1], refs[-len(brought) - 1]
            bufs = list(refs[-len(brought) :])
        near, used = [], 0
        for ref, k in zip(inner[:count], where, strict=True):
            if k not in "cd":
                near.append(ref)
                continue
            buf, copies = bufs.pop(0), []
            src = ref.at[pl.ds(6, 2)] if k == "d" else ref
            copies.append(pltpu.make_async_copy(src, buf, sems.at[used]))
            copies[-1].start()
            used += 1
            near.append(later(copies, buf))
        kernel(*near, *inner[count:])

    spaces = {"s": pltpu.SMEM, "v": pltpu.VMEM, "c": pltpu.HBM, "d": pltpu.HBM, "h": pltpu.HBM}
    extra = [pltpu.SemaphoreType.DMA((len(brought),))] if brought else []
    extra += [pltpu.VMEM((2,) + a.shape[1:] if k == "d" else a.shape, a.dtype) for a, k in brought]
    return pl.pallas_call(
        run,
        out_shape=[space(s, d) if space else jax.ShapeDtypeStruct(s, d) for s, d, space in out],
        in_specs=[pl.BlockSpec(memory_space=spaces[k]) for k in where],
        out_specs=[pl.BlockSpec(memory_space=space or pltpu.VMEM) for _, _, space in out],
        scratch_shapes=[*scratch, *extra],
        compiler_params=pltpu.CompilerParams(vmem_limit_bytes=limit * 2**20),
    )(
        *[
            a if k == "s" else pltpu.with_memory_space_constraint(a, spaces[k])
            for k, a in zip(where, args, strict=True)
        ]
    )


def later(copies, buf):
    arrived = set()

    def get(part=0):
        if part not in arrived:
            copies[part].wait()
            arrived.add(part)
        return buf

    return get


def body(field, velocity, stiffness, curl_matrix, mass, connect, wall_index, dtn):
    fwd, inv = tables(128, 256, 8)
    near_space, far_space = pltpu.VMEM, pltpu.HBM
    spots = lax.axis_size("mer")
    mer = lax.axis_index("mer").astype(jnp.int32).reshape(1)
    mode = lax.axis_index("mode").astype(jnp.int32).reshape(1)
    start = jnp.transpose(field, (1, 0, 2))
    wall = wall_index.reshape(1, 64)
    row = mass.reshape(1, 512)
    chunk = ((16, 16, 128), BF, near_space)

    table = [((256, 128), BF, near_space)] * 2 + [((256, 256), BF, near_space)] * 2
    packed, trace, *table = call(
        open_kernel,
        [chunk, ((spots, 8, 128), BF, near_space), ((16, 128), F32, near_space), *table],
        "scccchh",
        (mode, start, wall, connect, jnp.transpose(velocity, (0, 2, 1)), fwd, inv),
        [pltpu.SemaphoreType.DMA((2,))],
    )
    twins = [(i, i ^ 1) for i in range(spots)]
    others = [(i, ((i + 1) ^ 1) - 1) for i in range(1, spots - 1)]

    def exchange(packed, trace):
        moved = lax.all_to_all(packed, "mode", 0, 0, tiled=True)
        (back,) = call(
            induce_kernel, [((16, 32, 128), BF, near_space)], "vvvvvv", (moved, *table)
        )
        emf = lax.all_to_all(back, "mode", 0, 0, tiled=True)
        e_twin = lax.ppermute(emf, "mer", twins)
        e_other = lax.ppermute(emf, "mer", others)
        return emf, e_twin, e_other, lax.all_to_all(trace, "mer", 0, 0, tiled=True)

    rows = ((48, 512), F32, near_space)
    emf, e_twin, e_other, whole = exchange(packed, trace)
    works = [
        pltpu.VMEM((1536, 512), BF),
        pltpu.VMEM((1536, 256), BF),
        pltpu.VMEM((768, 1024), BF),
        pltpu.VMEM((2, 1024, 512), BF),
        pltpu.VMEM((16, 128), F32),
        pltpu.SemaphoreType.DMA((3,)),
    ]
    some = ((6, 64, 2048), BF, near_space)
    total, half, near, far = call(
        first_operator_kernel,
        [rows, some, ((1536, 512), BF, far_space), ((1536, 256), BF, far_space)],
        "scvvvccch",
        (mer, start, emf, e_twin, e_other, connect, stiffness, curl_matrix, dtn),
        works,
        32,
    )
    out = [((6, 8, 512), F32, near_space), chunk]
    out += [((spots, 16, 128), BF, near_space), ((16, 128), F32, near_space)]
    sect, packed, trace, flux = call(
        first_kernel, out, "sscvvccvd", (mode, mer, start, total, whole, wall, row, half, dtn)
    )
    emf, e_twin, e_other, whole = exchange(packed, trace)
    total, half = call(
        operator_kernel,
        [rows, some],
        "svvvvhhh",
        (mer, sect, emf, e_twin, e_other, near, far, dtn),
        [*works[:2], pltpu.SemaphoreType.DMA((5,))],
    )
    out = [((6, 8, 512), F32, None), ((2, 8, 2, 64), F32, None)]
    done, fluxes = call(
        second_kernel,
        out,
        "ssvvvccvdcv",
        (mode, mer, sect, total, whole, wall, row, half, dtn, start, flux),
    )
    return (jnp.transpose(done, (1, 0, 2)), fluxes)


def solution(mesh):
    placed = (
        P("mode", None, "mer"),
        P(None, None, ("mer", "mode")),
        P(),
        P(),
        P("mer"),
        P("mer", None),
        P("mer"),
        P("mode", "mer", None),
    )
    return jax.shard_map(
        body,
        mesh=mesh,
        in_specs=placed,
        out_specs=(P("mode", None, "mer"), P(None, "mode", None, "mer")),
        check_vma=False,
    )
```
